32 devices in a mesh: row: 4 (over y, x), col: 8 (over z, core).
Axes of the slice: x: 2, y: 2, z: 4, core: 2. Of those that a mesh axis runs over, the one named last changes fastest.
Arguments:
- coupling: float32 [4, 4608, 18432], P(None, 'col', 'row'), may hold values from -0.046875 to 0.046875
- energies: float32 [18432], P(('row', 'col')), may hold values from 0.7 to 14.2
- block: float32 [18432, 16], P(('row', 'col')), may hold values from -6 to 6
Outputs:
- basis: float32 [18432, 16], P(('row', 'col'))
- projections: float32 [2, 16, 16], replicated
- factors: float32 [2, 16, 16], replicated
The draws below stay inside these ranges and needn't reach their ends.
All inputs are finite; a program needn't handle non-finite values.
Results may differ from the reference program's by a relative error of at most 0.0003.
Values sent between devices are 32-bit elements; how exact they have to be, the bound alone decides.
No kernel may reach another device: no remote copies, remote signals or barrier semaphores. Data moves between devices by JAX's collectives and lax.ppermute only.
A program may use at most 128 MiB of HBM per device.

```python
import jax
import jax.numpy as jnp
from jax import lax

N = 18432
K = 16
ITERS = 2
SLAB = 4608
N_ROW = 4


def draw_energies(key, part):
    position = jnp.arange(N).astype(jnp.float32) / N
    baseline = 1.0 + 9.0 * position
    jitter = jnp.clip(0.15 * jax.random.normal(key, (N,), jnp.float32), -0.35, 0.35)
    return baseline * jnp.exp(jitter)


def spiked(result, own_key, source, target, blocks, factor):
    owner, partner = [(jnp.arange(result.shape[axis_at]) // (result.shape[axis_at] // blocks)).reshape([-1 if axis == axis_at else 1 for axis in range(result.ndim)]) for axis_at in (source, target)]
    chosen = jax.random.permutation(own_key, blocks)[partner]
    strong = (owner == chosen) | (owner == (partner + blocks // 2) % blocks)
    return jnp.where(strong, factor * result, result)


def block_scale(key, dims, pieces, least, top_value):
    level = 1.0
    for axis_at, blocks in pieces:
        heights = jax.random.uniform(jax.random.fold_in(jax.random.fold_in(key, 6), axis_at), (blocks,), jnp.float32, least / len(pieces), top_value / len(pieces))
        level = level * jnp.repeat(jnp.exp(heights), dims[axis_at] // blocks).reshape((-1,) + (1,) * (len(dims) - 1 - axis_at))
    return level


def gaussian(rng, shape, spread, limit, split=(), kind=jnp.bfloat16):
    gain = block_scale(rng, shape, split, -0.22, 0.18) if split else 1.0
    drawn = jax.random.normal(rng, shape, jnp.float32) * spread * gain
    return jnp.minimum(jnp.maximum(drawn, -limit), limit).astype(kind)


def gaussian_with(key, shape, scale, most, pieces, heavy, kind=jnp.bfloat16):
    array = scale * jax.random.normal(key, shape, jnp.float32)
    if pieces:
        array = array * block_scale(key, shape, pieces, -0.22, 0.18)
    return jnp.clip(spiked(array, jax.random.fold_in(key, 3), *heavy), -most, most).astype(kind)


def setup_inputs(seed: int = 0) -> dict:
    splits = jax.random.split(jax.random.key(seed), 4)
    coupling = gaussian_with(splits[0], (N_ROW, SLAB, N), (2 * N) ** -0.5, 0.046875, ((1, 8), (2, 4)), (1, 2, 8, 2.0), jnp.float32)
    energies = draw_energies(jax.random.fold_in(splits[3], 71), 0)
    block = gaussian(splits[2], (N, K), 1.0, 6.0, ((0, 32),), jnp.float32)
    return {"coupling": coupling, "energies": energies, "block": block}


precise = lax.Precision.HIGHEST

def reference(coupling, energies, block):
    matrix = coupling.reshape(N, N)
    current = block
    prior = jnp.zeros_like(block)
    projection_list = []
    factor_list = []
    for section in range(ITERS):
        product = energies[:, None] * current
        product = product + jnp.dot(matrix, current, precision=precise)
        product = product + jnp.einsum('nm,nk->mk', matrix, current, precision=precise)
        projection = jnp.dot(current.T, product, precision=precise) / N
        cross = jnp.dot(prior.T, product, precision=precise) / N
        residual = product - jnp.dot(current, projection, precision=precise) - jnp.dot(prior, cross, precision=precise)
        gram_matrix = jnp.dot(residual.T, residual, precision=precise) / N
        factor = jnp.linalg.cholesky(gram_matrix)
        prior = current
        current = jax.scipy.linalg.solve_triangular(factor, residual.T, lower=True).T
        projection_list.append(projection)
        factor_list.append(factor)
    return (current, jnp.stack(projection_list), jnp.stack(factor_list))
```

```python
import functools

import jax
import jax.numpy as jnp
from jax import lax
from jax.experimental import pallas as pl
from jax.experimental.pallas import tpu as pltpu
from jax.sharding import PartitionSpec as P

ITERS = 2
F32 = jnp.float32
BF16 = jnp.bfloat16

precise = lax.Precision.HIGHEST

NN = (((1,), (0,)), ((), ()))
NT = (((1,), (1,)), ((), ()))
TN = (((0,), (0,)), ((), ()))

VMEM_SPEC = pl.BlockSpec(memory_space=pltpu.VMEM)


def generic(coupling, energies, block):
    order = block.shape[0] * lax.axis_size("row") * lax.axis_size("col")
    segment = block.shape[0]
    width = block.shape[1]
    column = lax.axis_index("col")
    current, energy_rows = (
        lax.all_gather(block, "col", axis=0, tiled=True),
        lax.all_gather(energies, "col", axis=0, tiled=True),
    )
    prior = jnp.zeros_like(current)
    projection_list = []
    factor_list = []
    for section in range(ITERS):
        own_rows = lax.dynamic_slice_in_dim(current, column * segment, segment, 0)
        spread = lax.all_gather(own_rows, "row", axis=0, tiled=True)
        spread = spread.reshape(coupling.shape[0], segment, width)
        direct = lax.psum_scatter(
            jnp.einsum("aig,gk->aik", coupling, current, precision=precise),
            "row",
            scatter_dimension=0,
            tiled=True,
        ).reshape(segment, width)
        partial_value = jnp.einsum("aig,aik->gk", coupling, spread, precision=precise)
        transposed = lax.psum(partial_value, "col")
        direct_rows = lax.all_gather(direct, "col", axis=0, tiled=True)
        product = energy_rows[:, None] * current + direct_rows + transposed
        stacked = jnp.concatenate([current, prior, product], axis=1)
        moments = lax.psum(jnp.einsum("nk,nl->kl", stacked, stacked, precision=precise), "row") / order
        projection = moments[:width, 2 * width :]
        cross = moments[width : 2 * width, 2 * width :]
        weights = jnp.concatenate([-projection, -cross, jnp.eye(width, dtype=F32)], axis=0)
        gram_matrix = jnp.dot(weights.T, jnp.dot(moments, weights, precision=precise), precision=precise)
        factor = jnp.linalg.cholesky(gram_matrix)
        residual = (
            product
            - jnp.dot(current, projection, precision=precise)
            - jnp.dot(prior, cross, precision=precise)
        )
        prior = current
        current = jax.scipy.linalg.solve_triangular(factor, residual.T, lower=True).T
        projection_list.append(projection)
        factor_list.append(factor)
    basis = lax.dynamic_slice_in_dim(current, column * segment, segment, 0)
    return (basis, jnp.stack(projection_list), jnp.stack(factor_list))


def place():
    column = lax.axis_index("col")
    return lax.rem(column, 2), lax.div(column, 2), lax.axis_index("row")


def split(value):
    high = value.astype(BF16)
    return high, (value - high.astype(F32)).astype(BF16)


def dot(left, right, dims):
    return lax.dot_general(left, right, dims, preferred_element_type=F32)


def dot32(left, right, dims):
    return lax.dot_general(left, right, dims, preferred_element_type=F32, precision=precise)


def product_kernel(k, n, group, tile, a_ref, pair_ref, *refs):
    mine = refs[: group - 1]
    theirs = refs[group - 1 : 2 * (group - 1)]
    send_ref, keep_ref, xg, xr, rows, u_acc, v_acc = refs[2 * (group - 1) :]
    parity, z, r = place()
    even = parity == 0

    def put(slab, at, first, second):
        high, low = split(jnp.concatenate([first, second], axis=1))
        cols = pl.ds(pl.multiple_of(at * (2 * n), 2 * n), 2 * n)
        slab[:k, cols] = high
        slab[k:, cols] = low

    pair = pair_ref[: 2 * k, :]
    put(xg, z, pair[:k], pair[k:])
    rows[pl.ds(r, 1)] = jnp.where(even, pair[:k], pair[k:])[None]
    for s in range(1, group):
        y, w = mine[s - 1][: 2 * k, :], theirs[s - 1][: 2 * k, :]
        along_z = jnp.where(even, y, w)
        along_row = jnp.where(even, w, y)
        put(xg, lax.bitwise_xor(z, s), along_z[:k], along_z[k:])
        rows[pl.ds(lax.bitwise_xor(r, s), 1)] = jnp.where(even, along_row[:k], along_row[k:])[None]
    for a in range(0, group, 2):
        put(xr, a // 2, rows[a], rows[a + 1])

    v_acc[...] = jnp.zeros_like(v_acc)

    def step(t, carry):
        at = pl.ds(pl.multiple_of(t * tile, tile), tile)
        high, low = split(a_ref[at, :])
        p = dot(xr[:, at], high, NN)
        q = dot(xr[:k, at], low, NN)
        v_acc[...] += p[:k] + p[k:] + q
        p = dot(xg[...], high, NT)
        q = dot(xg[:k, :], low, NT)
        u_acc[:, at] = p[:k] + p[k:] + q
        return carry

    lax.fori_loop(0, a_ref.shape[0] // tile, step, 0)

    def by_z(out):
        for g in range(group):
            both = v_acc[:, 2 * n * g : 2 * n * (g + 1)]
            out[g, :k, :] = both[:, :n]
            out[g, k:, :] = both[:, n:]

    def by_row(out, first):
        for a in range(0, group, 2):
            both = u_acc[:, n * a : n * (a + 2)]
            at = slice(0, k) if first else slice(k, 2 * k)
            rest = slice(k, 2 * k) if first else slice(0, k)
            out[a, at, :] = both[:, :n]
            out[a + 1, at, :] = both[:, n:]
            out[a, rest, :] = jnp.zeros((k, n), F32)
            out[a + 1, rest, :] = jnp.zeros((k, n), F32)

    @pl.when(even)
    def _():
        by_z(keep_ref)
        by_row(send_ref, True)

    @pl.when(jnp.logical_not(even))
    def _():
        by_z(send_ref)
        by_row(keep_ref, False)


def combine_kernel(k, n, group, extra, keep_ref, got_ref, pair_ref, energy_ref, *refs):
    theirs = refs[: group - 1] if extra else ()
    outs = refs[len(theirs) :]
    parity, z, r = place()
    even = parity == 0
    at = jnp.where(even, z, r)
    for s in range(group):
        i = lax.bitwise_xor(at, s)
        total = keep_ref[pl.ds(i, 1)][0] + got_ref[pl.ds(i, 1)][0]
        if s == 0:
            own = energy_ref[...] * pair_ref[: 2 * k, :]
            row = lax.broadcasted_iota(jnp.int32, own.shape, 0)
            total = total + jnp.where((row < k) == even, own, 0.0)
        outs[s][: 2 * k, :] = total
    if extra:
        part = pair_ref[2 * k :, :]
        for w in theirs:
            part = part + w[2 * k :, :]
        part = jnp.where(even, part, jnp.zeros_like(part))
        for s in range(group):
            outs[s][2 * k :, :] = part


def pair_kernel(k, n, first_ref, mine_ref, got_ref, out_ref):
    value = mine_ref[...] + got_ref[...]
    out_ref[: 2 * k, :] = value
    moments = jnp.zeros((2 * k, 2 * k), F32)
    for p in range(2):
        s = jnp.concatenate([first_ref[p * k : (p + 1) * k, :], value[p * k : (p + 1) * k]], axis=0)
        moments = moments + dot32(s, s, NT)
    out_ref[2 * k :, :] = jnp.zeros((8, n), F32)
    for j in range(2 * k // 8):
        out_ref[2 * k : 2 * k + 8, 2 * k * j : 2 * k * (j + 1)] = moments[8 * j : 8 * (j + 1), :]


def factor_of(gram):
    k = gram.shape[0]
    rows = lax.broadcasted_iota(jnp.int32, (k, 2 * k), 0)
    cols = lax.broadcasted_iota(jnp.int32, (k, 2 * k), 1)
    row = lax.broadcasted_iota(jnp.int32, (k, 1), 0)
    both = jnp.concatenate([gram, jnp.where(rows == cols, 1.0, 0.0)[:, :k]], axis=1)
    lower = jnp.zeros((k, k), F32)
    for j in range(k):
        scale = 1.0 / jnp.sqrt(both[j : j + 1, j : j + 1])
        column = jnp.where(row >= j, both[:, j : j + 1] * scale, 0.0)
        lower = jnp.where(cols[:, :k] == j, column, lower)
        lead = both[j : j + 1, :] * scale
        below = jnp.where(row > j, column, 0.0)
        both = jnp.where(rows == j, lead, both - below * lead)
    return lower, both[:, k:]


def gram_of(moments, coefficients):
    k = moments.shape[0]
    w = coefficients.shape[1]
    parts = jnp.concatenate([-coefficients, eye(w)], axis=0)
    return dot32(parts, dot32(moments, parts, NN), TN)


def eye(k):
    return jnp.where(
        lax.broadcasted_iota(jnp.int32, (k, k), 0) == lax.broadcasted_iota(jnp.int32, (k, k), 1), 1.0, 0.0
    ).astype(F32)


def second_kernel(k, n, order, first_ref, pair_ref, mine_ref, got_ref, q_ref, prod_ref, mom_ref, proj_ref, fact_ref):
    packed = mine_ref[2 * k :, :] + got_ref[2 * k :, :]
    moments = jnp.concatenate(
        [packed[:, 2 * k * j : 2 * k * (j + 1)] for j in range(2 * k // 8)], axis=0
    ) * (1.0 / order)
    projection = moments[:k, k:]
    lower, inverse = factor_of(gram_of(moments, projection))
    proj_ref[...] = projection
    fact_ref[...] = lower
    total = jnp.zeros((3 * k, 3 * k), F32)
    for p in range(2):
        at = slice(p * k, (p + 1) * k)
        x, y = first_ref[at, :], pair_ref[at, :]
        w = mine_ref[at, :] + got_ref[at, :]
        q = dot32(inverse, y - dot32(projection, x, TN), NN)
        prod = dot32(inverse, w - dot32(projection, y, TN), NN)
        q_ref[at, :] = q
        prod_ref[at, :] = prod
        s = jnp.concatenate([q, x, prod], axis=0)
        total = total + dot32(s, s, NT)
    mom_ref[...] = total


def last_kernel(k, n, order, group, first_ref, q_ref, prod_ref, proj0_ref, fact0_ref, *refs):
    basis_ref, proj_ref, fact_ref = refs[group:]
    total = refs[0][...]
    for m in refs[1:group]:
        total = total + m[...]
    moments = total * (1.0 / order)
    coefficients = moments[: 2 * k, 2 * k :]
    lower, inverse = factor_of(gram_of(moments, coefficients))
    proj_ref[0] = proj0_ref[...]
    proj_ref[1] = coefficients[:k]
    fact_ref[0] = fact0_ref[...]
    fact_ref[1] = lower
    even = place()[0] == 0
    q = jnp.where(even, q_ref[:k, :], q_ref[k:, :])
    x = jnp.where(even, first_ref[:k, :], first_ref[k:, :])
    prod = jnp.where(even, prod_ref[:k, :], prod_ref[k:, :])
    rest = prod - dot32(coefficients[:k], q, TN) - dot32(coefficients[k:], x, TN)
    basis_ref[...] = dot32(inverse, rest, NN)


def call(kernel, out_shape, n_in, scratch=(), limit=8 << 20, name=None):
    many = isinstance(out_shape, (tuple, list))
    return pl.pallas_call(
        kernel,
        out_shape=out_shape,
        in_specs=[VMEM_SPEC] * n_in,
        out_specs=tuple([VMEM_SPEC] * len(out_shape)) if many else VMEM_SPEC,
        scratch_shapes=list(scratch),
        compiler_params=pltpu.CompilerParams(vmem_limit_bytes=limit),
        name=name,
    )


def shape(*dims):
    return jax.ShapeDtypeStruct(dims, F32)


def on_device(n_row, n_col, coupling, energies, block):
    n, k = block.shape
    group = n_row
    order = n * n_row * n_col
    rows = coupling.shape[0] * n
    width = coupling.shape[2]
    axes = ("row", "col")
    flat = [(r, c) for r in range(n_row) for c in range(n_col)]

    def send(value, to):
        return lax.ppermute(value, axes, [(r * n_col + c, to(r, c)) for r, c in flat])

    def swap(value):
        return send(value, lambda r, c: r * n_col + (c ^ 1))

    def spread(s):
        return lambda r, c: (r ^ s) * n_col + c if c % 2 else r * n_col + (c ^ (2 * s))

    steps = range(1, group)
    tile = 256 if rows % 256 == 0 else rows
    a = pltpu.with_memory_space_constraint(coupling.reshape(rows, width), pltpu.VMEM)
    energy = energies.reshape(1, n)
    own = block.T
    other = swap(own)
    even = lax.rem(lax.axis_index("col"), 2) == 0
    first = jnp.concatenate([jnp.where(even, own, other), jnp.where(even, other, own)], axis=0)

    def products(pair, name):
        mine = [send(pair, spread(s)) for s in steps]
        theirs = [swap(y) for y in mine]
        kept, gone = pltpu.VMEM, BF16
        keep_send = call(
            functools.partial(product_kernel, k, n, group, tile),
            (shape(group, 2 * k, n), shape(group, 2 * k, n)),
            2 + 2 * (group - 1),
            scratch=[
                pltpu.VMEM((2 * k, width), BF16),
                pltpu.VMEM((2 * k, rows), BF16),
                pltpu.VMEM((group, k, n), F32),
                pltpu.VMEM((k, rows), F32),
                pltpu.VMEM((k, width), F32),
            ],
            limit=14 << 20,
            name=name,
        )(a, pair, *mine, *theirs)
        out, keep = keep_send
        got = swap(out)
        extra = pair.shape[0] > 2 * k
        parts = call(
            functools.partial(combine_kernel, k, n, group, extra),
            tuple([shape(pair.shape[0], n)] * group),
            4 + (group - 1 if extra else 0),
            name=name + "_combine",
        )(keep, got, pair, energy, *(theirs if extra else ()))
        total = parts[0]
        for s in steps:
            total = total + send(parts[s], spread(s))
        return total, swap(total)

    mine, got = products(first, "first")
    pair = call(functools.partial(pair_kernel, k, n), shape(2 * k + 8, n), 3, name="pair")(first, mine, got)
    mine, got = products(pair, "second")
    q, prod, moments, proj0, fact0 = call(
        functools.partial(second_kernel, k, n, order),
        (shape(2 * k, n), shape(2 * k, n), shape(3 * k, 3 * k), shape(k, k), shape(k, k)),
        4,
        name="middle",
    )(first, pair, mine, got)
    for s in [None]:
        moments = sum([send(moments, lambda r, c, s=s: (r ^ s) * n_col + c) for s in steps], moments)
    parts = [moments] + [send(moments, lambda r, c, s=s: r * n_col + (c ^ (2 * s))) for s in steps]
    basis, proj, fact = call(
        functools.partial(last_kernel, k, n, order, group),
        (shape(k, n), shape(2, k, k), shape(2, k, k)),
        5 + group,
        name="last",
    )(first, q, prod, proj0, fact0, *parts)
    return basis.T, proj, fact


def solution(mesh):
    n_row, n_col = mesh.shape["row"], mesh.shape["col"]

    def body(coupling, energies, block):
        n, k = block.shape
        paired = n_col == 2 * n_row and n_row & (n_row - 1) == 0 and n_row > 1
        whole = n % 64 == 0 and k % 8 == 0 and 8 * k == 128
        small = coupling.size * 4 <= 44 << 20
        if paired and whole and small:
            return on_device(n_row, n_col, coupling, energies, block)
        return generic(coupling, energies, block)

    placed = (P(None, "col", "row"), P(("row", "col")), P(("row", "col"), None))
    return jax.shard_map(
        body,
        mesh=mesh,
        in_specs=placed,
        out_specs=(P(("row", "col"), None), P(), P()),
        check_vma=False,
    )
```

```python
import functools

import jax
import jax.numpy as jnp
from jax import lax
from jax.experimental import pallas as pl
from jax.experimental.pallas import tpu as pltpu
from jax.sharding import PartitionSpec as P

ITERS = 2
F32 = jnp.float32
BF16 = jnp.bfloat16

precise = lax.Precision.HIGHEST

NN = (((1,), (0,)), ((), ()))
NT = (((1,), (1,)), ((), ()))
TN = (((0,), (0,)), ((), ()))

VMEM_SPEC = pl.BlockSpec(memory_space=pltpu.VMEM)


def generic(coupling, energies, block):
    order = block.shape[0] * lax.axis_size("row") * lax.axis_size("col")
    segment = block.shape[0]
    width = block.shape[1]
    column = lax.axis_index("col")
    current, energy_rows = (
        lax.all_gather(block, "col", axis=0, tiled=True),
        lax.all_gather(energies, "col", axis=0, tiled=True),
    )
    prior = jnp.zeros_like(current)
    projection_list = []
    factor_list = []
    for section in range(ITERS):
        own_rows = lax.dynamic_slice_in_dim(current, column * segment, segment, 0)
        spread = lax.all_gather(own_rows, "row", axis=0, tiled=True)
        spread = spread.reshape(coupling.shape[0], segment, width)
        direct = lax.psum_scatter(
            jnp.einsum("aig,gk->aik", coupling, current, precision=precise),
            "row",
            scatter_dimension=0,
            tiled=True,
        ).reshape(segment, width)
        partial_value = jnp.einsum("aig,aik->gk", coupling, spread, precision=precise)
        transposed = lax.psum(partial_value, "col")
        direct_rows = lax.all_gather(direct, "col", axis=0, tiled=True)
        product = energy_rows[:, None] * current + direct_rows + transposed
        stacked = jnp.concatenate([current, prior, product], axis=1)
        moments = lax.psum(jnp.einsum("nk,nl->kl", stacked, stacked, precision=precise), "row") / order
        projection = moments[:width, 2 * width :]
        cross = moments[width : 2 * width, 2 * width :]
        weights = jnp.concatenate([-projection, -cross, jnp.eye(width, dtype=F32)], axis=0)
        gram_matrix = jnp.dot(weights.T, jnp.dot(moments, weights, precision=precise), precision=precise)
        factor = jnp.linalg.cholesky(gram_matrix)
        residual = (
            product
            - jnp.dot(current, projection, precision=precise)
            - jnp.dot(prior, cross, precision=precise)
        )
        prior = current
        current = jax.scipy.linalg.solve_triangular(factor, residual.T, lower=True).T
        projection_list.append(projection)
        factor_list.append(factor)
    basis = lax.dynamic_slice_in_dim(current, column * segment, segment, 0)
    return (basis, jnp.stack(projection_list), jnp.stack(factor_list))


def place():
    column = lax.axis_index("col")
    return lax.rem(column, 2), lax.div(column, 2), lax.axis_index("row")


def split(value):
    high = value.astype(BF16)
    return high, (value - high.astype(F32)).astype(BF16)


def dot(left, right, dims):
    return lax.dot_general(left, right, dims, preferred_element_type=F32)


def dot32(left, right, dims):
    return lax.dot_general(left, right, dims, preferred_element_type=F32, precision=precise)


def order_kernel(k, own_ref, other_ref, out_ref):
    even = place()[0] == 0
    own, other = own_ref[...], other_ref[...]
    out_ref[:k, :] = jnp.where(even, own, other)
    out_ref[k:, :] = jnp.where(even, other, own)


def product_kernel(k, n, group, tile, chunk, pieces, load, *refs):
    sources, refs = refs[: 1 if load else pieces], refs[1 if load else pieces :]
    pair_ref, mine, theirs = refs[0], refs[1:group], refs[group : 2 * group - 1]
    send_ref, keep_ref, *refs = refs[2 * group - 1 :]
    if load:
        held, (xg, xr, rows, u_acc, v_acc, arrived) = refs[:pieces], refs[pieces:]
    else:
        held, (xg, xr, rows, u_acc, v_acc) = sources, refs
    def fetch(p):
        at = pl.ds(p * tile, tile)
        return pltpu.make_async_copy(sources[0].at[at, :], held[p], arrived.at[p])

    if load:
        for p in range(pieces):
            fetch(p).start()
    parity, z, r = place()
    even = parity == 0

    def put(slab, at, first, second):
        high, low = split(jnp.concatenate([first, second], axis=1))
        cols = pl.ds(pl.multiple_of(at * (2 * n), 2 * n), 2 * n)
        slab[:k, cols] = high
        slab[k:, cols] = low

    pair = pair_ref[: 2 * k, :]
    put(xg, z, pair[:k], pair[k:])
    rows[pl.ds(r, 1)] = jnp.where(even, pair[:k], pair[k:])[None]
    for s in range(1, group):
        y, w = mine[s - 1][: 2 * k, :], theirs[s - 1][: 2 * k, :]
        along_z = jnp.where(even, y, w)
        along_row = jnp.where(even, w, y)
        put(xg, lax.bitwise_xor(z, s), along_z[:k], along_z[k:])
        rows[pl.ds(lax.bitwise_xor(r, s), 1)] = jnp.where(even, along_row[:k], along_row[k:])[None]
    for a in range(0, group, 2):
        put(xr, a // 2, rows[a], rows[a + 1])

    v_acc[...] = jnp.zeros_like(v_acc)

    def step(piece, at, c, total):
        cols = pl.ds(pl.multiple_of(c * chunk, chunk), chunk)
        high, low = split(held[piece][:, cols])
        p = dot(xr[:, at], high, NN)
        q = dot(xr[:k, at], low, NN)
        v_acc[:, cols] += p[:k] + p[k:] + q
        p = dot(xg[:, cols], high, NT)
        q = dot(xg[:k, cols], low, NT)
        return total + p[:k] + p[k:] + q

    for piece in range(pieces):
        if load:
            fetch(piece).wait()
        at = slice(piece * tile, (piece + 1) * tile)
        u_acc[:, at] = lax.fori_loop(
            0, held[piece].shape[1] // chunk, functools.partial(step, piece, at), jnp.zeros((k, tile), F32)
        )

    def by_z(out):
        for g in range(group):
            both = v_acc[:, 2 * n * g : 2 * n * (g + 1)]
            out[g, :k, :] = both[:, :n]
            out[g, k:, :] = both[:, n:]

    def by_row(out, first):
        for a in range(0, group, 2):
            both = u_acc[:, n * a : n * (a + 2)]
            at = slice(0, k) if first else slice(k, 2 * k)
            rest = slice(k, 2 * k) if first else slice(0, k)
            out[a, at, :] = both[:, :n]
            out[a + 1, at, :] = both[:, n:]
            out[a, rest, :] = jnp.zeros((k, n), F32)
            out[a + 1, rest, :] = jnp.zeros((k, n), F32)

    @pl.when(even)
    def _():
        by_z(keep_ref)
        by_row(send_ref, True)

    @pl.when(jnp.logical_not(even))
    def _():
        by_z(send_ref)
        by_row(keep_ref, False)


def combine_kernel(k, n, group, extra, keep_ref, got_ref, pair_ref, energy_ref, *refs):
    theirs = refs[: group - 1] if extra else ()
    outs = refs[len(refs) - group :]
    parity, z, r = place()
    even = parity == 0
    at = jnp.where(even, z, r)
    for s in range(group):
        i = lax.bitwise_xor(at, s)
        total = keep_ref[pl.ds(i, 1)][0] + got_ref[pl.ds(i, 1)][0]
        if s == 0:
            own = energy_ref[...] * pair_ref[: 2 * k, :]
            row = lax.broadcasted_iota(jnp.int32, own.shape, 0)
            total = total + jnp.where((row < k) == even, own, 0.0)
        outs[s][: 2 * k, :] = total
    if extra:
        part = pair_ref[2 * k :, :]
        for w in theirs:
            part = part + w[2 * k :, :]
        part = jnp.where(even, part, jnp.zeros_like(part))
        for s in range(group):
            outs[s][2 * k :, :] = part


def pair_kernel(k, n, first_ref, mine_ref, got_ref, out_ref):
    value = mine_ref[...] + got_ref[...]
    out_ref[: 2 * k, :] = value
    moments = jnp.zeros((2 * k, 2 * k), F32)
    for p in range(2):
        s = jnp.concatenate([first_ref[p * k : (p + 1) * k, :], value[p * k : (p + 1) * k]], axis=0)
        moments = moments + dot32(s, s, NT)
    out_ref[2 * k :, :] = jnp.zeros((8, n), F32)
    for j in range(2 * k // 8):
        out_ref[2 * k : 2 * k + 8, 2 * k * j : 2 * k * (j + 1)] = moments[8 * j : 8 * (j + 1), :]


def factor_of(gram):
    k = gram.shape[0]
    rows = lax.broadcasted_iota(jnp.int32, (k, 2 * k), 0)
    cols = lax.broadcasted_iota(jnp.int32, (k, 2 * k), 1)
    row = lax.broadcasted_iota(jnp.int32, (k, 1), 0)
    both = jnp.concatenate([gram, jnp.where(rows == cols, 1.0, 0.0)[:, :k]], axis=1)
    lower = jnp.zeros((k, k), F32)
    for j in range(k):
        scale = 1.0 / jnp.sqrt(both[j : j + 1, j : j + 1])
        column = jnp.where(row >= j, both[:, j : j + 1] * scale, 0.0)
        lower = jnp.where(cols[:, :k] == j, column, lower)
        lead = both[j : j + 1, :] * scale
        below = jnp.where(row > j, column, 0.0)
        both = jnp.where(rows == j, lead, both - below * lead)
    return lower, both[:, k:]


def gram_of(moments, coefficients):
    k = moments.shape[0]
    w = coefficients.shape[1]
    parts = jnp.concatenate([-coefficients, eye(w)], axis=0)
    return dot32(parts, dot32(moments, parts, NN), TN)


def eye(k):
    return jnp.where(
        lax.broadcasted_iota(jnp.int32, (k, k), 0) == lax.broadcasted_iota(jnp.int32, (k, k), 1), 1.0, 0.0
    ).astype(F32)


def second_kernel(k, n, order, first_ref, pair_ref, mine_ref, got_ref, q_ref, prod_ref, mom_ref, proj_ref, fact_ref):
    packed = mine_ref[2 * k :, :] + got_ref[2 * k :, :]
    moments = jnp.concatenate(
        [packed[:, 2 * k * j : 2 * k * (j + 1)] for j in range(2 * k // 8)], axis=0
    ) * (1.0 / order)
    projection = moments[:k, k:]
    lower, inverse = factor_of(gram_of(moments, projection))
    proj_ref[...] = projection
    fact_ref[...] = lower
    total = jnp.zeros((3 * k, 3 * k), F32)
    for p in range(2):
        at = slice(p * k, (p + 1) * k)
        x, y = first_ref[at, :], pair_ref[at, :]
        w = mine_ref[at, :] + got_ref[at, :]
        q = dot32(inverse, y - dot32(projection, x, TN), NN)
        prod = dot32(inverse, w - dot32(projection, y, TN), NN)
        q_ref[at, :] = q
        prod_ref[at, :] = prod
        s = jnp.concatenate([q, x, prod], axis=0)
        total = total + dot32(s, s, NT)
    mom_ref[...] = total


def last_kernel(k, n, order, group, first_ref, q_ref, prod_ref, proj0_ref, fact0_ref, *refs):
    basis_ref, proj_ref, fact_ref = refs[group:]
    total = refs[0][...]
    for m in refs[1:group]:
        total = total + m[...]
    moments = total * (1.0 / order)
    coefficients = moments[: 2 * k, 2 * k :]
    lower, inverse = factor_of(gram_of(moments, coefficients))
    proj_ref[0] = proj0_ref[...]
    proj_ref[1] = coefficients[:k]
    fact_ref[0] = fact0_ref[...]
    fact_ref[1] = lower
    even = place()[0] == 0
    q = jnp.where(even, q_ref[:k, :], q_ref[k:, :])
    x = jnp.where(even, first_ref[:k, :], first_ref[k:, :])
    prod = jnp.where(even, prod_ref[:k, :], prod_ref[k:, :])
    rest = prod - dot32(coefficients[:k], q, TN) - dot32(coefficients[k:], x, TN)
    basis_ref[...] = dot32(inverse, rest, NN)


def call(kernel, out_shape, n_in, scratch=(), limit=1 << 20, name=None, load=False):
    many = isinstance(out_shape, (tuple, list))
    run = pl.pallas_call(
        kernel,
        out_shape=out_shape,
        in_specs=[pl.BlockSpec(memory_space=pl.ANY) if load and i == 0 else VMEM_SPEC for i in range(n_in)],
        out_specs=tuple([VMEM_SPEC] * len(out_shape)) if many else VMEM_SPEC,
        scratch_shapes=list(scratch),
        compiler_params=pltpu.CompilerParams(vmem_limit_bytes=limit),
        name=name,
    )

    def keep(i, v):
        return v if load and i == 0 else pltpu.with_memory_space_constraint(v, pltpu.VMEM)

    return lambda *args: run(*[keep(i, v) for i, v in enumerate(args)])


def shape(*dims):
    return jax.ShapeDtypeStruct(dims, F32)


def on_device(n_row, n_col, coupling, energies, block):
    n, k = block.shape
    group = n_row
    order = n * n_row * n_col
    rows = coupling.shape[0] * n
    width = coupling.shape[2]
    axes = ("row", "col")
    flat = [(r, c) for r in range(n_row) for c in range(n_col)]

    def send(value, to):
        return lax.ppermute(value, axes, [(r * n_col + c, to(r, c)) for r, c in flat])

    def swap(value):
        return send(value, lambda r, c: r * n_col + (c ^ 1))

    def spread(s):
        return lambda r, c: (r ^ s) * n_col + c if c % 2 else r * n_col + (c ^ (2 * s))

    steps = range(1, group)
    tile = 256
    pieces = rows // tile
    chunk = width // 3
    a = coupling.reshape(rows, width)
    energy = energies.reshape(1, n)
    own = block.T
    other = swap(own)
    first = call(functools.partial(order_kernel, k), shape(2 * k, n), 2, name="order")(own, other)

    def products(a, pair, name, load=False):
        mine = [send(pair, spread(s)) for s in steps]
        theirs = [swap(y) for y in mine]
        out, keep, *held = call(
            functools.partial(product_kernel, k, n, group, tile, chunk, pieces, load),
            (shape(group, 2 * k, n), shape(group, 2 * k, n))
            + ((shape(tile, width),) * pieces if load else ()),
            len(a) + 2 * group - 1,
            scratch=[
                pltpu.VMEM((2 * k, width), BF16),
                pltpu.VMEM((2 * k, rows), BF16),
                pltpu.VMEM((group, k, n), F32),
                pltpu.VMEM((k, rows), F32),
                pltpu.VMEM((k, width), F32),
            ]
            + ([pltpu.SemaphoreType.DMA((pieces,))] if load else []),
            limit=8 << 20,
            name=name,
            load=load,
        )(*a, pair, *mine, *theirs)
        got = swap(out)
        extra = pair.shape[0] > 2 * k
        parts = call(
            functools.partial(combine_kernel, k, n, group, extra),
            tuple([shape(pair.shape[0], n)] * group),
            4 + (group - 1 if extra else 0),
            name=name + "_combine",
        )(keep, got, pair, energy, *(theirs if extra else ()))
        total = parts[0]
        for s in steps:
            total = total + send(parts[s], spread(s))
        return total, swap(total), held

    mine, got, held = products([a], first, "first", load=True)
    pair = call(functools.partial(pair_kernel, k, n), shape(2 * k + 8, n), 3, name="pair")(first, mine, got)
    mine, got, _ = products(held, pair, "second")
    q, prod, moments, proj0, fact0 = call(
        functools.partial(second_kernel, k, n, order),
        (shape(2 * k, n), shape(2 * k, n), shape(3 * k, 3 * k), shape(k, k), shape(k, k)),
        4,
        name="middle",
    )(first, pair, mine, got)
    moments = sum([send(moments, lambda r, c, s=s: (r ^ s) * n_col + c) for s in steps], moments)
    parts = [moments] + [send(moments, lambda r, c, s=s: r * n_col + (c ^ (2 * s))) for s in steps]
    basis, proj, fact = call(
        functools.partial(last_kernel, k, n, order, group),
        (shape(k, n), shape(2, k, k), shape(2, k, k)),
        5 + group,
        name="last",
    )(first, q, prod, proj0, fact0, *parts)
    return basis.T, proj, fact


def solution(mesh):
    n_row, n_col = mesh.shape["row"], mesh.shape["col"]

    def body(coupling, energies, block):
        n, k = block.shape
        paired = n_col == 2 * n_row and n_row & (n_row - 1) == 0 and n_row > 1
        divides = coupling.shape[0] * n % 256 == 0
        whole = divides and n % 64 == 0 and 8 * k == 128 and coupling.shape[2] % 384 == 0
        small = coupling.size * 4 <= 44 << 20
        if paired and whole and small:
            return on_device(n_row, n_col, coupling, energies, block)
        return generic(coupling, energies, block)

    placed = (P(None, "col", "row"), P(("row", "col")), P(("row", "col"), None))
    return jax.shard_map(
        body,
        mesh=mesh,
        in_specs=placed,
        out_specs=(P(("row", "col"), None), P(), P()),
        check_vma=False,
    )
```

```python
import functools

import jax
import jax.numpy as jnp
from jax import lax
from jax.experimental import pallas as pl
from jax.experimental.pallas import tpu as pltpu
from jax.sharding import PartitionSpec as P

ITERS = 2
F32 = jnp.float32
BF16 = jnp.bfloat16

precise = lax.Precision.HIGHEST

NN = (((1,), (0,)), ((), ()))
NT = (((1,), (1,)), ((), ()))
TN = (((0,), (0,)), ((), ()))

VMEM_SPEC = pl.BlockSpec(memory_space=pltpu.VMEM)


def generic(coupling, energies, block):
    order = block.shape[0] * lax.axis_size("row") * lax.axis_size("col")
    segment = block.shape[0]
    width = block.shape[1]
    column = lax.axis_index("col")
    current, energy_rows = (
        lax.all_gather(block, "col", axis=0, tiled=True),
        lax.all_gather(energies, "col", axis=0, tiled=True),
    )
    prior = jnp.zeros_like(current)
    projection_list = []
    factor_list = []
    for section in range(ITERS):
        own_rows = lax.dynamic_slice_in_dim(current, column * segment, segment, 0)
        spread = lax.all_gather(own_rows, "row", axis=0, tiled=True)
        spread = spread.reshape(coupling.shape[0], segment, width)
        direct = lax.psum_scatter(
            jnp.einsum("aig,gk->aik", coupling, current, precision=precise),
            "row",
            scatter_dimension=0,
            tiled=True,
        ).reshape(segment, width)
        partial_value = jnp.einsum("aig,aik->gk", coupling, spread, precision=precise)
        transposed = lax.psum(partial_value, "col")
        direct_rows = lax.all_gather(direct, "col", axis=0, tiled=True)
        product = energy_rows[:, None] * current + direct_rows + transposed
        stacked = jnp.concatenate([current, prior, product], axis=1)
        moments = lax.psum(jnp.einsum("nk,nl->kl", stacked, stacked, precision=precise), "row") / order
        projection = moments[:width, 2 * width :]
        cross = moments[width : 2 * width, 2 * width :]
        weights = jnp.concatenate([-projection, -cross, jnp.eye(width, dtype=F32)], axis=0)
        gram_matrix = jnp.dot(weights.T, jnp.dot(moments, weights, precision=precise), precision=precise)
        factor = jnp.linalg.cholesky(gram_matrix)
        residual = (
            product
            - jnp.dot(current, projection, precision=precise)
            - jnp.dot(prior, cross, precision=precise)
        )
        prior = current
        current = jax.scipy.linalg.solve_triangular(factor, residual.T, lower=True).T
        projection_list.append(projection)
        factor_list.append(factor)
    basis = lax.dynamic_slice_in_dim(current, column * segment, segment, 0)
    return (basis, jnp.stack(projection_list), jnp.stack(factor_list))


def place():
    column = lax.axis_index("col")
    return lax.rem(column, 2), lax.div(column, 2), lax.axis_index("row")


def split(value):
    high = value.astype(BF16)
    return high, (value - high.astype(F32)).astype(BF16)


def dot(left, right, dims):
    return lax.dot_general(left, right, dims, preferred_element_type=F32)


def dot32(left, right, dims):
    return lax.dot_general(left, right, dims, preferred_element_type=F32, precision=precise)


def order_kernel(k, own_ref, other_ref, out_ref):
    even = place()[0] == 0
    own, other = own_ref[...], other_ref[...]
    out_ref[:k, :] = jnp.where(even, own, other)
    out_ref[k:, :] = jnp.where(even, other, own)


def pieces_of(part, group, n, rows):
    found, at, end = [], part * rows, (part + 1) * rows
    while at < end:
        s, off = divmod(at, n)
        count = min(n - off, end - at)
        found.append((s, off, at - part * rows, count))
        at += count
    return found


class Loader:
    def __init__(self, source, arrived, n, group, parts, r, z):
        self.source, self.arrived, self.n, self.group, self.parts, self.r, self.z = source, arrived, n, group, parts, r, z
        self.rows = group * n // parts

    def copies(self, number, part, s, into):
        cols = pl.ds(pl.multiple_of(lax.bitwise_xor(self.z, s) * (2 * self.n), 128), 2 * self.n)
        return [
            pltpu.make_async_copy(
                self.source.at[pl.ds(pl.multiple_of(lax.bitwise_xor(self.r, peer) * self.n + off, 8), count), cols],
                into.at[pl.ds(at, count), :],
                self.arrived.at[number, i],
            )
            for i, (peer, off, at, count) in enumerate(pieces_of(part, self.group, self.n, self.rows))
        ]

    def start(self, *where):
        for copy in self.copies(*where):
            copy.start()

    def wait(self, *where):
        for copy in self.copies(*where):
            copy.wait()


def both_halves(slab, at, k, n, first, second):
    high, low = split(jnp.concatenate([first, second], axis=1))
    slab[:k, at * 2 * n : (at + 1) * 2 * n] = high
    slab[k:, at * 2 * n : (at + 1) * 2 * n] = low


def early_kernel(k, n, group, tile, parts, load, *refs):
    parity, z, r = place()
    if load:
        source, pair_ref, u_ref, *held, xg, arrived = refs
        loader = Loader(source, arrived, n, group, parts, r, z)
        for p in range(parts):
            loader.start(p, p, 0, held[p])
    else:
        *held, pair_ref, u_ref, xg = refs
    both_halves(xg, 0, k, n, pair_ref[:k, :], pair_ref[k : 2 * k, :])
    rows = held[0].shape[0]

    def step(p, t, carry):
        high, low = split(held[p][pl.ds(pl.multiple_of(t * tile, tile), tile), :])
        one = dot(xg[...], high, NT)
        two = dot(xg[:k, :], low, NT)
        u_ref[:, pl.ds(pl.multiple_of(p * rows + t * tile, tile), tile)] = one[:k] + one[k:] + two
        return carry

    for p in range(parts):
        if load:
            loader.wait(p, p, 0, held[p])
        lax.fori_loop(0, rows // tile, functools.partial(step, p), 0)


def main_kernel(k, n, group, tile, parts, load, *refs):
    parity, z, r = place()
    even = parity == 0
    count = (group - 1) * parts
    if load:
        source, refs = refs[0], refs[1:]
    else:
        held, refs = refs[:count], refs[count:]
    pair_ref, u0_ref, mine, theirs = refs[0], refs[1], refs[2 : group + 1], refs[group + 1 : 2 * group]
    send_ref, keep_ref, own_ref, xr, *refs = refs[2 * group :]
    if load:
        held, refs = refs[:count], refs[count:]
        xg, u_acc, v_acc, arrived = refs
        loader = Loader(source, arrived, n, group, parts, r, z)
        for i in range(count):
            loader.start(i, i % parts, 1 + i // parts, held[i])
    else:
        xg, u_acc, v_acc = refs
    rows = held[0].shape[0]

    segments = [jnp.where(even, pair_ref[:k, :], pair_ref[k : 2 * k, :])]
    for s in range(1, group):
        y, w = mine[s - 1][: 2 * k, :], theirs[s - 1][: 2 * k, :]
        along_z = jnp.where(even, y, w)
        along_row = jnp.where(even, w, y)
        both_halves(xg, s - 1, k, n, along_z[:k], along_z[k:])
        segments.append(jnp.where(even, along_row[:k], along_row[k:]))
    for a in range(0, group, 2):
        both_halves(xr, a // 2, k, n, segments[a], segments[a + 1])
    u_acc[...] = u0_ref[...]
    v_acc[...] = jnp.zeros_like(v_acc)

    def step(i, t, carry):
        s, p = divmod(i, parts)
        cols = slice(s * 2 * n, (s + 1) * 2 * n)
        at = pl.ds(pl.multiple_of(p * rows + t * tile, tile), tile)
        high, low = split(held[i][pl.ds(pl.multiple_of(t * tile, tile), tile), :])
        one = dot(xr[:, at], high, NN)
        two = dot(xr[:k, at], low, NN)
        v_acc[:, cols] += one[:k] + one[k:] + two
        one = dot(xg[:, cols], high, NT)
        two = dot(xg[:k, cols], low, NT)
        u_acc[:, at] += one[:k] + one[k:] + two
        return carry

    for i in range(count):
        if load:
            loader.wait(i, i % parts, 1 + i // parts, held[i])
        lax.fori_loop(0, rows // tile, functools.partial(step, i), 0)

    own_ref[...] = u_acc[:, :n]

    def by_z(out):
        for s in range(1, group):
            both = v_acc[:, 2 * n * (s - 1) : 2 * n * s]
            out[s - 1, :k, :] = both[:, :n]
            out[s - 1, k:, :] = both[:, n:]

    def by_row(out, first):
        at = slice(0, k) if first else slice(k, 2 * k)
        rest = slice(k, 2 * k) if first else slice(0, k)
        for a in range(0, group, 2):
            both = u_acc[:, n * a : n * (a + 2)]
            for s in (a, a + 1):
                if s:
                    out[s - 1, at, :] = both[:, n * (s - a) : n * (s - a + 1)]
                    out[s - 1, rest, :] = jnp.zeros((k, n), F32)

    @pl.when(even)
    def _():
        by_z(keep_ref)
        by_row(send_ref, True)

    @pl.when(jnp.logical_not(even))
    def _():
        by_z(send_ref)
        by_row(keep_ref, False)


def late_kernel(k, n, group, tile, parts, extra, *refs):
    held, refs = refs[:parts], refs[parts:]
    xr, own_ref, pair_ref, energy_ref, *refs = refs
    more, refs = (refs[0], refs[1:]) if extra else (None, refs)
    out_ref, v_acc = refs
    even = place()[0] == 0
    rows = held[0].shape[0]
    v_acc[...] = jnp.zeros_like(v_acc)

    def step(p, t, carry):
        at = pl.ds(pl.multiple_of(p * rows + t * tile, tile), tile)
        high, low = split(held[p][pl.ds(pl.multiple_of(t * tile, tile), tile), :])
        one = dot(xr[:, at], high, NN)
        two = dot(xr[:k, at], low, NN)
        v_acc[...] += one[:k] + one[k:] + two
        return carry

    for p in range(parts):
        lax.fori_loop(0, rows // tile, functools.partial(step, p), 0)
    own = jnp.where(even, pair_ref[:k, :], pair_ref[k : 2 * k, :])
    own = energy_ref[...] * own + own_ref[...]
    zero = jnp.zeros_like(own)
    both = v_acc[...]
    out_ref[:k, :] = both[:, :n] + jnp.where(even, own, zero)
    out_ref[k : 2 * k, :] = both[:, n:] + jnp.where(even, zero, own)
    if extra:
        out_ref[2 * k :, :] = more[...]


def combine_kernel(k, n, group, extra, keep_ref, got_ref, *refs):
    if extra:
        pair_ref, theirs, outs = refs[0], refs[1:group], refs[group:]
    else:
        outs = refs
    for s in range(1, group):
        outs[s - 1][: 2 * k, :] = keep_ref[s - 1] + got_ref[s - 1]
    if extra:
        part = pair_ref[2 * k :, :]
        for w in theirs:
            part = part + w[2 * k :, :]
        part = jnp.where(place()[0] == 0, part, jnp.zeros_like(part))
        for s in range(1, group):
            outs[s - 1][2 * k :, :] = part
        outs[group - 1][...] = part


def pair_kernel(k, n, first_ref, mine_ref, got_ref, out_ref):
    value = mine_ref[...] + got_ref[...]
    out_ref[: 2 * k, :] = value
    moments = jnp.zeros((2 * k, 2 * k), F32)
    for p in range(2):
        s = jnp.concatenate([first_ref[p * k : (p + 1) * k, :], value[p * k : (p + 1) * k]], axis=0)
        moments = moments + dot32(s, s, NT)
    out_ref[2 * k :, :] = jnp.zeros((8, n), F32)
    for j in range(2 * k // 8):
        out_ref[2 * k : 2 * k + 8, 2 * k * j : 2 * k * (j + 1)] = moments[8 * j : 8 * (j + 1), :]


def factor_of(gram):
    k = gram.shape[0]
    rows = lax.broadcasted_iota(jnp.int32, (k, 2 * k), 0)
    cols = lax.broadcasted_iota(jnp.int32, (k, 2 * k), 1)
    row = lax.broadcasted_iota(jnp.int32, (k, 1), 0)
    both = jnp.concatenate([gram, jnp.where(rows == cols, 1.0, 0.0)[:, :k]], axis=1)
    lower = jnp.zeros((k, k), F32)
    for j in range(k):
        scale = 1.0 / jnp.sqrt(both[j : j + 1, j : j + 1])
        column = jnp.where(row >= j, both[:, j : j + 1] * scale, 0.0)
        lower = jnp.where(cols[:, :k] == j, column, lower)
        lead = both[j : j + 1, :] * scale
        below = jnp.where(row > j, column, 0.0)
        both = jnp.where(rows == j, lead, both - below * lead)
    return lower, both[:, k:]


def gram_of(moments, coefficients):
    k = moments.shape[0]
    w = coefficients.shape[1]
    parts = jnp.concatenate([-coefficients, eye(w)], axis=0)
    return dot32(parts, dot32(moments, parts, NN), TN)


def eye(k):
    return jnp.where(
        lax.broadcasted_iota(jnp.int32, (k, k), 0) == lax.broadcasted_iota(jnp.int32, (k, k), 1), 1.0, 0.0
    ).astype(F32)


def second_kernel(k, n, order, first_ref, pair_ref, mine_ref, got_ref, q_ref, prod_ref, mom_ref, proj_ref, fact_ref):
    packed = mine_ref[2 * k :, :] + got_ref[2 * k :, :]
    moments = jnp.concatenate(
        [packed[:, 2 * k * j : 2 * k * (j + 1)] for j in range(2 * k // 8)], axis=0
    ) * (1.0 / order)
    projection = moments[:k, k:]
    lower, inverse = factor_of(gram_of(moments, projection))
    proj_ref[...] = projection
    fact_ref[...] = lower
    total = jnp.zeros((3 * k, 3 * k), F32)
    for p in range(2):
        at = slice(p * k, (p + 1) * k)
        x, y = first_ref[at, :], pair_ref[at, :]
        w = mine_ref[at, :] + got_ref[at, :]
        q = dot32(inverse, y - dot32(projection, x, TN), NN)
        prod = dot32(inverse, w - dot32(projection, y, TN), NN)
        q_ref[at, :] = q
        prod_ref[at, :] = prod
        s = jnp.concatenate([q, x, prod], axis=0)
        total = total + dot32(s, s, NT)
    mom_ref[...] = total


def last_kernel(k, n, order, group, first_ref, q_ref, prod_ref, proj0_ref, fact0_ref, *refs):
    basis_ref, proj_ref, fact_ref = refs[group:]
    total = refs[0][...]
    for m in refs[1:group]:
        total = total + m[...]
    moments = total * (1.0 / order)
    coefficients = moments[: 2 * k, 2 * k :]
    lower, inverse = factor_of(gram_of(moments, coefficients))
    proj_ref[0] = proj0_ref[...]
    proj_ref[1] = coefficients[:k]
    fact_ref[0] = fact0_ref[...]
    fact_ref[1] = lower
    even = place()[0] == 0
    q = jnp.where(even, q_ref[:k, :], q_ref[k:, :])
    x = jnp.where(even, first_ref[:k, :], first_ref[k:, :])
    prod = jnp.where(even, prod_ref[:k, :], prod_ref[k:, :])
    rest = prod - dot32(coefficients[:k], q, TN) - dot32(coefficients[k:], x, TN)
    basis_ref[...] = dot32(inverse, rest, NN)


def call(kernel, out_shape, n_in, scratch=(), limit=1 << 20, name=None, load=False, flops=0):
    many = isinstance(out_shape, (tuple, list))
    run = pl.pallas_call(
        kernel,
        out_shape=out_shape,
        in_specs=[pl.BlockSpec(memory_space=pl.ANY) if load and i == 0 else VMEM_SPEC for i in range(n_in)],
        out_specs=tuple([VMEM_SPEC] * len(out_shape)) if many else VMEM_SPEC,
        scratch_shapes=list(scratch),
        compiler_params=pltpu.CompilerParams(vmem_limit_bytes=limit),
        cost_estimate=pl.CostEstimate(flops=flops, transcendentals=0, bytes_accessed=flops // 128) if flops else None,
        name=name,
    )

    def keep(i, v):
        return v if load and i == 0 else pltpu.with_memory_space_constraint(v, pltpu.VMEM)

    return lambda *args: run(*[keep(i, v) for i, v in enumerate(args)])


def shape(*dims):
    return jax.ShapeDtypeStruct(dims, F32)


def on_device(n_row, n_col, coupling, energies, block):
    n, k = block.shape
    group = n_row
    order = n * n_row * n_col
    rows = coupling.shape[0] * n
    width = coupling.shape[2]
    axes = ("row", "col")
    flat = [(r, c) for r in range(n_row) for c in range(n_col)]

    def send(value, to):
        return lax.ppermute(value, axes, [(r * n_col + c, to(r, c)) for r, c in flat])

    def swap(value):
        return send(value, lambda r, c: r * n_col + (c ^ 1))

    def spread(s):
        return lambda r, c: (r ^ s) * n_col + c if c % 2 else r * n_col + (c ^ (2 * s))

    steps = range(1, group)
    tile = 256
    parts = 3
    a = coupling.reshape(rows, width)
    energy = energies.reshape(1, n)
    own = block.T
    other = swap(own)
    first = call(functools.partial(order_kernel, k), shape(2 * k, n), 2, name="order")(own, other)

    def products(a, pair, name, load=False):
        extra = pair.shape[0] > 2 * k
        block = (shape(rows // parts, 2 * n),) * parts
        sizes = (k, n, group, tile, parts)
        work = rows * 2 * n * 256
        count = (group - 1) * parts
        most = max(len(pieces_of(p, group, n, rows // parts)) for p in range(parts))
        mine = [send(pair, spread(s)) for s in steps]
        u0, *near = call(
            functools.partial(early_kernel, *sizes, load),
            (shape(k, rows),) + (block if load else ()),
            2 if load else 1 + parts,
            scratch=[pltpu.VMEM((2 * k, 2 * n), BF16)] + ([pltpu.SemaphoreType.DMA((parts, most))] if load else []),
            limit=8 << 20,
            name=name + "_early",
            flops=2 * work,
            load=load,
        )(*([a] if load else a[:parts]), pair)
        u0, *mine = lax.optimization_barrier((u0, *mine))
        theirs = [swap(y) for y in mine]
        out, keep, own, xr, *far = call(
            functools.partial(main_kernel, *sizes, load),
            (shape(group - 1, 2 * k, n), shape(group - 1, 2 * k, n), shape(k, n), jax.ShapeDtypeStruct((2 * k, rows), BF16))
            + (block * (group - 1) if load else ()),
            (1 if load else count) + 2 * group,
            scratch=[
                pltpu.VMEM((2 * k, (group - 1) * 2 * n), BF16),
                pltpu.VMEM((k, rows), F32),
                pltpu.VMEM((k, (group - 1) * 2 * n), F32),
            ]
            + ([pltpu.SemaphoreType.DMA((count, most))] if load else []),
            limit=8 << 20,
            name=name,
            load=load,
            flops=4 * work * (group - 1),
        )(*([a] if load else a[parts:]), pair, u0, *mine, *theirs)
        held = near + far if load else a
        got = swap(out)
        parts_out = call(
            functools.partial(combine_kernel, k, n, group, extra),
            (shape(pair.shape[0], n),) * (group - 1) + ((shape(8, n),) if extra else ()),
            2 + (group if extra else 0),
            name=name + "_combine",
        )(keep, got, *((pair, *theirs) if extra else ()))
        arrived = [send(parts_out[s - 1], spread(s)) for s in steps]
        total = call(
            functools.partial(late_kernel, *sizes, extra),
            shape(pair.shape[0], n),
            parts + 4 + extra,
            scratch=[pltpu.VMEM((k, 2 * n), F32)],
            limit=8 << 20,
            name=name + "_late",
            flops=2 * work,
        )(*held[:parts], xr, own, pair, energy, *parts_out[group - 1 :])
        for v in arrived:
            total = total + v
        return total, swap(total), held

    mine, got, held = products(a, first, "first", load=True)
    pair = call(functools.partial(pair_kernel, k, n), shape(2 * k + 8, n), 3, name="pair")(first, mine, got)
    mine, got, _ = products(held, pair, "second")
    q, prod, moments, proj0, fact0 = call(
        functools.partial(second_kernel, k, n, order),
        (shape(2 * k, n), shape(2 * k, n), shape(3 * k, 3 * k), shape(k, k), shape(k, k)),
        4,
        name="middle",
    )(first, pair, mine, got)
    moments = sum([send(moments, lambda r, c, s=s: (r ^ s) * n_col + c) for s in steps], moments)
    parts = [moments] + [send(moments, lambda r, c, s=s: r * n_col + (c ^ (2 * s))) for s in steps]
    basis, proj, fact = call(
        functools.partial(last_kernel, k, n, order, group),
        (shape(k, n), shape(2, k, k), shape(2, k, k)),
        5 + group,
        name="last",
    )(first, q, prod, proj0, fact0, *parts)
    return basis.T, proj, fact


def solution(mesh):
    n_row, n_col = mesh.shape["row"], mesh.shape["col"]

    def body(coupling, energies, block):
        n, k = block.shape
        paired = n_col == 2 * n_row and n_row & (n_row - 1) == 0 and n_row > 1
        divides = coupling.shape[0] * n % 768 == 0
        whole = divides and n % 64 == 0 and 8 * k == 128 and coupling.shape[2] == coupling.shape[0] * n * 2
        small = coupling.size * 4 <= 44 << 20
        if paired and whole and small:
            return on_device(n_row, n_col, coupling, energies, block)
        return generic(coupling, energies, block)

    placed = (P(None, "col", "row"), P(("row", "col")), P(("row", "col"), None))
    return jax.shard_map(
        body,
        mesh=mesh,
        in_specs=placed,
        out_specs=(P(("row", "col"), None), P(), P()),
        check_vma=False,
    )
```

```python
import functools

import jax
import jax.numpy as jnp
from jax import lax
from jax.experimental import pallas as pl
from jax.experimental.pallas import tpu as pltpu
from jax.sharding import PartitionSpec as P

ITERS = 2
F32 = jnp.float32
BF16 = jnp.bfloat16

precise = lax.Precision.HIGHEST

NN = (((1,), (0,)), ((), ()))
NT = (((1,), (1,)), ((), ()))
TN = (((0,), (0,)), ((), ()))

VMEM_SPEC = pl.BlockSpec(memory_space=pltpu.VMEM)


def generic(coupling, energies, block):
    order = block.shape[0] * lax.axis_size("row") * lax.axis_size("col")
    segment = block.shape[0]
    width = block.shape[1]
    column = lax.axis_index("col")
    current, energy_rows = (
        lax.all_gather(block, "col", axis=0, tiled=True),
        lax.all_gather(energies, "col", axis=0, tiled=True),
    )
    prior = jnp.zeros_like(current)
    projection_list = []
    factor_list = []
    for section in range(ITERS):
        own_rows = lax.dynamic_slice_in_dim(current, column * segment, segment, 0)
        spread = lax.all_gather(own_rows, "row", axis=0, tiled=True)
        spread = spread.reshape(coupling.shape[0], segment, width)
        direct = lax.psum_scatter(
            jnp.einsum("aig,gk->aik", coupling, current, precision=precise),
            "row",
            scatter_dimension=0,
            tiled=True,
        ).reshape(segment, width)
        partial_value = jnp.einsum("aig,aik->gk", coupling, spread, precision=precise)
        transposed = lax.psum(partial_value, "col")
        direct_rows = lax.all_gather(direct, "col", axis=0, tiled=True)
        product = energy_rows[:, None] * current + direct_rows + transposed
        stacked = jnp.concatenate([current, prior, product], axis=1)
        moments = lax.psum(jnp.einsum("nk,nl->kl", stacked, stacked, precision=precise), "row") / order
        projection = moments[:width, 2 * width :]
        cross = moments[width : 2 * width, 2 * width :]
        weights = jnp.concatenate([-projection, -cross, jnp.eye(width, dtype=F32)], axis=0)
        gram_matrix = jnp.dot(weights.T, jnp.dot(moments, weights, precision=precise), precision=precise)
        factor = jnp.linalg.cholesky(gram_matrix)
        residual = (
            product
            - jnp.dot(current, projection, precision=precise)
            - jnp.dot(prior, cross, precision=precise)
        )
        prior = current
        current = jax.scipy.linalg.solve_triangular(factor, residual.T, lower=True).T
        projection_list.append(projection)
        factor_list.append(factor)
    basis = lax.dynamic_slice_in_dim(current, column * segment, segment, 0)
    return (basis, jnp.stack(projection_list), jnp.stack(factor_list))


def place():
    column = lax.axis_index("col")
    return lax.rem(column, 2), lax.div(column, 2), lax.axis_index("row")


def split(value):
    high = value.astype(BF16)
    return high, (value - high.astype(F32)).astype(BF16)


def dot(left, right, dims):
    return lax.dot_general(left, right, dims, preferred_element_type=F32)


def dot32(left, right, dims):
    return lax.dot_general(left, right, dims, preferred_element_type=F32, precision=precise)


def own_half(value, even, n):
    return jnp.where(even, value[:, :n], value[:, n : 2 * n])


def in_half(value, even):
    zero = jnp.zeros_like(value)
    return jnp.concatenate([jnp.where(even, value, zero), jnp.where(even, zero, value)], axis=1)


def pieces_of(part, group, n, rows):
    found, at, end = [], part * rows, (part + 1) * rows
    while at < end:
        s, off = divmod(at, n)
        count = min(n - off, end - at)
        found.append((s, off, at - part * rows, count))
        at += count
    return found


class Loader:
    def __init__(self, source, arrived, n, group, parts, first, held):
        _, z, r = place()
        self.held, self.first = held, first

        def copies(i):
            cols = pl.ds(pl.multiple_of(lax.bitwise_xor(z, (first + i) // parts) * (2 * n), 128), 2 * n)
            return [
                pltpu.make_async_copy(
                    source.at[pl.ds(pl.multiple_of(lax.bitwise_xor(r, peer) * n + off, 8), count), cols],
                    held[i].at[pl.ds(at, count), :],
                    arrived.at[i, j],
                )
                for j, (peer, off, at, count) in enumerate(
                    pieces_of((first + i) % parts, group, n, group * n // parts)
                )
            ]

        self.copies = copies
        for i in range(len(held)):
            for copy in copies(i):
                copy.start()

    def wait(self, i):
        for copy in self.copies(i):
            copy.wait()


def begin_kernel(k, n, group, parts, source, block_ref, own_ref, *refs):
    *held, arrived, ready = refs
    copy = pltpu.make_async_copy(block_ref, own_ref, ready)
    copy.start()
    loader = Loader(source, arrived, n, group, parts, 0, held)
    copy.wait()
    for i in range(len(held)):
        loader.wait(i)


def order_kernel(k, n, own_ref, other_ref, out_ref):
    even = place()[0] == 0
    own, other = own_ref[...], other_ref[...]
    out_ref[...] = jnp.concatenate([jnp.where(even, own, other), jnp.where(even, other, own)], axis=1)


def put(slab, at, k, value):
    high, low = split(value)
    slab[:k, at : at + value.shape[1]] = high
    slab[k:, at : at + value.shape[1]] = low


def early_kernel(k, n, group, tile, parts, given, new, *refs):
    source, refs = (refs[0], refs[1:]) if new else (None, refs)
    held, refs = list(refs[:given]), refs[given:]
    pair_ref, u_ref, *refs = refs
    if new:
        *fresh, xg, arrived = refs
        loader = Loader(source, arrived, n, group, parts, given, fresh)
        held = held + fresh
    else:
        (xg,) = refs
    put(xg, 0, k, pair_ref[:, : 2 * n])
    rows = held[0].shape[0]

    def step(p, t, carry):
        high, low = split(held[p][pl.ds(pl.multiple_of(t * tile, tile), tile), :])
        one = dot(xg[...], high, NT)
        two = dot(xg[:k, :], low, NT)
        u_ref[:, pl.ds(pl.multiple_of(p * rows + t * tile, tile), tile)] = one[:k] + one[k:] + two
        return carry

    for p in range(parts):
        if p >= given:
            loader.wait(p - given)
        lax.fori_loop(0, rows // tile, functools.partial(step, p), 0)
    for p in range(parts, given + new):
        loader.wait(p - given)


def turned(s, group, even):
    return jnp.logical_not(even) if s == group - 1 else even


def main_kernel(k, n, group, tile, parts, given, new, *refs):
    even = place()[0] == 0
    source, refs = (refs[0], refs[1:]) if new else (None, refs)
    held, refs = list(refs[:given]), refs[given:]
    pair_ref, u0_ref, mine, theirs = refs[0], refs[1], refs[2 : group + 1], refs[group + 1 : 2 * group]
    send_ref, keep_ref, own_ref, xr, *refs = refs[2 * group :]
    if new:
        *fresh, xg, u_acc, v_acc, arrived = refs
        loader = Loader(source, arrived, n, group, parts, parts + given, fresh)
        held = held + fresh
    else:
        xg, u_acc, v_acc = refs
    rows = held[0].shape[0]

    segments = [own_half(pair_ref, even, n)]
    for s in range(1, group):
        y, w = mine[s - 1][:, : 2 * n], theirs[s - 1][:, : 2 * n]
        along = turned(s, group, even)
        put(xg, (s - 1) * 2 * n, k, jnp.where(along, y, w))
        segments.append(own_half(jnp.where(along, w, y), even, n))
    for a in range(0, group, 2):
        put(xr, a * n, k, jnp.concatenate(segments[a : a + 2], axis=1))
    u_acc[...] = u0_ref[...]
    v_acc[...] = jnp.zeros_like(v_acc)

    def step(i, t, carry):
        s, p = divmod(i, parts)
        cols = slice(s * 2 * n, (s + 1) * 2 * n)
        at = pl.ds(pl.multiple_of(p * rows + t * tile, tile), tile)
        high, low = split(held[i][pl.ds(pl.multiple_of(t * tile, tile), tile), :])
        one = dot(xr[:, at], high, NN)
        two = dot(xr[:k, at], low, NN)
        v_acc[:, cols] += one[:k] + one[k:] + two
        one = dot(xg[:, cols], high, NT)
        two = dot(xg[:k, cols], low, NT)
        u_acc[:, at] += one[:k] + one[k:] + two
        return carry

    for i in range(len(held)):
        if i >= given:
            loader.wait(i - given)
        lax.fori_loop(0, rows // tile, functools.partial(step, i), 0)

    own_ref[...] = u_acc[:, :n]
    for s in range(1, group):
        along = turned(s, group, even)
        by_z = v_acc[:, 2 * n * (s - 1) : 2 * n * s]
        by_row = in_half(u_acc[:, n * s : n * (s + 1)], even)
        keep_ref[s - 1] = jnp.where(along, by_z, by_row)
        send_ref[s - 1] = jnp.where(along, by_row, by_z)


def late_kernel(k, n, group, tile, parts, extra, *refs):
    held, refs = refs[:parts], refs[parts:]
    xr, own_ref, pair_ref, energy_ref, *refs = refs
    more, refs = (refs[0], refs[1:]) if extra else (None, refs)
    out_ref, v_acc = refs
    even = place()[0] == 0
    rows = held[0].shape[0]
    v_acc[...] = jnp.zeros_like(v_acc)

    def step(p, t, carry):
        at = pl.ds(pl.multiple_of(p * rows + t * tile, tile), tile)
        high, low = split(held[p][pl.ds(pl.multiple_of(t * tile, tile), tile), :])
        one = dot(xr[:, at], high, NN)
        two = dot(xr[:k, at], low, NN)
        v_acc[...] += one[:k] + one[k:] + two
        return carry

    for p in range(parts):
        lax.fori_loop(0, rows // tile, functools.partial(step, p), 0)
    own = energy_ref[...] * own_half(pair_ref, even, n) + own_ref[...]
    out_ref[:, : 2 * n] = v_acc[...] + in_half(own, even)
    if extra:
        part = more[...]
        out_ref[:, 2 * n :] = jnp.where(even, part, jnp.zeros_like(part))


def combine_kernel(k, n, group, extra, keep_ref, got_ref, *refs):
    even = place()[0] == 0
    if extra:
        pair_ref, mine, theirs, outs = refs[0], refs[1:group], refs[group : 2 * group - 1], refs[2 * group - 1 :]
        part = pair_ref[:, 2 * n :]
        for s in range(1, group):
            along = turned(s, group, even)
            part = part + jnp.where(along, theirs[s - 1][:, 2 * n :], mine[s - 1][:, 2 * n :])
        outs[group - 1][...] = part
    else:
        outs = refs
    for s in range(1, group):
        outs[s - 1][:, : 2 * n] = keep_ref[s - 1] + got_ref[s - 1]
        if extra:
            outs[s - 1][:, 2 * n :] = jnp.where(turned(s, group, even), part, jnp.zeros_like(part))


def pair_kernel(k, n, first_ref, mine_ref, got_ref, out_ref):
    value = mine_ref[...] + got_ref[...]
    s = jnp.concatenate([first_ref[...], value], axis=0)
    moments = dot32(s, s, NT)
    out_ref[:, : 2 * n] = value
    out_ref[:, 2 * n :] = jnp.zeros((k, 8 * k), F32)
    out_ref[:, 2 * n : 2 * n + 2 * k] = moments[:k]
    out_ref[:, 2 * n + 2 * k : 2 * n + 4 * k] = moments[k:]


def factor_of(gram):
    k = gram.shape[0]
    rows = lax.broadcasted_iota(jnp.int32, (k, 2 * k), 0)
    cols = lax.broadcasted_iota(jnp.int32, (k, 2 * k), 1)
    row = lax.broadcasted_iota(jnp.int32, (k, 1), 0)
    both = jnp.concatenate([gram, jnp.where(rows == cols, 1.0, 0.0)[:, :k]], axis=1)
    lower = jnp.zeros((k, k), F32)
    for j in range(k):
        scale = 1.0 / jnp.sqrt(both[j : j + 1, j : j + 1])
        column = jnp.where(row >= j, both[:, j : j + 1] * scale, 0.0)
        lower = jnp.where(cols[:, :k] == j, column, lower)
        lead = both[j : j + 1, :] * scale
        below = jnp.where(row > j, column, 0.0)
        both = jnp.where(rows == j, lead, both - below * lead)
    return lower, both[:, k:]


def gram_of(moments, coefficients):
    k = moments.shape[0]
    w = coefficients.shape[1]
    parts = jnp.concatenate([-coefficients, eye(w)], axis=0)
    return dot32(parts, dot32(moments, parts, NN), TN)


def eye(k):
    return jnp.where(
        lax.broadcasted_iota(jnp.int32, (k, k), 0) == lax.broadcasted_iota(jnp.int32, (k, k), 1), 1.0, 0.0
    ).astype(F32)


def second_kernel(k, n, order, first_ref, pair_ref, mine_ref, got_ref, q_ref, prod_ref, mom_ref, base_ref, proj_ref, fact_ref):
    packed = mine_ref[:, 2 * n :] + got_ref[:, 2 * n :]
    moments = jnp.concatenate([packed[:, : 2 * k], packed[:, 2 * k : 4 * k]], axis=0) * (1.0 / order)
    projection = moments[:k, k:]
    lower, inverse = factor_of(gram_of(moments, projection))
    proj_ref[...] = projection
    fact_ref[...] = lower
    x, y = first_ref[...], pair_ref[:, : 2 * n]
    w = mine_ref[:, : 2 * n] + got_ref[:, : 2 * n]
    q = dot32(inverse, y - dot32(projection, x, TN), NN)
    prod = dot32(inverse, w - dot32(projection, y, TN), NN)
    q_ref[...] = q
    prod_ref[...] = prod
    s = jnp.concatenate([q, x, prod], axis=0)
    total = dot32(s, s, NT)
    mom_ref[...] = total
    base_ref[...] = jnp.where(place()[0] == 0, total, jnp.zeros_like(total))


def last_kernel(k, n, order, first_ref, q_ref, prod_ref, proj0_ref, fact0_ref, mine_ref, got_ref, basis_ref, proj_ref, fact_ref):
    moments = (mine_ref[...] + got_ref[...]) * (1.0 / order)
    coefficients = moments[: 2 * k, 2 * k :]
    lower, inverse = factor_of(gram_of(moments, coefficients))
    proj_ref[0] = proj0_ref[...]
    proj_ref[1] = coefficients[:k]
    fact_ref[0] = fact0_ref[...]
    fact_ref[1] = lower
    even = place()[0] == 0
    rest = (
        own_half(prod_ref, even, n)
        - dot32(coefficients[:k], own_half(q_ref, even, n), TN)
        - dot32(coefficients[k:], own_half(first_ref, even, n), TN)
    )
    basis_ref[...] = dot32(inverse, rest, NN)


def call(kernel, out_shape, n_in, scratch=(), limit=1 << 20, name=None, far=0, flops=0):
    many = isinstance(out_shape, (tuple, list))
    run = pl.pallas_call(
        kernel,
        out_shape=out_shape,
        in_specs=[pl.BlockSpec(memory_space=pl.ANY) if i < far else VMEM_SPEC for i in range(n_in)],
        out_specs=tuple([VMEM_SPEC] * len(out_shape)) if many else VMEM_SPEC,
        scratch_shapes=list(scratch),
        compiler_params=pltpu.CompilerParams(vmem_limit_bytes=limit),
        cost_estimate=pl.CostEstimate(flops=flops, transcendentals=0, bytes_accessed=flops // 128) if flops else None,
        name=name,
    )
    return lambda *args: run(
        *[v if i < far else pltpu.with_memory_space_constraint(v, pltpu.VMEM) for i, v in enumerate(args)]
    )


def shape(*dims):
    return jax.ShapeDtypeStruct(dims, F32)


def on_device(n_row, n_col, coupling, energies, block):
    n, k = block.shape
    group = n_row
    order = n * n_row * n_col
    rows = coupling.shape[0] * n
    width = coupling.shape[2]
    axes = ("row", "col")
    flat = [(r, c) for r in range(n_row) for c in range(n_col)]

    def send(value, to):
        pairs = [(r * n_col + c, to(r, c)) for r, c in flat]
        return lax.ppermute(value, axes, [p for p in pairs if p[1] is not None])

    def swap(value):
        return send(value, lambda r, c: r * n_col + (c ^ 1))

    def chip(r, c, s_row, s_z):
        return (r ^ s_row) * n_col + (c ^ (2 * s_z))

    def spread(s):
        def to(r, c):
            along_z = (c % 2 == 0) != (s == group - 1)
            return chip(r, c, 0, s) if along_z else chip(r, c, s, 0)

        return to

    steps = range(1, group)
    tile, parts = 256, 3
    total_pieces = group * parts
    block_shape = shape(rows // parts, 2 * n)
    most = max(len(pieces_of(p, group, n, rows // parts)) for p in range(parts))
    semaphores = lambda count: [pltpu.SemaphoreType.DMA((count, most))]
    work = rows * 2 * n * 256
    a = coupling.reshape(rows, width)
    energy = energies.reshape(1, n)

    other = swap(block.T)
    own, *held = call(
        functools.partial(begin_kernel, k, n, group, parts),
        (shape(k, n), block_shape),
        2,
        scratch=semaphores(1) + [pltpu.SemaphoreType.DMA],
        name="begin",
        far=2,
        flops=work // 4,
    )(a, block.T)
    first = call(functools.partial(order_kernel, k, n), shape(k, 2 * n), 2, name="order")(own, other)

    def products(held, pair, name):
        extra = pair.shape[1] > 2 * n
        sizes = (k, n, group, tile, parts)
        load = len(held) < total_pieces
        mine = [send(pair, spread(s)) for s in steps]
        near = held[:parts]
        new = parts + 1 - len(near) if load else 0
        u0, *fresh = call(
            functools.partial(early_kernel, *sizes, len(near), new),
            (shape(k, rows),) + (block_shape,) * new,
            load + len(near) + 1,
            scratch=[pltpu.VMEM((2 * k, 2 * n), BF16)] + (semaphores(new) if new else []),
            limit=8 << 20,
            name=name + "_early",
            far=int(load),
            flops=2 * work,
        )(*([a] if load else []), *near, pair)
        held = held + fresh
        u0, *mine = lax.optimization_barrier((u0, *mine))
        theirs = [swap(y) for y in mine]
        new = total_pieces - len(held)
        out, keep, mine_u, xr, *fresh = call(
            functools.partial(main_kernel, *sizes, len(held) - parts, new),
            (shape(group - 1, k, 2 * n), shape(group - 1, k, 2 * n), shape(k, n), jax.ShapeDtypeStruct((2 * k, rows), BF16))
            + (block_shape,) * new,
            load + len(held) - parts + 2 * group,
            scratch=[
                pltpu.VMEM((2 * k, (group - 1) * 2 * n), BF16),
                pltpu.VMEM((k, rows), F32),
                pltpu.VMEM((k, (group - 1) * 2 * n), F32),
            ]
            + (semaphores(new) if new else []),
            limit=8 << 20,
            name=name,
            far=int(load),
            flops=4 * work * (group - 1),
        )(*([a] if load else []), *held[parts:], pair, u0, *mine, *theirs)
        held = held + fresh
        got = swap(out)
        sums = call(
            functools.partial(combine_kernel, k, n, group, extra),
            (shape(k, pair.shape[1]),) * (group - 1) + ((shape(k, 8 * k),) if extra else ()),
            2 + (2 * group - 1 if extra else 0),
            name=name + "_combine",
        )(keep, got, *((pair, *mine, *theirs) if extra else ()))
        arrived = [send(sums[s - 1], spread(s)) for s in steps]
        total = call(
            functools.partial(late_kernel, *sizes, extra),
            shape(k, pair.shape[1]),
            parts + 4 + extra,
            scratch=[pltpu.VMEM((k, 2 * n), F32)],
            limit=8 << 20,
            name=name + "_late",
            flops=2 * work,
        )(*held[:parts], xr, mine_u, pair, energy, *sums[group - 1 :])
        for v in arrived:
            total = total + v
        return total, swap(total), held

    mine, got, held = products(held, first, "first")
    pair = call(functools.partial(pair_kernel, k, n), shape(k, 2 * n + 8 * k), 3, name="pair")(first, mine, got)
    mine, got, held = products(held, pair, "second")
    q, prod, moments, total, proj0, fact0 = call(
        functools.partial(second_kernel, k, n, order),
        (shape(k, 2 * n), shape(k, 2 * n), shape(3 * k, 3 * k), shape(3 * k, 3 * k), shape(k, k), shape(k, k)),
        4,
        name="middle",
    )(first, pair, mine, got)
    half = group * group // 2
    for i in range(1, half + 1):

        def to(r, c, i=i):
            s = half - 1 + i if c % 2 else i
            return None if c % 2 == 0 and i == half else chip(r, c, s // group, s % group)

        total = total + send(moments, to)
    basis, proj, fact = call(
        functools.partial(last_kernel, k, n, order),
        (shape(k, n), shape(2, k, k), shape(2, k, k)),
        7,
        name="last",
    )(first, q, prod, proj0, fact0, total, swap(total))
    return basis.T, proj, fact


def solution(mesh):
    n_row, n_col = mesh.shape["row"], mesh.shape["col"]

    def body(coupling, energies, block):
        n, k = block.shape
        paired = n_col == 2 * n_row and n_row & (n_row - 1) == 0 and n_row > 1
        divides = coupling.shape[0] * n % 768 == 0
        whole = divides and n % 64 == 0 and 8 * k == 128 and coupling.shape[2] == coupling.shape[0] * n * 2
        small = coupling.size * 4 <= 44 << 20
        if paired and whole and small:
            return on_device(n_row, n_col, coupling, energies, block)
        return generic(coupling, energies, block)

    placed = (P(None, "col", "row"), P(("row", "col")), P(("row", "col"), None))
    return jax.shard_map(
        body,
        mesh=mesh,
        in_specs=placed,
        out_specs=(P(("row", "col"), None), P(), P()),
        check_vma=False,
    )
```

```python
import functools

import jax
import jax.numpy as jnp
from jax import lax
from jax.experimental import pallas as pl
from jax.experimental.pallas import tpu as pltpu
from jax.sharding import PartitionSpec as P

ITERS = 2
F32 = jnp.float32
BF16 = jnp.bfloat16

precise = lax.Precision.HIGHEST

NN = (((1,), (0,)), ((), ()))
NT = (((1,), (1,)), ((), ()))
TN = (((0,), (0,)), ((), ()))

VMEM_SPEC = pl.BlockSpec(memory_space=pltpu.VMEM)


def generic(coupling, energies, block):
    order = block.shape[0] * lax.axis_size("row") * lax.axis_size("col")
    segment = block.shape[0]
    width = block.shape[1]
    column = lax.axis_index("col")
    current, energy_rows = (
        lax.all_gather(block, "col", axis=0, tiled=True),
        lax.all_gather(energies, "col", axis=0, tiled=True),
    )
    prior = jnp.zeros_like(current)
    projection_list = []
    factor_list = []
    for section in range(ITERS):
        own_rows = lax.dynamic_slice_in_dim(current, column * segment, segment, 0)
        spread = lax.all_gather(own_rows, "row", axis=0, tiled=True)
        spread = spread.reshape(coupling.shape[0], segment, width)
        direct = lax.psum_scatter(
            jnp.einsum("aig,gk->aik", coupling, current, precision=precise),
            "row",
            scatter_dimension=0,
            tiled=True,
        ).reshape(segment, width)
        partial_value = jnp.einsum("aig,aik->gk", coupling, spread, precision=precise)
        transposed = lax.psum(partial_value, "col")
        direct_rows = lax.all_gather(direct, "col", axis=0, tiled=True)
        product = energy_rows[:, None] * current + direct_rows + transposed
        stacked = jnp.concatenate([current, prior, product], axis=1)
        moments = lax.psum(jnp.einsum("nk,nl->kl", stacked, stacked, precision=precise), "row") / order
        projection = moments[:width, 2 * width :]
        cross = moments[width : 2 * width, 2 * width :]
        weights = jnp.concatenate([-projection, -cross, jnp.eye(width, dtype=F32)], axis=0)
        gram_matrix = jnp.dot(weights.T, jnp.dot(moments, weights, precision=precise), precision=precise)
        factor = jnp.linalg.cholesky(gram_matrix)
        residual = (
            product
            - jnp.dot(current, projection, precision=precise)
            - jnp.dot(prior, cross, precision=precise)
        )
        prior = current
        current = jax.scipy.linalg.solve_triangular(factor, residual.T, lower=True).T
        projection_list.append(projection)
        factor_list.append(factor)
    basis = lax.dynamic_slice_in_dim(current, column * segment, segment, 0)
    return (basis, jnp.stack(projection_list), jnp.stack(factor_list))


def place():
    column = lax.axis_index("col")
    return lax.rem(column, 2), lax.div(column, 2), lax.axis_index("row")


def split(value):
    high = value.astype(BF16)
    return high, (value - high.astype(F32)).astype(BF16)


def dot(left, right, dims):
    return lax.dot_general(left, right, dims, preferred_element_type=F32)


def dot32(left, right, dims):
    return lax.dot_general(left, right, dims, preferred_element_type=F32, precision=precise)


def own_half(value, even, n):
    return jnp.where(even, value[:, :n], value[:, n : 2 * n])


def in_half(value, even):
    zero = jnp.zeros_like(value)
    return jnp.concatenate([jnp.where(even, value, zero), jnp.where(even, zero, value)], axis=1)


def pieces_of(part, group, n, rows):
    found, at, end = [], part * rows, (part + 1) * rows
    while at < end:
        s, off = divmod(at, n)
        count = min(n - off, end - at)
        found.append((s, off, at - part * rows, count))
        at += count
    return found


class Loader:
    def __init__(self, source, arrived, n, group, parts, first, held):
        _, z, r = place()
        self.held, self.first = held, first

        def copies(i):
            cols = pl.ds(pl.multiple_of(lax.bitwise_xor(z, (first + i) // parts) * (2 * n), 128), 2 * n)
            return [
                pltpu.make_async_copy(
                    source.at[pl.ds(pl.multiple_of(lax.bitwise_xor(r, peer) * n + off, 8), count), cols],
                    held[i].at[pl.ds(at, count), :],
                    arrived.at[i, j],
                )
                for j, (peer, off, at, count) in enumerate(
                    pieces_of((first + i) % parts, group, n, group * n // parts)
                )
            ]

        self.copies = copies
        for i in range(len(held)):
            for copy in copies(i):
                copy.start()

    def wait(self, i):
        for copy in self.copies(i):
            copy.wait()


def begin_kernel(k, n, group, parts, source, block_ref, own_ref, *refs):
    *held, arrived, ready = refs
    copy = pltpu.make_async_copy(block_ref, own_ref, ready)
    copy.start()
    loader = Loader(source, arrived, n, group, parts, 0, held)
    copy.wait()
    for i in range(len(held)):
        loader.wait(i)


def order_kernel(k, n, own_ref, other_ref, out_ref):
    even = place()[0] == 0
    own, other = own_ref[...], other_ref[...]
    out_ref[...] = jnp.concatenate([jnp.where(even, own, other), jnp.where(even, other, own)], axis=1)


def put(slab, at, k, value):
    high, low = split(value)
    slab[:k, at : at + value.shape[1]] = high
    slab[k:, at : at + value.shape[1]] = low


def early_kernel(k, n, group, tile, parts, given, new, *refs):
    source, refs = (refs[0], refs[1:]) if new else (None, refs)
    held, refs = list(refs[:given]), refs[given:]
    pair_ref, u_ref, *refs = refs
    if new:
        *fresh, xg, arrived = refs
        loader = Loader(source, arrived, n, group, parts, given, fresh)
        held = held + fresh
    else:
        (xg,) = refs
    put(xg, 0, k, pair_ref[:, : 2 * n])
    rows = held[0].shape[0]

    def step(p, t, carry):
        high, low = split(held[p][pl.ds(pl.multiple_of(t * tile, tile), tile), :])
        one = dot(xg[...], high, NT)
        two = dot(xg[:k, :], low, NT)
        u_ref[:, pl.ds(pl.multiple_of(p * rows + t * tile, tile), tile)] = one[:k] + one[k:] + two
        return carry

    for p in range(parts):
        if p >= given:
            loader.wait(p - given)
        lax.fori_loop(0, rows // tile, functools.partial(step, p), 0)
    for p in range(parts, given + new):
        loader.wait(p - given)


def turned(s, group, even):
    return jnp.logical_not(even) if s == group - 1 else even


def main_kernel(k, n, group, tile, parts, given, new, *refs):
    even = place()[0] == 0
    source, refs = (refs[0], refs[1:]) if new else (None, refs)
    held, refs = list(refs[:given]), refs[given:]
    pair_ref, u0_ref, mine, theirs = refs[0], refs[1], refs[2 : group + 1], refs[group + 1 : 2 * group]
    send_ref, keep_ref, own_ref, xr, *refs = refs[2 * group :]
    if new:
        *fresh, xg, u_acc, v_acc, arrived = refs
        loader = Loader(source, arrived, n, group, parts, parts + given, fresh)
        held = held + fresh
    else:
        xg, u_acc, v_acc = refs
    rows = held[0].shape[0]

    segments = [own_half(pair_ref, even, n)]
    for s in range(1, group):
        y, w = mine[s - 1][:, : 2 * n], theirs[s - 1][:, : 2 * n]
        along = turned(s, group, even)
        put(xg, (s - 1) * 2 * n, k, jnp.where(along, y, w))
        segments.append(own_half(jnp.where(along, w, y), even, n))
    for a in range(0, group, 2):
        put(xr, a * n, k, jnp.concatenate(segments[a : a + 2], axis=1))
    u_acc[...] = u0_ref[...]
    v_acc[...] = jnp.zeros_like(v_acc)

    def step(i, t, carry):
        s, p = divmod(i, parts)
        cols = slice(s * 2 * n, (s + 1) * 2 * n)
        at = pl.ds(pl.multiple_of(p * rows + t * tile, tile), tile)
        high, low = split(held[i][pl.ds(pl.multiple_of(t * tile, tile), tile), :])
        one = dot(xr[:, at], high, NN)
        two = dot(xr[:k, at], low, NN)
        v_acc[:, cols] += one[:k] + one[k:] + two
        one = dot(xg[:, cols], high, NT)
        two = dot(xg[:k, cols], low, NT)
        u_acc[:, at] += one[:k] + one[k:] + two
        return carry

    for i in range(len(held)):
        if i >= given:
            loader.wait(i - given)
        lax.fori_loop(0, rows // tile, functools.partial(step, i), 0)

    own_ref[...] = u_acc[:, :n]
    for s in range(1, group):
        along = turned(s, group, even)
        by_z = v_acc[:, 2 * n * (s - 1) : 2 * n * s]
        by_row = in_half(u_acc[:, n * s : n * (s + 1)], even)
        keep_ref[s - 1] = jnp.where(along, by_z, by_row)
        send_ref[s - 1] = jnp.where(along, by_row, by_z)


def late_kernel(k, n, group, tile, parts, extra, *refs):
    held, refs = refs[:parts], refs[parts:]
    xr, own_ref, pair_ref, energy_ref, *refs = refs
    more, refs = (refs[0], refs[1:]) if extra else (None, refs)
    out_ref, v_acc = refs
    even = place()[0] == 0
    rows = held[0].shape[0]
    v_acc[...] = jnp.zeros_like(v_acc)

    def step(p, t, carry):
        at = pl.ds(pl.multiple_of(p * rows + t * tile, tile), tile)
        high, low = split(held[p][pl.ds(pl.multiple_of(t * tile, tile), tile), :])
        one = dot(xr[:, at], high, NN)
        two = dot(xr[:k, at], low, NN)
        v_acc[...] += one[:k] + one[k:] + two
        return carry

    for p in range(parts):
        lax.fori_loop(0, rows // tile, functools.partial(step, p), 0)
    own = energy_ref[...] * own_half(pair_ref, even, n) + own_ref[...]
    out_ref[:, : 2 * n] = v_acc[...] + in_half(own, even)
    if extra:
        part = more[...]
        out_ref[:, 2 * n :] = jnp.where(even, part, jnp.zeros_like(part))


def combine_kernel(k, n, group, extra, keep_ref, got_ref, *refs):
    even = place()[0] == 0
    if extra:
        pair_ref, mine, theirs, outs = refs[0], refs[1:group], refs[group : 2 * group - 1], refs[2 * group - 1 :]
        part = pair_ref[:, 2 * n :]
        for s in range(1, group):
            along = turned(s, group, even)
            part = part + jnp.where(along, theirs[s - 1][:, 2 * n :], mine[s - 1][:, 2 * n :])
        outs[group - 1][...] = part
    else:
        outs = refs
    for s in range(1, group):
        outs[s - 1][:, : 2 * n] = keep_ref[s - 1] + got_ref[s - 1]
        if extra:
            outs[s - 1][:, 2 * n :] = jnp.where(turned(s, group, even), part, jnp.zeros_like(part))


def pair_kernel(k, n, first_ref, mine_ref, got_ref, out_ref):
    value = mine_ref[...] + got_ref[...]
    s = jnp.concatenate([first_ref[...], value], axis=0)
    moments = dot32(s, s, NT)
    out_ref[:, : 2 * n] = value
    out_ref[:, 2 * n :] = jnp.zeros((k, 8 * k), F32)
    out_ref[:, 2 * n : 2 * n + 2 * k] = moments[:k]
    out_ref[:, 2 * n + 2 * k : 2 * n + 4 * k] = moments[k:]


def factor_of(gram):
    k = gram.shape[0]
    rows = lax.broadcasted_iota(jnp.int32, (k, 2 * k), 0)
    cols = lax.broadcasted_iota(jnp.int32, (k, 2 * k), 1)
    row = lax.broadcasted_iota(jnp.int32, (k, 1), 0)
    both = jnp.concatenate([gram, jnp.where(rows == cols, 1.0, 0.0)[:, :k]], axis=1)
    lower = jnp.zeros((k, k), F32)
    for j in range(k):
        scale = 1.0 / jnp.sqrt(both[j : j + 1, j : j + 1])
        column = jnp.where(row >= j, both[:, j : j + 1] * scale, 0.0)
        lower = jnp.where(cols[:, :k] == j, column, lower)
        lead = both[j : j + 1, :] * scale
        below = jnp.where(row > j, column, 0.0)
        both = jnp.where(rows == j, lead, both - below * lead)
    return lower, both[:, k:]


def gram_of(moments, coefficients):
    k = moments.shape[0]
    w = coefficients.shape[1]
    parts = jnp.concatenate([-coefficients, eye(w)], axis=0)
    return dot32(parts, dot32(moments, parts, NN), TN)


def eye(k):
    return jnp.where(
        lax.broadcasted_iota(jnp.int32, (k, k), 0) == lax.broadcasted_iota(jnp.int32, (k, k), 1), 1.0, 0.0
    ).astype(F32)


def second_kernel(k, n, order, first_ref, pair_ref, mine_ref, got_ref, q_ref, prod_ref, mom_ref, base_ref, proj_ref, fact_ref):
    packed = mine_ref[:, 2 * n :] + got_ref[:, 2 * n :]
    moments = jnp.concatenate([packed[:, : 2 * k], packed[:, 2 * k : 4 * k]], axis=0) * (1.0 / order)
    projection = moments[:k, k:]
    lower, inverse = factor_of(gram_of(moments, projection))
    proj_ref[...] = projection
    fact_ref[...] = lower
    x, y = first_ref[...], pair_ref[:, : 2 * n]
    w = mine_ref[:, : 2 * n] + got_ref[:, : 2 * n]
    q = dot32(inverse, y - dot32(projection, x, TN), NN)
    prod = dot32(inverse, w - dot32(projection, y, TN), NN)
    q_ref[...] = q
    prod_ref[...] = prod
    s = jnp.concatenate([q, x, prod], axis=0)
    total = dot32(s, s, NT)
    mom_ref[...] = total
    base_ref[...] = jnp.where(place()[0] == 0, total, jnp.zeros_like(total))


def last_kernel(k, n, order, first_ref, q_ref, prod_ref, proj0_ref, fact0_ref, mine_ref, got_ref, basis_ref, proj_ref, fact_ref):
    moments = (mine_ref[...] + got_ref[...]) * (1.0 / order)
    coefficients = moments[: 2 * k, 2 * k :]
    lower, inverse = factor_of(gram_of(moments, coefficients))
    proj_ref[0] = proj0_ref[...]
    proj_ref[1] = coefficients[:k]
    fact_ref[0] = fact0_ref[...]
    fact_ref[1] = lower
    even = place()[0] == 0
    rest = (
        own_half(prod_ref, even, n)
        - dot32(coefficients[:k], own_half(q_ref, even, n), TN)
        - dot32(coefficients[k:], own_half(first_ref, even, n), TN)
    )
    basis_ref[...] = dot32(inverse, rest, NN)


def call(kernel, out_shape, n_in, scratch=(), limit=1 << 20, name=None, far=0, flops=0):
    many = isinstance(out_shape, (tuple, list))
    run = pl.pallas_call(
        kernel,
        out_shape=out_shape,
        in_specs=[pl.BlockSpec(memory_space=pl.ANY) if i < far else VMEM_SPEC for i in range(n_in)],
        out_specs=tuple([VMEM_SPEC] * len(out_shape)) if many else VMEM_SPEC,
        scratch_shapes=list(scratch),
        compiler_params=pltpu.CompilerParams(vmem_limit_bytes=limit),
        cost_estimate=pl.CostEstimate(flops=flops, transcendentals=0, bytes_accessed=flops // 128) if flops else None,
        name=name,
    )
    return lambda *args: run(
        *[pltpu.with_memory_space_constraint(v, pltpu.HBM if i < far else pltpu.VMEM) for i, v in enumerate(args)]
    )


def shape(*dims):
    return jax.ShapeDtypeStruct(dims, F32)


def on_device(n_row, n_col, coupling, energies, block):
    n, k = block.shape
    group = n_row
    order = n * n_row * n_col
    rows = coupling.shape[0] * n
    width = coupling.shape[2]
    axes = ("row", "col")
    flat = [(r, c) for r in range(n_row) for c in range(n_col)]

    def send(value, to):
        pairs = [(r * n_col + c, to(r, c)) for r, c in flat]
        return lax.ppermute(value, axes, [p for p in pairs if p[1] is not None])

    def swap(value):
        return send(value, lambda r, c: r * n_col + (c ^ 1))

    def chip(r, c, s_row, s_z):
        return (r ^ s_row) * n_col + (c ^ (2 * s_z))

    def spread(s):
        def to(r, c):
            along_z = (c % 2 == 0) != (s == group - 1)
            return chip(r, c, 0, s) if along_z else chip(r, c, s, 0)

        return to

    steps = range(1, group)
    tile, parts = 256, 3
    total_pieces = group * parts
    block_shape = shape(rows // parts, 2 * n)
    most = max(len(pieces_of(p, group, n, rows // parts)) for p in range(parts))
    semaphores = lambda count: [pltpu.SemaphoreType.DMA((count, most))]
    work = rows * 2 * n * 256
    a = coupling.reshape(rows, width)
    energy = energies.reshape(1, n)

    other = swap(block.T)
    own, *held = call(
        functools.partial(begin_kernel, k, n, group, parts),
        (shape(k, n), block_shape),
        2,
        scratch=semaphores(1) + [pltpu.SemaphoreType.DMA],
        name="begin",
        far=2,
        flops=work // 4,
    )(a, block.T)
    first = call(functools.partial(order_kernel, k, n), shape(k, 2 * n), 2, name="order")(own, other)

    def products(held, pair, name):
        extra = pair.shape[1] > 2 * n
        sizes = (k, n, group, tile, parts)
        load = len(held) < total_pieces
        mine = [send(pair, spread(s)) for s in steps]
        near = held[:parts]
        new = parts + 1 - len(near) if load else 0
        u0, *fresh = call(
            functools.partial(early_kernel, *sizes, len(near), new),
            (shape(k, rows),) + (block_shape,) * new,
            load + len(near) + 1,
            scratch=[pltpu.VMEM((2 * k, 2 * n), BF16)] + (semaphores(new) if new else []),
            limit=8 << 20,
            name=name + "_early",
            far=int(load),
            flops=2 * work,
        )(*([a] if load else []), *near, pair)
        held = held + fresh
        u0, *mine = lax.optimization_barrier((u0, *mine))
        theirs = [swap(y) for y in mine]
        new = total_pieces - len(held)
        out, keep, mine_u, xr, *fresh = call(
            functools.partial(main_kernel, *sizes, len(held) - parts, new),
            (shape(group - 1, k, 2 * n), shape(group - 1, k, 2 * n), shape(k, n), jax.ShapeDtypeStruct((2 * k, rows), BF16))
            + (block_shape,) * new,
            load + len(held) - parts + 2 * group,
            scratch=[
                pltpu.VMEM((2 * k, (group - 1) * 2 * n), BF16),
                pltpu.VMEM((k, rows), F32),
                pltpu.VMEM((k, (group - 1) * 2 * n), F32),
            ]
            + (semaphores(new) if new else []),
            limit=8 << 20,
            name=name,
            far=int(load),
            flops=4 * work * (group - 1),
        )(*([a] if load else []), *held[parts:], pair, u0, *mine, *theirs)
        held = held + fresh
        got = swap(out)
        sums = call(
            functools.partial(combine_kernel, k, n, group, extra),
            (shape(k, pair.shape[1]),) * (group - 1) + ((shape(k, 8 * k),) if extra else ()),
            2 + (2 * group - 1 if extra else 0),
            name=name + "_combine",
        )(keep, got, *((pair, *mine, *theirs) if extra else ()))
        arrived = [send(sums[s - 1], spread(s)) for s in steps]
        total = call(
            functools.partial(late_kernel, *sizes, extra),
            shape(k, pair.shape[1]),
            parts + 4 + extra,
            scratch=[pltpu.VMEM((k, 2 * n), F32)],
            limit=8 << 20,
            name=name + "_late",
            flops=2 * work,
        )(*held[:parts], xr, mine_u, pair, energy, *sums[group - 1 :])
        for v in arrived:
            total = total + v
        return total, swap(total), held

    mine, got, held = products(held, first, "first")
    pair = call(functools.partial(pair_kernel, k, n), shape(k, 2 * n + 8 * k), 3, name="pair")(first, mine, got)
    mine, got, held = products(held, pair, "second")
    q, prod, moments, total, proj0, fact0 = call(
        functools.partial(second_kernel, k, n, order),
        (shape(k, 2 * n), shape(k, 2 * n), shape(3 * k, 3 * k), shape(3 * k, 3 * k), shape(k, k), shape(k, k)),
        4,
        name="middle",
    )(first, pair, mine, got)
    half = group * group // 2
    for i in range(1, half + 1):

        def to(r, c, i=i):
            s = half - 1 + i if c % 2 else i
            return None if c % 2 == 0 and i == half else chip(r, c, s // group, s % group)

        total = total + send(moments, to)
    basis, proj, fact = call(
        functools.partial(last_kernel, k, n, order),
        (shape(k, n), shape(2, k, k), shape(2, k, k)),
        7,
        name="last",
    )(first, q, prod, proj0, fact0, total, swap(total))
    return basis.T, proj, fact


def solution(mesh):
    n_row, n_col = mesh.shape["row"], mesh.shape["col"]

    def body(coupling, energies, block):
        n, k = block.shape
        paired = n_col == 2 * n_row and n_row & (n_row - 1) == 0 and n_row > 1
        divides = coupling.shape[0] * n % 768 == 0
        whole = divides and n % 64 == 0 and 8 * k == 128 and coupling.shape[2] == coupling.shape[0] * n * 2
        small = coupling.size * 4 <= 44 << 20
        if paired and whole and small:
            return on_device(n_row, n_col, coupling, energies, block)
        return generic(coupling, energies, block)

    placed = (P(None, "col", "row"), P(("row", "col")), P(("row", "col"), None))
    return jax.shard_map(
        body,
        mesh=mesh,
        in_specs=placed,
        out_specs=(P(("row", "col"), None), P(), P()),
        check_vma=False,
    )
```

```python
import functools

import jax
import jax.numpy as jnp
from jax import lax
from jax.experimental import pallas as pl
from jax.experimental.pallas import tpu as pltpu
from jax.sharding import PartitionSpec as P

ITERS = 2
F32 = jnp.float32
BF16 = jnp.bfloat16

precise = lax.Precision.HIGHEST

NN = (((1,), (0,)), ((), ()))
NT = (((1,), (1,)), ((), ()))
TN = (((0,), (0,)), ((), ()))

VMEM_SPEC = pl.BlockSpec(memory_space=pltpu.VMEM)


def generic(coupling, energies, block):
    order = block.shape[0] * lax.axis_size("row") * lax.axis_size("col")
    segment = block.shape[0]
    width = block.shape[1]
    column = lax.axis_index("col")
    current, energy_rows = (
        lax.all_gather(block, "col", axis=0, tiled=True),
        lax.all_gather(energies, "col", axis=0, tiled=True),
    )
    prior = jnp.zeros_like(current)
    projection_list = []
    factor_list = []
    for section in range(ITERS):
        own_rows = lax.dynamic_slice_in_dim(current, column * segment, segment, 0)
        spread = lax.all_gather(own_rows, "row", axis=0, tiled=True)
        spread = spread.reshape(coupling.shape[0], segment, width)
        direct = lax.psum_scatter(
            jnp.einsum("aig,gk->aik", coupling, current, precision=precise),
            "row",
            scatter_dimension=0,
            tiled=True,
        ).reshape(segment, width)
        partial_value = jnp.einsum("aig,aik->gk", coupling, spread, precision=precise)
        transposed = lax.psum(partial_value, "col")
        direct_rows = lax.all_gather(direct, "col", axis=0, tiled=True)
        product = energy_rows[:, None] * current + direct_rows + transposed
        stacked = jnp.concatenate([current, prior, product], axis=1)
        moments = lax.psum(jnp.einsum("nk,nl->kl", stacked, stacked, precision=precise), "row") / order
        projection = moments[:width, 2 * width :]
        cross = moments[width : 2 * width, 2 * width :]
        weights = jnp.concatenate([-projection, -cross, jnp.eye(width, dtype=F32)], axis=0)
        gram_matrix = jnp.dot(weights.T, jnp.dot(moments, weights, precision=precise), precision=precise)
        factor = jnp.linalg.cholesky(gram_matrix)
        residual = (
            product
            - jnp.dot(current, projection, precision=precise)
            - jnp.dot(prior, cross, precision=precise)
        )
        prior = current
        current = jax.scipy.linalg.solve_triangular(factor, residual.T, lower=True).T
        projection_list.append(projection)
        factor_list.append(factor)
    basis = lax.dynamic_slice_in_dim(current, column * segment, segment, 0)
    return (basis, jnp.stack(projection_list), jnp.stack(factor_list))


def place():
    column = lax.axis_index("col")
    return lax.rem(column, 2), lax.div(column, 2), lax.axis_index("row")


def split(value):
    high = value.astype(BF16)
    return high, (value - high.astype(F32)).astype(BF16)


def dot(left, right, dims):
    return lax.dot_general(left, right, dims, preferred_element_type=F32)


def dot32(left, right, dims):
    return lax.dot_general(left, right, dims, preferred_element_type=F32, precision=precise)


def own_half(value, even, n):
    return jnp.where(even, value[:, :n], value[:, n : 2 * n])


def in_half(value, even):
    zero = jnp.zeros_like(value)
    return jnp.concatenate([jnp.where(even, value, zero), jnp.where(even, zero, value)], axis=1)


def pieces_of(part, group, n, rows):
    found, at, end = [], part * rows, (part + 1) * rows
    while at < end:
        s, off = divmod(at, n)
        count = min(n - off, end - at)
        found.append((s, off, at - part * rows, count))
        at += count
    return found


def order_of(group, parts):
    near = [(0, p) for p in range(parts)]
    lead = [(s, 0) for s in range(1, group)]
    return near + lead + [(s, p) for s in range(1, group) for p in range(1, parts)]


class Loader:
    def __init__(self, source, arrived, n, group, parts, where, held):
        _, z, r = place()

        def copies(i):
            s, part = where[i]
            cols = pl.ds(pl.multiple_of(lax.bitwise_xor(z, s) * (2 * n), 128), 2 * n)
            return [
                pltpu.make_async_copy(
                    source.at[pl.ds(pl.multiple_of(lax.bitwise_xor(r, peer) * n + off, 8), count), cols],
                    held[i].at[pl.ds(at, count), :],
                    arrived.at[i, j],
                )
                for j, (peer, off, at, count) in enumerate(pieces_of(part, group, n, group * n // parts))
            ]

        self.copies = copies
        for i in range(len(held)):
            for copy in copies(i):
                copy.start()

    def wait(self, i):
        for copy in self.copies(i):
            copy.wait()


class Pieces:
    def __init__(self, n, group, parts, given, new, scratch, refs):
        order = order_of(group, parts)
        refs = list(refs)
        source = refs.pop(0) if len(new) else None
        held = {order[i]: refs.pop(0) for i in given}
        self.waits = {}
        if len(new):
            arrived = refs.pop()
            at = len(refs) - scratch - len(new)
            fresh, refs = refs[at : at + len(new)], refs[:at] + refs[at + len(new) :]
            where = [order[i] for i in new]
            self.loader = Loader(source, arrived, n, group, parts, where, fresh)
            self.waits = {key: i for i, key in enumerate(where)}
            held.update(zip(where, fresh))
        self.held, self.refs = held, refs

    def get(self, s, p):
        if (s, p) in self.waits:
            self.loader.wait(self.waits.pop((s, p)))
        return self.held[s, p]

    def finish(self):
        for key in list(self.waits):
            self.get(*key)


def tiles_of(piece, tile, first, last, step):
    def body(t, carry):
        high, low = split(piece[pl.ds(pl.multiple_of(t * tile, tile), tile), :])
        step(t, high, low)
        return carry

    lax.fori_loop(first, last, body, 0)


def across(xg, cols, k, high, low):
    one = dot(xg[:, cols], high, NT)
    two = dot(xg[:k, cols], low, NT)
    return one[:k] + one[k:] + two


def along(xr, at, k, high, low):
    one = dot(xr[:, at], high, NN)
    two = dot(xr[:k, at], low, NN)
    return one[:k] + one[k:] + two


def begin_kernel(k, n, group, parts, source, block_ref, own_ref, *refs):
    *held, arrived, ready = refs
    copy = pltpu.make_async_copy(block_ref, own_ref, ready)
    copy.start()
    loader = Loader(source, arrived, n, group, parts, order_of(group, parts), held)
    copy.wait()
    for i in range(len(held)):
        loader.wait(i)


def order_kernel(k, n, own_ref, other_ref, out_ref):
    even = place()[0] == 0
    own, other = own_ref[...], other_ref[...]
    out_ref[...] = jnp.concatenate([jnp.where(even, own, other), jnp.where(even, other, own)], axis=1)


def put(slab, at, k, value):
    high, low = split(value)
    slab[:k, at : at + value.shape[1]] = high
    slab[k:, at : at + value.shape[1]] = low


def turned(s, group, even):
    return jnp.logical_not(even) if s == group - 1 else even


def early_kernel(k, n, group, tile, parts, given, new, *refs):
    pieces = Pieces(n, group, parts, given, new, 1, refs)
    xg = pieces.refs.pop(-1)
    pair_ref, u_ref = pieces.refs
    put(xg, 0, k, pair_ref[:, : 2 * n])
    for p in range(parts):
        piece = pieces.get(0, p)
        rows = piece.shape[0]

        def step(t, high, low):
            u_ref[:, pl.ds(pl.multiple_of(p * rows + t * tile, tile), tile)] = across(xg, slice(None), k, high, low)

        tiles_of(piece, tile, 0, rows // tile, step)
    pieces.finish()


def own_kernel(k, n, group, tile, parts, given, new, *refs):
    pieces = Pieces(n, group, parts, given, new, 1, refs)
    xr = pieces.refs.pop(-1)
    pair_ref, v_ref = pieces.refs
    even = place()[0] == 0
    put(xr, 0, k, own_half(pair_ref, even, n))
    v_ref[...] = jnp.zeros_like(v_ref)
    for s in range(1, group):
        cols = slice((s - 1) * 2 * n, s * 2 * n)

        def step(t, high, low):
            v_ref[:, cols] += along(xr, pl.ds(pl.multiple_of(t * tile, tile), tile), k, high, low)

        tiles_of(pieces.get(s, 0), tile, 0, n // tile, step)
    pieces.finish()


def main_kernel(k, n, group, tile, parts, given, new, *refs):
    pieces = Pieces(n, group, parts, given, new, 2, refs)
    u_acc, v_acc = pieces.refs[-2:]
    refs = pieces.refs[:-2]
    pair_ref, u0_ref, v0_ref, mine, theirs = refs[0], refs[1], refs[2], refs[3 : group + 2], refs[group + 2 : 2 * group + 1]
    send_ref, keep_ref, own_ref, xr, xg = refs[2 * group + 1 :]
    even = place()[0] == 0

    segments = [own_half(pair_ref, even, n)]
    for s in range(1, group):
        y, w = mine[s - 1][:, : 2 * n], theirs[s - 1][:, : 2 * n]
        to_z = turned(s, group, even)
        put(xg, (s - 1) * 2 * n, k, jnp.where(to_z, y, w))
        segments.append(own_half(jnp.where(to_z, w, y), even, n))
    for a in range(0, group, 2):
        put(xr, a * n, k, jnp.concatenate(segments[a : a + 2], axis=1))
    u_acc[...] = u0_ref[...]
    v_acc[...] = v0_ref[...]

    for s, p in order_of(group, parts)[parts:]:
        piece = pieces.get(s, p)
        rows = piece.shape[0]
        cols = slice((s - 1) * 2 * n, s * 2 * n)

        def step(t, high, low):
            at = pl.ds(pl.multiple_of(p * rows + t * tile, tile), tile)
            v_acc[:, cols] += along(xr, at, k, high, low)
            u_acc[:, at] += across(xg, cols, k, high, low)

        tiles_of(piece, tile, n // tile if p == 0 else 0, rows // tile, step)

    own_ref[...] = u_acc[:, :n]
    for s in range(1, group):
        to_z = turned(s, group, even)
        by_z = v_acc[:, 2 * n * (s - 1) : 2 * n * s]
        by_row = in_half(u_acc[:, n * s : n * (s + 1)], even)
        keep_ref[s - 1] = jnp.where(to_z, by_z, by_row)
        send_ref[s - 1] = jnp.where(to_z, by_row, by_z)


def near_kernel(k, n, tile, piece, xr, v_ref):
    v_ref[...] = jnp.zeros_like(v_ref)

    def step(t, high, low):
        v_ref[...] += along(xr, pl.ds(pl.multiple_of(t * tile, tile), tile), k, high, low)

    tiles_of(piece, tile, 0, piece.shape[0] // tile, step)


def late_kernel(k, n, group, tile, parts, extra, *refs):
    near, lead, refs = refs[: parts - 1], refs[parts - 1 : parts + group - 2], refs[parts + group - 2 :]
    xr, xg, v_ref, own_ref, pair_ref, energy_ref, *refs = refs
    more, refs = (refs[0], refs[1:]) if extra else (None, refs)
    out_ref, v_acc, u_acc = refs
    even = place()[0] == 0
    v_acc[...] = v_ref[...]
    u_acc[...] = own_ref[...]
    for p in range(1, parts):
        rows = near[p - 1].shape[0]

        def step(t, high, low):
            v_acc[...] += along(xr, pl.ds(pl.multiple_of(p * rows + t * tile, tile), tile), k, high, low)

        tiles_of(near[p - 1], tile, 0, rows // tile, step)
    for s in range(1, group):
        cols = slice((s - 1) * 2 * n, s * 2 * n)

        def step(t, high, low):
            u_acc[:, pl.ds(pl.multiple_of(t * tile, tile), tile)] += across(xg, cols, k, high, low)

        tiles_of(lead[s - 1], tile, 0, n // tile, step)
    own = energy_ref[...] * own_half(pair_ref, even, n) + u_acc[...]
    out_ref[:, : 2 * n] = v_acc[...] + in_half(own, even)
    if extra:
        part = more[...]
        out_ref[:, 2 * n :] = jnp.where(even, part, jnp.zeros_like(part))


def combine_kernel(k, n, group, extra, keep_ref, got_ref, *refs):
    even = place()[0] == 0
    if extra:
        pair_ref, mine, theirs, outs = refs[0], refs[1:group], refs[group : 2 * group - 1], refs[2 * group - 1 :]
        part = pair_ref[:, 2 * n :]
        for s in range(1, group):
            to_z = turned(s, group, even)
            part = part + jnp.where(to_z, theirs[s - 1][:, 2 * n :], mine[s - 1][:, 2 * n :])
        outs[group - 1][...] = part
    else:
        outs = refs
    for s in range(1, group):
        outs[s - 1][:, : 2 * n] = keep_ref[s - 1] + got_ref[s - 1]
        if extra:
            outs[s - 1][:, 2 * n :] = jnp.where(turned(s, group, even), part, jnp.zeros_like(part))


def pair_kernel(k, n, first_ref, mine_ref, got_ref, out_ref):
    value = mine_ref[...] + got_ref[...]
    s = jnp.concatenate([first_ref[...], value], axis=0)
    moments = dot32(s, s, NT)
    out_ref[:, : 2 * n] = value
    out_ref[:, 2 * n :] = jnp.zeros((k, 8 * k), F32)
    out_ref[:, 2 * n : 2 * n + 2 * k] = moments[:k]
    out_ref[:, 2 * n + 2 * k : 2 * n + 4 * k] = moments[k:]


def factor_of(gram):
    k = gram.shape[0]
    rows = lax.broadcasted_iota(jnp.int32, (k, 2 * k), 0)
    cols = lax.broadcasted_iota(jnp.int32, (k, 2 * k), 1)
    row = lax.broadcasted_iota(jnp.int32, (k, 1), 0)
    both = jnp.concatenate([gram, eye(k)], axis=1)
    for j in range(k - 1):
        lead = both[j : j + 1, :]
        lead = lead * (1.0 / both[j : j + 1, j : j + 1])
        both = both - jnp.where(row > j, both[:, j : j + 1], 0.0) * lead
    pivots = jnp.sum(jnp.where(rows == cols, both, 0.0), axis=1, keepdims=True)
    both = both * (1.0 / jnp.sqrt(pivots))
    upper = jnp.where(rows <= cols, both, 0.0)[:, :k]
    return dot32(upper, eye(k), TN), both[:, k:]


def gram_of(moments, coefficients):
    k = moments.shape[0]
    w = coefficients.shape[1]
    parts = jnp.concatenate([-coefficients, eye(w)], axis=0)
    return dot32(parts, dot32(moments, parts, NN), TN)


def eye(k):
    return jnp.where(
        lax.broadcasted_iota(jnp.int32, (k, k), 0) == lax.broadcasted_iota(jnp.int32, (k, k), 1), 1.0, 0.0
    ).astype(F32)


def second_kernel(k, n, order, first_ref, pair_ref, mine_ref, got_ref, q_ref, prod_ref, mom_ref, proj_ref, fact_ref):
    packed = mine_ref[:, 2 * n :] + got_ref[:, 2 * n :]
    moments = jnp.concatenate([packed[:, : 2 * k], packed[:, 2 * k : 4 * k]], axis=0) * (1.0 / order)
    projection = moments[:k, k:]
    lower, inverse = factor_of(gram_of(moments, projection))
    proj_ref[...] = projection
    fact_ref[...] = lower
    x, y = first_ref[...], pair_ref[:, : 2 * n]
    w = mine_ref[:, : 2 * n] + got_ref[:, : 2 * n]
    rest = jnp.concatenate([y, w], axis=1) - dot32(projection, jnp.concatenate([x, y], axis=1), TN)
    both = dot32(inverse, rest, NN)
    q, prod = both[:, : 2 * n], both[:, 2 * n :]
    q_ref[...] = q
    prod_ref[...] = prod
    s = jnp.concatenate([q, x, prod], axis=0)
    mom_ref[...] = dot32(s, s, NT)


def last_kernel(k, n, order, first_ref, q_ref, prod_ref, proj0_ref, fact0_ref, *refs):
    *sums, basis_ref, proj_ref, fact_ref = refs
    total = sums[0][...]
    for m in sums[1:]:
        total = total + m[...]
    moments = total * (1.0 / order)
    coefficients = moments[: 2 * k, 2 * k :]
    lower, inverse = factor_of(gram_of(moments, coefficients))
    proj_ref[0] = proj0_ref[...]
    proj_ref[1] = coefficients[:k]
    fact_ref[0] = fact0_ref[...]
    fact_ref[1] = lower
    even = place()[0] == 0
    before = jnp.concatenate([own_half(q_ref, even, n), own_half(first_ref, even, n)], axis=0)
    rest = own_half(prod_ref, even, n) - dot32(coefficients, before, TN)
    basis_ref[...] = dot32(inverse, rest, NN)


def call(kernel, out_shape, n_in, scratch=(), limit=1 << 20, name=None, far=0, flops=0):
    many = isinstance(out_shape, (tuple, list))
    run = pl.pallas_call(
        kernel,
        out_shape=out_shape,
        in_specs=[pl.BlockSpec(memory_space=pl.ANY) if i < far else VMEM_SPEC for i in range(n_in)],
        out_specs=tuple([VMEM_SPEC] * len(out_shape)) if many else VMEM_SPEC,
        scratch_shapes=list(scratch),
        compiler_params=pltpu.CompilerParams(vmem_limit_bytes=limit),
        cost_estimate=pl.CostEstimate(flops=flops, transcendentals=0, bytes_accessed=flops // 128) if flops else None,
        name=name,
    )
    return lambda *args: run(
        *[pltpu.with_memory_space_constraint(v, pltpu.HBM if i < far else pltpu.VMEM) for i, v in enumerate(args)]
    )


def shape(*dims):
    return jax.ShapeDtypeStruct(dims, F32)


def on_device(n_row, n_col, coupling, energies, block):
    n, k = block.shape
    group = n_row
    order = n * n_row * n_col
    rows = coupling.shape[0] * n
    width = coupling.shape[2]
    axes = ("row", "col")
    flat = [(r, c) for r in range(n_row) for c in range(n_col)]

    def send(value, to):
        pairs = [(r * n_col + c, to(r, c)) for r, c in flat]
        return lax.ppermute(value, axes, [p for p in pairs if p[1] is not None])

    def swap(value):
        return send(value, lambda r, c: r * n_col + (c ^ 1))

    def chip(r, c, s_row, s_z):
        return (r ^ s_row) * n_col + (c ^ (2 * s_z))

    def spread(s):
        def to(r, c):
            along_z = (c % 2 == 0) != (s == group - 1)
            return chip(r, c, 0, s) if along_z else chip(r, c, s, 0)

        return to

    steps = range(1, group)
    tile, parts = 256, 3
    total_pieces = group * parts
    block_shape = shape(rows // parts, 2 * n)
    most = max(len(pieces_of(p, group, n, rows // parts)) for p in range(parts))
    semaphores = lambda count: [pltpu.SemaphoreType.DMA((count, most))]
    work = rows * 2 * n * 256
    a = coupling.reshape(rows, width)
    energy = energies.reshape(1, n)

    other = swap(block.T)
    own, *held = call(
        functools.partial(begin_kernel, k, n, group, parts),
        (shape(k, n), block_shape),
        2,
        scratch=semaphores(1) + [pltpu.SemaphoreType.DMA],
        name="begin",
        far=2,
        flops=work // 4,
    )(a, block.T)
    first = call(functools.partial(order_kernel, k, n), shape(k, 2 * n), 2, name="order")(own, other)

    def products(held, pair, name):
        extra = pair.shape[1] > 2 * n
        sizes = (k, n, group, tile, parts)
        load = len(held) < total_pieces

        def matrix_call(kernel, need, upto, out_shapes, args, scratch, label, flops):
            given = [i for i in need if i < len(held)]
            new = range(len(held), max(upto, len(held)))
            outs = call(
                functools.partial(kernel, *sizes, given, new),
                tuple(out_shapes) + (block_shape,) * len(new),
                (len(new) > 0) + len(given) + len(args),
                scratch=list(scratch) + (semaphores(len(new)) if new else []),
                limit=8 << 20,
                name=name + label,
                far=int(len(new) > 0),
                flops=flops,
            )(*([a] if new else []), *[held[i] for i in given], *args)
            held.extend(outs[len(out_shapes) :])
            return outs[: len(out_shapes)]

        mine = [send(pair, spread(s)) for s in steps]
        (u0,) = matrix_call(
            early_kernel,
            range(parts),
            parts + 1,
            [shape(k, rows)],
            [pair],
            [pltpu.VMEM((2 * k, 2 * n), BF16)],
            "_early",
            2 * work,
        )
        u0, same, *mine = lax.optimization_barrier((u0, pair, *mine))
        theirs = [swap(y) for y in mine]
        (v0,) = matrix_call(
            own_kernel,
            range(parts, parts + group - 1),
            parts + group - 1,
            [shape(k, (group - 1) * 2 * n)],
            [same],
            [pltpu.VMEM((2 * k, n), BF16)],
            "_own",
            work,
        )
        out, keep, mine_u, xr, xg = matrix_call(
            main_kernel,
            range(parts, total_pieces),
            total_pieces,
            [
                shape(group - 1, k, 2 * n),
                shape(group - 1, k, 2 * n),
                shape(k, n),
                jax.ShapeDtypeStruct((2 * k, rows), BF16),
                jax.ShapeDtypeStruct((2 * k, (group - 1) * 2 * n), BF16),
            ],
            [pair, u0, v0, *mine, *theirs],
            [pltpu.VMEM((k, rows), F32), pltpu.VMEM((k, (group - 1) * 2 * n), F32)],
            "",
            8 * work,
        )
        got = swap(out)
        near = call(
            functools.partial(near_kernel, k, n, tile),
            shape(k, 2 * n),
            2,
            limit=8 << 20,
            name=name + "_near",
            flops=work,
        )(held[0], xr)
        got, near = lax.optimization_barrier((got, near))
        sums = call(
            functools.partial(combine_kernel, k, n, group, extra),
            (shape(k, pair.shape[1]),) * (group - 1) + ((shape(k, 8 * k),) if extra else ()),
            2 + (2 * group - 1 if extra else 0),
            name=name + "_combine",
        )(keep, got, *((pair, *mine, *theirs) if extra else ()))
        arrived = [send(sums[s - 1], spread(s)) for s in steps]
        total = call(
            functools.partial(late_kernel, *sizes, extra),
            shape(k, pair.shape[1]),
            parts - 1 + group - 1 + 6 + extra,
            scratch=[pltpu.VMEM((k, 2 * n), F32), pltpu.VMEM((k, n), F32)],
            limit=8 << 20,
            name=name + "_late",
            flops=3 * work,
        )(*held[1 : parts + group - 1], xr, xg, near, mine_u, pair, energy, *sums[group - 1 :])
        for v in arrived:
            total = total + v
        return total, swap(total), held

    mine, got, held = products(held, first, "first")
    pair = call(functools.partial(pair_kernel, k, n), shape(k, 2 * n + 8 * k), 3, name="pair")(first, mine, got)
    mine, got, held = products(held, pair, "second")
    q, prod, moments, proj0, fact0 = call(
        functools.partial(second_kernel, k, n, order),
        (shape(k, 2 * n), shape(k, 2 * n), shape(3 * k, 3 * k), shape(k, k), shape(k, k)),
        4,
        name="middle",
    )(first, pair, mine, got)
    moments = sum([send(moments, lambda r, c, s=s: chip(r, c, s, 0)) for s in steps], moments)
    sums = [moments] + [send(moments, lambda r, c, s=s: chip(r, c, 0, s)) for s in steps]
    basis, proj, fact = call(
        functools.partial(last_kernel, k, n, order),
        (shape(k, n), shape(2, k, k), shape(2, k, k)),
        5 + group,
        name="last",
    )(first, q, prod, proj0, fact0, *sums)
    return basis.T, proj, fact


def solution(mesh):
    n_row, n_col = mesh.shape["row"], mesh.shape["col"]

    def body(coupling, energies, block):
        n, k = block.shape
        paired = n_col == 2 * n_row and n_row & (n_row - 1) == 0 and n_row > 1
        divides = coupling.shape[0] * n % 768 == 0
        whole = divides and n % 64 == 0 and n >= 256 and 8 * k == 128 and coupling.shape[2] == coupling.shape[0] * n * 2
        small = coupling.size * 4 <= 44 << 20
        if paired and whole and small:
            return on_device(n_row, n_col, coupling, energies, block)
        return generic(coupling, energies, block)

    placed = (P(None, "col", "row"), P(("row", "col")), P(("row", "col"), None))
    return jax.shard_map(
        body,
        mesh=mesh,
        in_specs=placed,
        out_specs=(P(("row", "col"), None), P(), P()),
        check_vma=False,
    )
```

```python
import functools

import jax
import jax.numpy as jnp
from jax import lax
from jax.experimental import pallas as pl
from jax.experimental.pallas import tpu as pltpu
from jax.sharding import PartitionSpec as P

ITERS = 2
F32 = jnp.float32
BF16 = jnp.bfloat16

precise = lax.Precision.HIGHEST

NN = (((1,), (0,)), ((), ()))
NT = (((1,), (1,)), ((), ()))
TN = (((0,), (0,)), ((), ()))

VMEM_SPEC = pl.BlockSpec(memory_space=pltpu.VMEM)


def generic(coupling, energies, block):
    order = block.shape[0] * lax.axis_size("row") * lax.axis_size("col")
    segment = block.shape[0]
    width = block.shape[1]
    column = lax.axis_index("col")
    current, energy_rows = (
        lax.all_gather(block, "col", axis=0, tiled=True),
        lax.all_gather(energies, "col", axis=0, tiled=True),
    )
    prior = jnp.zeros_like(current)
    projection_list = []
    factor_list = []
    for section in range(ITERS):
        own_rows = lax.dynamic_slice_in_dim(current, column * segment, segment, 0)
        spread = lax.all_gather(own_rows, "row", axis=0, tiled=True)
        spread = spread.reshape(coupling.shape[0], segment, width)
        direct = lax.psum_scatter(
            jnp.einsum("aig,gk->aik", coupling, current, precision=precise),
            "row",
            scatter_dimension=0,
            tiled=True,
        ).reshape(segment, width)
        partial_value = jnp.einsum("aig,aik->gk", coupling, spread, precision=precise)
        transposed = lax.psum(partial_value, "col")
        direct_rows = lax.all_gather(direct, "col", axis=0, tiled=True)
        product = energy_rows[:, None] * current + direct_rows + transposed
        stacked = jnp.concatenate([current, prior, product], axis=1)
        moments = lax.psum(jnp.einsum("nk,nl->kl", stacked, stacked, precision=precise), "row") / order
        projection = moments[:width, 2 * width :]
        cross = moments[width : 2 * width, 2 * width :]
        weights = jnp.concatenate([-projection, -cross, jnp.eye(width, dtype=F32)], axis=0)
        gram_matrix = jnp.dot(weights.T, jnp.dot(moments, weights, precision=precise), precision=precise)
        factor = jnp.linalg.cholesky(gram_matrix)
        residual = (
            product
            - jnp.dot(current, projection, precision=precise)
            - jnp.dot(prior, cross, precision=precise)
        )
        prior = current
        current = jax.scipy.linalg.solve_triangular(factor, residual.T, lower=True).T
        projection_list.append(projection)
        factor_list.append(factor)
    basis = lax.dynamic_slice_in_dim(current, column * segment, segment, 0)
    return (basis, jnp.stack(projection_list), jnp.stack(factor_list))


def place():
    column = lax.axis_index("col")
    return lax.rem(column, 2), lax.div(column, 2), lax.axis_index("row")


def split(value):
    high = value.astype(BF16)
    return high, (value - high.astype(F32)).astype(BF16)


def dot(left, right, dims):
    return lax.dot_general(left, right, dims, preferred_element_type=F32)


def dot32(left, right, dims):
    return lax.dot_general(left, right, dims, preferred_element_type=F32, precision=precise)


def own_half(value, even, n):
    return jnp.where(even, value[:, :n], value[:, n : 2 * n])


def in_half(value, even):
    zero = jnp.zeros_like(value)
    return jnp.concatenate([jnp.where(even, value, zero), jnp.where(even, zero, value)], axis=1)


def pieces_of(part, group, n, rows):
    found, at, end = [], part * rows, (part + 1) * rows
    while at < end:
        s, off = divmod(at, n)
        count = min(n - off, end - at)
        found.append((s, off, at - part * rows, count))
        at += count
    return found


def order_of(group, parts):
    near = [(0, p) for p in range(parts)]
    lead = [(s, 0) for s in range(1, group)]
    return near + lead + [(s, p) for s in range(1, group) for p in range(1, parts)]


class Loader:
    def __init__(self, source, arrived, n, group, parts, where, held):
        _, z, r = place()

        def copies(i):
            s, part = where[i]
            cols = pl.ds(pl.multiple_of(lax.bitwise_xor(z, s) * (2 * n), 128), 2 * n)
            return [
                pltpu.make_async_copy(
                    source.at[pl.ds(pl.multiple_of(lax.bitwise_xor(r, peer) * n + off, 8), count), cols],
                    held[i].at[pl.ds(at, count), :],
                    arrived.at[i, j],
                )
                for j, (peer, off, at, count) in enumerate(pieces_of(part, group, n, group * n // parts))
            ]

        self.copies = copies
        for i in range(len(held)):
            for copy in copies(i):
                copy.start()

    def wait(self, i):
        for copy in self.copies(i):
            copy.wait()


class Pieces:
    def __init__(self, n, group, parts, given, new, scratch, refs):
        order = order_of(group, parts)
        refs = list(refs)
        source = refs.pop(0) if len(new) else None
        held = {order[i]: refs.pop(0) for i in given}
        self.waits = {}
        if len(new):
            arrived = refs.pop()
            at = len(refs) - scratch - len(new)
            fresh, refs = refs[at : at + len(new)], refs[:at] + refs[at + len(new) :]
            where = [order[i] for i in new]
            self.loader = Loader(source, arrived, n, group, parts, where, fresh)
            self.waits = {key: i for i, key in enumerate(where)}
            held.update(zip(where, fresh))
        self.held, self.refs = held, refs

    def get(self, s, p):
        if (s, p) in self.waits:
            self.loader.wait(self.waits.pop((s, p)))
        return self.held[s, p]

    def finish(self):
        for key in list(self.waits):
            self.get(*key)


def tiles_of(piece, tile, first, last, step):
    def body(t, carry):
        high, low = split(piece[pl.ds(pl.multiple_of(t * tile, tile), tile), :])
        step(t, high, low)
        return carry

    lax.fori_loop(first, last, body, 0)


def across(xg, cols, k, high, low):
    one = dot(xg[:, cols], high, NT)
    two = dot(xg[:k, cols], low, NT)
    return one[:k] + one[k:] + two


def along(xr, at, k, high, low):
    one = dot(xr[:, at], high, NN)
    two = dot(xr[:k, at], low, NN)
    return one[:k] + one[k:] + two


def begin_kernel(k, n, group, parts, source, block_ref, own_ref, *refs):
    *held, arrived, ready = refs
    copy = pltpu.make_async_copy(block_ref, own_ref, ready)
    copy.start()
    loader = Loader(source, arrived, n, group, parts, order_of(group, parts), held)
    copy.wait()
    for i in range(len(held)):
        loader.wait(i)


def order_kernel(k, n, own_ref, other_ref, out_ref):
    even = place()[0] == 0
    own, other = own_ref[...], other_ref[...]
    out_ref[...] = jnp.concatenate([jnp.where(even, own, other), jnp.where(even, other, own)], axis=1)


def put(slab, at, k, value):
    high, low = split(value)
    slab[:k, at : at + value.shape[1]] = high
    slab[k:, at : at + value.shape[1]] = low


def turned(s, group, even):
    return jnp.logical_not(even) if s == group - 1 else even


def early_kernel(k, n, group, tile, parts, given, new, *refs):
    pieces = Pieces(n, group, parts, given, new, 1, refs)
    xg = pieces.refs.pop(-1)
    pair_ref, u_ref = pieces.refs
    put(xg, 0, k, pair_ref[:, : 2 * n])
    for p in range(parts):
        piece = pieces.get(0, p)
        rows = piece.shape[0]

        def step(t, high, low):
            u_ref[:, pl.ds(pl.multiple_of(p * rows + t * tile, tile), tile)] = across(xg, slice(None), k, high, low)

        tiles_of(piece, tile, 0, rows // tile, step)
    pieces.finish()


def own_kernel(k, n, group, tile, parts, given, new, *refs):
    pieces = Pieces(n, group, parts, given, new, 1, refs)
    xr = pieces.refs.pop(-1)
    pair_ref, v_ref = pieces.refs
    even = place()[0] == 0
    put(xr, 0, k, own_half(pair_ref, even, n))
    v_ref[...] = jnp.zeros_like(v_ref)
    for s in range(1, group):
        cols = slice((s - 1) * 2 * n, s * 2 * n)

        def step(t, high, low):
            v_ref[:, cols] += along(xr, pl.ds(pl.multiple_of(t * tile, tile), tile), k, high, low)

        tiles_of(pieces.get(s, 0), tile, 0, n // tile, step)
    pieces.finish()


def main_kernel(k, n, group, tile, parts, given, new, *refs):
    pieces = Pieces(n, group, parts, given, new, 2, refs)
    u_acc, v_acc = pieces.refs[-2:]
    refs = pieces.refs[:-2]
    pair_ref, u0_ref, v0_ref, mine, theirs = refs[0], refs[1], refs[2], refs[3 : group + 2], refs[group + 2 : 2 * group + 1]
    send_ref, keep_ref, own_ref, xr, xg = refs[2 * group + 1 :]
    even = place()[0] == 0

    segments = [own_half(pair_ref, even, n)]
    for s in range(1, group):
        y, w = mine[s - 1][:, : 2 * n], theirs[s - 1][:, : 2 * n]
        to_z = turned(s, group, even)
        put(xg, (s - 1) * 2 * n, k, jnp.where(to_z, y, w))
        segments.append(own_half(jnp.where(to_z, w, y), even, n))
    for a in range(0, group, 2):
        put(xr, a * n, k, jnp.concatenate(segments[a : a + 2], axis=1))
    u_acc[...] = u0_ref[...]
    v_acc[...] = v0_ref[...]

    for s, p in order_of(group, parts)[parts:]:
        piece = pieces.get(s, p)
        rows = piece.shape[0]
        cols = slice((s - 1) * 2 * n, s * 2 * n)

        def step(t, high, low):
            at = pl.ds(pl.multiple_of(p * rows + t * tile, tile), tile)
            v_acc[:, cols] += along(xr, at, k, high, low)
            u_acc[:, at] += across(xg, cols, k, high, low)

        tiles_of(piece, tile, n // tile if p == 0 else 0, rows // tile, step)

    own_ref[...] = u_acc[:, :n]
    for s in range(1, group):
        to_z = turned(s, group, even)
        by_z = v_acc[:, 2 * n * (s - 1) : 2 * n * s]
        by_row = in_half(u_acc[:, n * s : n * (s + 1)], even)
        keep_ref[s - 1] = jnp.where(to_z, by_z, by_row)
        send_ref[s - 1] = jnp.where(to_z, by_row, by_z)


def near_kernel(k, n, tile, piece, xr, v_ref):
    v_ref[...] = jnp.zeros_like(v_ref)

    def step(t, high, low):
        v_ref[...] += along(xr, pl.ds(pl.multiple_of(t * tile, tile), tile), k, high, low)

    tiles_of(piece, tile, 0, piece.shape[0] // tile, step)


def late_kernel(k, n, group, tile, parts, extra, *refs):
    near, lead, refs = refs[: parts - 1], refs[parts - 1 : parts + group - 2], refs[parts + group - 2 :]
    xr, xg, v_ref, own_ref, pair_ref, energy_ref, *refs = refs
    more, refs = (refs[0], refs[1:]) if extra else (None, refs)
    out_ref, v_acc, u_acc = refs
    even = place()[0] == 0
    v_acc[...] = v_ref[...]
    u_acc[...] = own_ref[...]
    for p in range(1, parts):
        rows = near[p - 1].shape[0]

        def step(t, high, low):
            v_acc[...] += along(xr, pl.ds(pl.multiple_of(p * rows + t * tile, tile), tile), k, high, low)

        tiles_of(near[p - 1], tile, 0, rows // tile, step)
    for s in range(1, group):
        cols = slice((s - 1) * 2 * n, s * 2 * n)

        def step(t, high, low):
            u_acc[:, pl.ds(pl.multiple_of(t * tile, tile), tile)] += across(xg, cols, k, high, low)

        tiles_of(lead[s - 1], tile, 0, n // tile, step)
    own = energy_ref[...] * own_half(pair_ref, even, n) + u_acc[...]
    out_ref[:, : 2 * n] = v_acc[...] + in_half(own, even)
    if extra:
        part = more[...]
        out_ref[:, 2 * n :] = jnp.where(even, part, jnp.zeros_like(part))


def combine_kernel(k, n, group, extra, keep_ref, got_ref, *refs):
    even = place()[0] == 0
    if extra:
        pair_ref, mine, theirs, outs = refs[0], refs[1:group], refs[group : 2 * group - 1], refs[2 * group - 1 :]
        part = pair_ref[:, 2 * n :]
        for s in range(1, group):
            to_z = turned(s, group, even)
            part = part + jnp.where(to_z, theirs[s - 1][:, 2 * n :], mine[s - 1][:, 2 * n :])
        outs[group - 1][...] = part
    else:
        outs = refs
    for s in range(1, group):
        outs[s - 1][:, : 2 * n] = keep_ref[s - 1] + got_ref[s - 1]
        if extra:
            outs[s - 1][:, 2 * n :] = jnp.where(turned(s, group, even), part, jnp.zeros_like(part))


def pair_kernel(k, n, first_ref, mine_ref, got_ref, out_ref):
    value = mine_ref[...] + got_ref[...]
    s = jnp.concatenate([first_ref[...], value], axis=0)
    moments = dot32(s, s, NT)
    out_ref[:, : 2 * n] = value
    out_ref[:, 2 * n :] = jnp.zeros((k, 8 * k), F32)
    out_ref[:, 2 * n : 2 * n + 2 * k] = moments[:k]
    out_ref[:, 2 * n + 2 * k : 2 * n + 4 * k] = moments[k:]


def factor_of(gram):
    k = gram.shape[0]
    rows = lax.broadcasted_iota(jnp.int32, (k, 2 * k), 0)
    cols = lax.broadcasted_iota(jnp.int32, (k, 2 * k), 1)
    row = lax.broadcasted_iota(jnp.int32, (k, 1), 0)
    both = jnp.concatenate([gram, eye(k)], axis=1)
    for j in range(k - 1):
        lead = both[j : j + 1, :]
        lead = lead * (1.0 / both[j : j + 1, j : j + 1])
        both = both - jnp.where(row > j, both[:, j : j + 1], 0.0) * lead
    pivots = jnp.sum(jnp.where(rows == cols, both, 0.0), axis=1, keepdims=True)
    both = both * (1.0 / jnp.sqrt(pivots))
    upper = jnp.where(rows <= cols, both, 0.0)[:, :k]
    return dot32(upper, eye(k), TN), both[:, k:]


def gram_of(moments, coefficients):
    k = moments.shape[0]
    w = coefficients.shape[1]
    parts = jnp.concatenate([-coefficients, eye(w)], axis=0)
    return dot32(parts, dot32(moments, parts, NN), TN)


def eye(k):
    return jnp.where(
        lax.broadcasted_iota(jnp.int32, (k, k), 0) == lax.broadcasted_iota(jnp.int32, (k, k), 1), 1.0, 0.0
    ).astype(F32)


def second_kernel(k, n, order, first_ref, pair_ref, mine_ref, got_ref, q_ref, prod_ref, mom_ref, proj_ref, fact_ref):
    packed = mine_ref[:, 2 * n :] + got_ref[:, 2 * n :]
    moments = jnp.concatenate([packed[:, : 2 * k], packed[:, 2 * k : 4 * k]], axis=0) * (1.0 / order)
    projection = moments[:k, k:]
    lower, inverse = factor_of(gram_of(moments, projection))
    proj_ref[...] = projection
    fact_ref[...] = lower
    x, y = first_ref[...], pair_ref[:, : 2 * n]
    w = mine_ref[:, : 2 * n] + got_ref[:, : 2 * n]
    rest = jnp.concatenate([y, w], axis=1) - dot32(projection, jnp.concatenate([x, y], axis=1), TN)
    both = dot32(inverse, rest, NN)
    q, prod = both[:, : 2 * n], both[:, 2 * n :]
    q_ref[...] = q
    prod_ref[...] = prod
    s = jnp.concatenate([q, x, prod], axis=0)
    mom_ref[...] = dot32(s, s, NT)


def last_kernel(k, n, order, first_ref, q_ref, prod_ref, proj0_ref, fact0_ref, *refs):
    *sums, basis_ref, proj_ref, fact_ref = refs
    total = sums[0][...]
    for m in sums[1:]:
        total = total + m[...]
    moments = total * (1.0 / order)
    coefficients = moments[: 2 * k, 2 * k :]
    lower, inverse = factor_of(gram_of(moments, coefficients))
    proj_ref[0] = proj0_ref[...]
    proj_ref[1] = coefficients[:k]
    fact_ref[0] = fact0_ref[...]
    fact_ref[1] = lower
    even = place()[0] == 0
    before = jnp.concatenate([own_half(q_ref, even, n), own_half(first_ref, even, n)], axis=0)
    rest = own_half(prod_ref, even, n) - dot32(coefficients, before, TN)
    basis_ref[...] = dot32(inverse, rest, NN)


def call(kernel, out_shape, n_in, scratch=(), limit=1 << 20, name=None, far=0, flops=0):
    many = isinstance(out_shape, (tuple, list))
    run = pl.pallas_call(
        kernel,
        out_shape=out_shape,
        in_specs=[pl.BlockSpec(memory_space=pl.ANY) if i < far else VMEM_SPEC for i in range(n_in)],
        out_specs=tuple([VMEM_SPEC] * len(out_shape)) if many else VMEM_SPEC,
        scratch_shapes=list(scratch),
        compiler_params=pltpu.CompilerParams(vmem_limit_bytes=limit),
        cost_estimate=pl.CostEstimate(flops=flops, transcendentals=0, bytes_accessed=flops // 128) if flops else None,
        name=name,
    )
    return lambda *args: run(
        *[pltpu.with_memory_space_constraint(v, pltpu.HBM if i < far else pltpu.VMEM) for i, v in enumerate(args)]
    )


def shape(*dims):
    return jax.ShapeDtypeStruct(dims, F32)


def on_device(n_row, n_col, coupling, energies, block):
    n, k = block.shape
    group = n_row
    order = n * n_row * n_col
    rows = coupling.shape[0] * n
    width = coupling.shape[2]
    axes = ("row", "col")
    flat = [(r, c) for r in range(n_row) for c in range(n_col)]

    def send(value, to):
        pairs = [(r * n_col + c, to(r, c)) for r, c in flat]
        return lax.ppermute(value, axes, [p for p in pairs if p[1] is not None])

    def swap(value):
        return send(value, lambda r, c: r * n_col + (c ^ 1))

    def chip(r, c, s_row, s_z):
        return (r ^ s_row) * n_col + (c ^ (2 * s_z))

    def spread(s):
        def to(r, c):
            along_z = (c % 2 == 0) != (s == group - 1)
            return chip(r, c, 0, s) if along_z else chip(r, c, s, 0)

        return to

    steps = range(1, group)
    tile, parts = 256, 3
    total_pieces = group * parts
    block_shape = shape(rows // parts, 2 * n)
    most = max(len(pieces_of(p, group, n, rows // parts)) for p in range(parts))
    semaphores = lambda count: [pltpu.SemaphoreType.DMA((count, most))]
    work = rows * 2 * n * 256
    a = coupling.reshape(rows, width)
    energy = energies.reshape(1, n)

    other = swap(block.T)
    own, *held = call(
        functools.partial(begin_kernel, k, n, group, parts),
        (shape(k, n), block_shape),
        2,
        scratch=semaphores(1) + [pltpu.SemaphoreType.DMA],
        name="begin",
        far=2,
        flops=work // 4,
    )(a, block.T)
    first = call(functools.partial(order_kernel, k, n), shape(k, 2 * n), 2, name="order")(own, other)

    def products(held, pair, name):
        extra = pair.shape[1] > 2 * n
        sizes = (k, n, group, tile, parts)
        load = len(held) < total_pieces

        def matrix_call(kernel, need, upto, out_shapes, args, scratch, label, flops):
            given = [i for i in need if i < len(held)]
            new = range(len(held), max(upto, len(held)))
            outs = call(
                functools.partial(kernel, *sizes, given, new),
                tuple(out_shapes) + (block_shape,) * len(new),
                (len(new) > 0) + len(given) + len(args),
                scratch=list(scratch) + (semaphores(len(new)) if new else []),
                limit=8 << 20,
                name=name + label,
                far=int(len(new) > 0),
                flops=flops,
            )(*([a] if new else []), *[held[i] for i in given], *args)
            held.extend(outs[len(out_shapes) :])
            return outs[: len(out_shapes)]

        mine = [send(pair, spread(s)) for s in reversed(steps)][::-1]
        (u0,) = matrix_call(
            early_kernel,
            range(parts),
            parts + 2,
            [shape(k, rows)],
            [pair],
            [pltpu.VMEM((2 * k, 2 * n), BF16)],
            "_early",
            2 * work,
        )
        u0, same, *mine = lax.optimization_barrier((u0, pair, *mine))
        theirs = [swap(y) for y in mine]
        (v0,) = matrix_call(
            own_kernel,
            range(parts, parts + group - 1),
            parts + group,
            [shape(k, (group - 1) * 2 * n)],
            [same],
            [pltpu.VMEM((2 * k, n), BF16)],
            "_own",
            work,
        )
        out, keep, mine_u, xr, xg = matrix_call(
            main_kernel,
            range(parts, total_pieces),
            total_pieces,
            [
                shape(group - 1, k, 2 * n),
                shape(group - 1, k, 2 * n),
                shape(k, n),
                jax.ShapeDtypeStruct((2 * k, rows), BF16),
                jax.ShapeDtypeStruct((2 * k, (group - 1) * 2 * n), BF16),
            ],
            [pair, u0, v0, *mine, *theirs],
            [pltpu.VMEM((k, rows), F32), pltpu.VMEM((k, (group - 1) * 2 * n), F32)],
            "",
            8 * work,
        )
        got = swap(out)
        near = call(
            functools.partial(near_kernel, k, n, tile),
            shape(k, 2 * n),
            2,
            limit=8 << 20,
            name=name + "_near",
            flops=work,
        )(held[0], xr)
        got, near = lax.optimization_barrier((got, near))
        sums = call(
            functools.partial(combine_kernel, k, n, group, extra),
            (shape(k, pair.shape[1]),) * (group - 1) + ((shape(k, 8 * k),) if extra else ()),
            2 + (2 * group - 1 if extra else 0),
            name=name + "_combine",
        )(keep, got, *((pair, *mine, *theirs) if extra else ()))
        arrived = [send(sums[s - 1], spread(s)) for s in steps]
        total = call(
            functools.partial(late_kernel, *sizes, extra),
            shape(k, pair.shape[1]),
            parts - 1 + group - 1 + 6 + extra,
            scratch=[pltpu.VMEM((k, 2 * n), F32), pltpu.VMEM((k, n), F32)],
            limit=8 << 20,
            name=name + "_late",
            flops=3 * work,
        )(*held[1 : parts + group - 1], xr, xg, near, mine_u, pair, energy, *sums[group - 1 :])
        for v in arrived:
            total = total + v
        return total, swap(total), held

    mine, got, held = products(held, first, "first")
    pair = call(functools.partial(pair_kernel, k, n), shape(k, 2 * n + 8 * k), 3, name="pair")(first, mine, got)
    mine, got, held = products(held, pair, "second")
    q, prod, moments, proj0, fact0 = call(
        functools.partial(second_kernel, k, n, order),
        (shape(k, 2 * n), shape(k, 2 * n), shape(3 * k, 3 * k), shape(k, k), shape(k, k)),
        4,
        name="middle",
    )(first, pair, mine, got)
    moments = sum([send(moments, lambda r, c, s=s: chip(r, c, s, 0)) for s in reversed(steps)], moments)
    sums = [moments] + [send(moments, lambda r, c, s=s: chip(r, c, 0, s)) for s in reversed(steps)]
    basis, proj, fact = call(
        functools.partial(last_kernel, k, n, order),
        (shape(k, n), shape(2, k, k), shape(2, k, k)),
        5 + group,
        name="last",
    )(first, q, prod, proj0, fact0, *sums)
    return basis.T, proj, fact


def solution(mesh):
    n_row, n_col = mesh.shape["row"], mesh.shape["col"]

    def body(coupling, energies, block):
        n, k = block.shape
        paired = n_col == 2 * n_row and n_row & (n_row - 1) == 0 and n_row > 1
        divides = coupling.shape[0] * n % 768 == 0
        whole = divides and n % 64 == 0 and n >= 256 and 8 * k == 128 and coupling.shape[2] == coupling.shape[0] * n * 2
        small = coupling.size * 4 <= 44 << 20
        if paired and whole and small:
            return on_device(n_row, n_col, coupling, energies, block)
        return generic(coupling, energies, block)

    placed = (P(None, "col", "row"), P(("row", "col")), P(("row", "col"), None))
    return jax.shard_map(
        body,
        mesh=mesh,
        in_specs=placed,
        out_specs=(P(("row", "col"), None), P(), P()),
        check_vma=False,
    )
```

```python
import functools

import jax
import jax.numpy as jnp
from jax import lax
from jax.experimental import pallas as pl
from jax.experimental.pallas import tpu as pltpu
from jax.sharding import PartitionSpec as P

ITERS = 2
F32 = jnp.float32
BF16 = jnp.bfloat16

precise = lax.Precision.HIGHEST

NN = (((1,), (0,)), ((), ()))
NT = (((1,), (1,)), ((), ()))
TN = (((0,), (0,)), ((), ()))

VMEM_SPEC = pl.BlockSpec(memory_space=pltpu.VMEM)


def generic(coupling, energies, block):
    order = block.shape[0] * lax.axis_size("row") * lax.axis_size("col")
    segment = block.shape[0]
    width = block.shape[1]
    column = lax.axis_index("col")
    current, energy_rows = (
        lax.all_gather(block, "col", axis=0, tiled=True),
        lax.all_gather(energies, "col", axis=0, tiled=True),
    )
    prior = jnp.zeros_like(current)
    projection_list = []
    factor_list = []
    for section in range(ITERS):
        own_rows = lax.dynamic_slice_in_dim(current, column * segment, segment, 0)
        spread = lax.all_gather(own_rows, "row", axis=0, tiled=True)
        spread = spread.reshape(coupling.shape[0], segment, width)
        direct = lax.psum_scatter(
            jnp.einsum("aig,gk->aik", coupling, current, precision=precise),
            "row",
            scatter_dimension=0,
            tiled=True,
        ).reshape(segment, width)
        partial_value = jnp.einsum("aig,aik->gk", coupling, spread, precision=precise)
        transposed = lax.psum(partial_value, "col")
        direct_rows = lax.all_gather(direct, "col", axis=0, tiled=True)
        product = energy_rows[:, None] * current + direct_rows + transposed
        stacked = jnp.concatenate([current, prior, product], axis=1)
        moments = lax.psum(jnp.einsum("nk,nl->kl", stacked, stacked, precision=precise), "row") / order
        projection = moments[:width, 2 * width :]
        cross = moments[width : 2 * width, 2 * width :]
        weights = jnp.concatenate([-projection, -cross, jnp.eye(width, dtype=F32)], axis=0)
        gram_matrix = jnp.dot(weights.T, jnp.dot(moments, weights, precision=precise), precision=precise)
        factor = jnp.linalg.cholesky(gram_matrix)
        residual = (
            product
            - jnp.dot(current, projection, precision=precise)
            - jnp.dot(prior, cross, precision=precise)
        )
        prior = current
        current = jax.scipy.linalg.solve_triangular(factor, residual.T, lower=True).T
        projection_list.append(projection)
        factor_list.append(factor)
    basis = lax.dynamic_slice_in_dim(current, column * segment, segment, 0)
    return (basis, jnp.stack(projection_list), jnp.stack(factor_list))


def place():
    column = lax.axis_index("col")
    return lax.rem(column, 2), lax.div(column, 2), lax.axis_index("row")


def split(value):
    high = value.astype(BF16)
    return high, (value - high.astype(F32)).astype(BF16)


def dot(left, right, dims):
    return lax.dot_general(left, right, dims, preferred_element_type=F32)


def dot32(left, right, dims):
    return lax.dot_general(left, right, dims, preferred_element_type=F32, precision=precise)


def own_half(value, even, n):
    return jnp.where(even, value[:, :n], value[:, n : 2 * n])


def in_half(value, even):
    zero = jnp.zeros_like(value)
    return jnp.concatenate([jnp.where(even, value, zero), jnp.where(even, zero, value)], axis=1)


def pieces_of(part, group, n, rows):
    found, at, end = [], part * rows, (part + 1) * rows
    while at < end:
        s, off = divmod(at, n)
        count = min(n - off, end - at)
        found.append((s, off, at - part * rows, count))
        at += count
    return found


def order_of(group, parts):
    near = [(0, p) for p in range(parts)]
    lead = [(s, 0) for s in range(1, group)]
    return near + lead + [(s, p) for s in range(1, group) for p in range(1, parts)]


class Loader:
    def __init__(self, source, arrived, n, group, parts, where, held):
        _, z, r = place()

        def copies(i):
            s, part = where[i]
            cols = pl.ds(pl.multiple_of(lax.bitwise_xor(z, s) * (2 * n), 128), 2 * n)
            return [
                pltpu.make_async_copy(
                    source.at[pl.ds(pl.multiple_of(lax.bitwise_xor(r, peer) * n + off, 8), count), cols],
                    held[i].at[pl.ds(at, count), :],
                    arrived.at[i, j],
                )
                for j, (peer, off, at, count) in enumerate(pieces_of(part, group, n, group * n // parts))
            ]

        self.copies = copies
        for i in range(len(held)):
            for copy in copies(i):
                copy.start()

    def wait(self, i):
        for copy in self.copies(i):
            copy.wait()


class Pieces:
    def __init__(self, n, group, parts, given, new, scratch, refs):
        order = order_of(group, parts)
        refs = list(refs)
        source = refs.pop(0) if len(new) else None
        held = {order[i]: refs.pop(0) for i in given}
        self.waits = {}
        if len(new):
            arrived = refs.pop()
            at = len(refs) - scratch - len(new)
            fresh, refs = refs[at : at + len(new)], refs[:at] + refs[at + len(new) :]
            where = [order[i] for i in new]
            self.loader = Loader(source, arrived, n, group, parts, where, fresh)
            self.waits = {key: i for i, key in enumerate(where)}
            held.update(zip(where, fresh))
        self.held, self.refs = held, refs

    def get(self, s, p):
        if (s, p) in self.waits:
            self.loader.wait(self.waits.pop((s, p)))
        return self.held[s, p]

    def finish(self):
        for key in list(self.waits):
            self.get(*key)


def tiles_of(piece, tile, first, last, step):
    def body(t, carry):
        high, low = split(piece[pl.ds(pl.multiple_of(t * tile, tile), tile), :])
        step(t, high, low)
        return carry

    lax.fori_loop(first, last, body, 0)


def across(xg, cols, k, high, low):
    one = dot(xg[:, cols], high, NT)
    two = dot(xg[:k, cols], low, NT)
    return one[:k] + one[k:] + two


def along(xr, at, k, high, low):
    one = dot(xr[:, at], high, NN)
    two = dot(xr[:k, at], low, NN)
    return one[:k] + one[k:] + two


def begin_kernel(k, n, group, parts, source, block_ref, own_ref, *refs):
    *held, arrived, ready = refs
    copy = pltpu.make_async_copy(block_ref, own_ref, ready)
    copy.start()
    loader = Loader(source, arrived, n, group, parts, order_of(group, parts), held)
    copy.wait()
    for i in range(len(held)):
        loader.wait(i)


def order_kernel(k, n, own_ref, other_ref, out_ref):
    even = place()[0] == 0
    own, other = own_ref[...], other_ref[...]
    out_ref[...] = jnp.concatenate([jnp.where(even, own, other), jnp.where(even, other, own)], axis=1)


def put(slab, at, k, value):
    high, low = split(value)
    slab[:k, at : at + value.shape[1]] = high
    slab[k:, at : at + value.shape[1]] = low


def turned(s, group, even):
    return jnp.logical_not(even) if s == group - 1 else even


def early_kernel(k, n, group, tile, parts, given, new, *refs):
    pieces = Pieces(n, group, parts, given, new, 1, refs)
    xg = pieces.refs.pop(-1)
    pair_ref, u_ref = pieces.refs
    put(xg, 0, k, pair_ref[:, : 2 * n])
    for p in range(parts):
        piece = pieces.get(0, p)
        rows = piece.shape[0]

        def step(t, high, low):
            u_ref[:, pl.ds(pl.multiple_of(p * rows + t * tile, tile), tile)] = across(xg, slice(None), k, high, low)

        tiles_of(piece, tile, 0, rows // tile, step)
    pieces.finish()


def own_kernel(k, n, group, tile, parts, given, new, *refs):
    pieces = Pieces(n, group, parts, given, new, 1, refs)
    xr = pieces.refs.pop(-1)
    pair_ref, v_ref = pieces.refs
    even = place()[0] == 0
    put(xr, 0, k, own_half(pair_ref, even, n))
    v_ref[...] = jnp.zeros_like(v_ref)
    for s in range(1, group):
        cols = slice((s - 1) * 2 * n, s * 2 * n)

        def step(t, high, low):
            v_ref[:, cols] += along(xr, pl.ds(pl.multiple_of(t * tile, tile), tile), k, high, low)

        tiles_of(pieces.get(s, 0), tile, 0, n // tile, step)
    pieces.finish()


def main_kernel(k, n, group, tile, parts, given, new, *refs):
    pieces = Pieces(n, group, parts, given, new, 2, refs)
    u_acc, v_acc = pieces.refs[-2:]
    refs = pieces.refs[:-2]
    pair_ref, u0_ref, v0_ref, mine, theirs = refs[0], refs[1], refs[2], refs[3 : group + 2], refs[group + 2 : 2 * group + 1]
    send_ref, keep_ref, own_ref, xr, xg = refs[2 * group + 1 :]
    even = place()[0] == 0

    segments = [own_half(pair_ref, even, n)]
    for s in range(1, group):
        y, w = mine[s - 1][:, : 2 * n], theirs[s - 1][:, : 2 * n]
        to_z = turned(s, group, even)
        put(xg, (s - 1) * 2 * n, k, jnp.where(to_z, y, w))
        segments.append(own_half(jnp.where(to_z, w, y), even, n))
    for a in range(0, group, 2):
        put(xr, a * n, k, jnp.concatenate(segments[a : a + 2], axis=1))
    u_acc[...] = u0_ref[...]
    v_acc[...] = v0_ref[...]

    for s, p in order_of(group, parts)[parts:]:
        piece = pieces.get(s, p)
        rows = piece.shape[0]
        cols = slice((s - 1) * 2 * n, s * 2 * n)

        def step(t, high, low):
            at = pl.ds(pl.multiple_of(p * rows + t * tile, tile), tile)
            v_acc[:, cols] += along(xr, at, k, high, low)
            u_acc[:, at] += across(xg, cols, k, high, low)

        tiles_of(piece, tile, n // tile if p == 0 else 0, rows // tile, step)

    own_ref[...] = u_acc[:, :n]
    for s in range(1, group):
        to_z = turned(s, group, even)
        by_z = v_acc[:, 2 * n * (s - 1) : 2 * n * s]
        by_row = in_half(u_acc[:, n * s : n * (s + 1)], even)
        keep_ref[s - 1] = jnp.where(to_z, by_z, by_row)
        send_ref[s - 1] = jnp.where(to_z, by_row, by_z)


def near_kernel(k, n, tile, piece, xr, v_ref):
    v_ref[...] = jnp.zeros_like(v_ref)

    def step(t, high, low):
        v_ref[...] += along(xr, pl.ds(pl.multiple_of(t * tile, tile), tile), k, high, low)

    tiles_of(piece, tile, 0, piece.shape[0] // tile, step)


def late_kernel(k, n, group, tile, parts, extra, *refs):
    near, lead, refs = refs[: parts - 1], refs[parts - 1 : parts + group - 2], refs[parts + group - 2 :]
    xr, xg, v_ref, own_ref, pair_ref, energy_ref, *refs = refs
    more, refs = (refs[0], refs[1:]) if extra else (None, refs)
    out_ref, v_acc, u_acc = refs
    even = place()[0] == 0
    v_acc[...] = v_ref[...]
    u_acc[...] = own_ref[...]
    for p in range(1, parts):
        rows = near[p - 1].shape[0]

        def step(t, high, low):
            v_acc[...] += along(xr, pl.ds(pl.multiple_of(p * rows + t * tile, tile), tile), k, high, low)

        tiles_of(near[p - 1], tile, 0, rows // tile, step)
    for s in range(1, group):
        cols = slice((s - 1) * 2 * n, s * 2 * n)

        def step(t, high, low):
            u_acc[:, pl.ds(pl.multiple_of(t * tile, tile), tile)] += across(xg, cols, k, high, low)

        tiles_of(lead[s - 1], tile, 0, n // tile, step)
    own = energy_ref[...] * own_half(pair_ref, even, n) + u_acc[...]
    out_ref[:, : 2 * n] = v_acc[...] + in_half(own, even)
    if extra:
        part = more[...]
        out_ref[:, 2 * n :] = jnp.where(even, part, jnp.zeros_like(part))


def combine_kernel(k, n, group, extra, keep_ref, got_ref, *refs):
    even = place()[0] == 0
    if extra:
        pair_ref, mine, theirs, outs = refs[0], refs[1:group], refs[group : 2 * group - 1], refs[2 * group - 1 :]
        part = pair_ref[:, 2 * n :]
        for s in range(1, group):
            to_z = turned(s, group, even)
            part = part + jnp.where(to_z, theirs[s - 1][:, 2 * n :], mine[s - 1][:, 2 * n :])
        outs[group - 1][...] = part
    else:
        outs = refs
    for s in range(1, group):
        outs[s - 1][:, : 2 * n] = keep_ref[s - 1] + got_ref[s - 1]
        if extra:
            outs[s - 1][:, 2 * n :] = jnp.where(turned(s, group, even), part, jnp.zeros_like(part))


def pair_kernel(k, n, first_ref, mine_ref, got_ref, out_ref):
    value = mine_ref[...] + got_ref[...]
    s = jnp.concatenate([first_ref[...], value], axis=0)
    moments = dot32(s, s, NT)
    out_ref[:, : 2 * n] = value
    out_ref[:, 2 * n :] = jnp.zeros((k, 8 * k), F32)
    out_ref[:, 2 * n : 2 * n + 2 * k] = moments[:k]
    out_ref[:, 2 * n + 2 * k : 2 * n + 4 * k] = moments[k:]


def factor_of(gram):
    k = gram.shape[0]
    rows = lax.broadcasted_iota(jnp.int32, (k, 2 * k), 0)
    cols = lax.broadcasted_iota(jnp.int32, (k, 2 * k), 1)
    row = lax.broadcasted_iota(jnp.int32, (k, 1), 0)
    both = jnp.concatenate([gram, eye(k)], axis=1)
    for j in range(k - 1):
        lead = both[j : j + 1, :]
        lead = lead * (1.0 / both[j : j + 1, j : j + 1])
        both = both - jnp.where(row > j, both[:, j : j + 1], 0.0) * lead
    pivots = jnp.sum(jnp.where(rows == cols, both, 0.0), axis=1, keepdims=True)
    both = both * (1.0 / jnp.sqrt(pivots))
    upper = jnp.where(rows <= cols, both, 0.0)[:, :k]
    return dot32(upper, eye(k), TN), both[:, k:]


def gram_of(moments, coefficients):
    k = moments.shape[0]
    w = coefficients.shape[1]
    parts = jnp.concatenate([-coefficients, eye(w)], axis=0)
    return dot32(parts, dot32(moments, parts, NN), TN)


def eye(k):
    return jnp.where(
        lax.broadcasted_iota(jnp.int32, (k, k), 0) == lax.broadcasted_iota(jnp.int32, (k, k), 1), 1.0, 0.0
    ).astype(F32)


def second_kernel(k, n, order, first_ref, pair_ref, mine_ref, got_ref, q_ref, prod_ref, mom_ref, proj_ref, fact_ref):
    packed = mine_ref[:, 2 * n :] + got_ref[:, 2 * n :]
    moments = jnp.concatenate([packed[:, : 2 * k], packed[:, 2 * k : 4 * k]], axis=0) * (1.0 / order)
    projection = moments[:k, k:]
    lower, inverse = factor_of(gram_of(moments, projection))
    proj_ref[...] = projection
    fact_ref[...] = lower
    x, y = first_ref[...], pair_ref[:, : 2 * n]
    w = mine_ref[:, : 2 * n] + got_ref[:, : 2 * n]
    rest = jnp.concatenate([y, w], axis=1) - dot32(projection, jnp.concatenate([x, y], axis=1), TN)
    both = dot32(inverse, rest, NN)
    q, prod = both[:, : 2 * n], both[:, 2 * n :]
    q_ref[...] = q
    prod_ref[...] = prod
    s = jnp.concatenate([q, x, prod], axis=0)
    mom_ref[...] = dot32(s, s, NT)


def last_kernel(k, n, order, first_ref, q_ref, prod_ref, proj0_ref, fact0_ref, *refs):
    *sums, basis_ref, proj_ref, fact_ref = refs
    total = sums[0][...]
    for m in sums[1:]:
        total = total + m[...]
    moments = total * (1.0 / order)
    coefficients = moments[: 2 * k, 2 * k :]
    lower, inverse = factor_of(gram_of(moments, coefficients))
    proj_ref[0] = proj0_ref[...]
    proj_ref[1] = coefficients[:k]
    fact_ref[0] = fact0_ref[...]
    fact_ref[1] = lower
    even = place()[0] == 0
    before = jnp.concatenate([own_half(q_ref, even, n), own_half(first_ref, even, n)], axis=0)
    rest = own_half(prod_ref, even, n) - dot32(coefficients, before, TN)
    basis_ref[...] = dot32(inverse, rest, NN)


def call(kernel, out_shape, n_in, scratch=(), limit=1 << 20, name=None, far=0, flops=0):
    many = isinstance(out_shape, (tuple, list))
    run = pl.pallas_call(
        kernel,
        out_shape=out_shape,
        in_specs=[pl.BlockSpec(memory_space=pl.ANY) if i < far else VMEM_SPEC for i in range(n_in)],
        out_specs=tuple([VMEM_SPEC] * len(out_shape)) if many else VMEM_SPEC,
        scratch_shapes=list(scratch),
        compiler_params=pltpu.CompilerParams(vmem_limit_bytes=limit),
        cost_estimate=pl.CostEstimate(flops=flops, transcendentals=0, bytes_accessed=flops // 128) if flops else None,
        name=name,
    )
    return lambda *args: run(
        *[pltpu.with_memory_space_constraint(v, pltpu.HBM if i < far else pltpu.VMEM) for i, v in enumerate(args)]
    )


def shape(*dims):
    return jax.ShapeDtypeStruct(dims, F32)


def on_device(n_row, n_col, coupling, energies, block):
    n, k = block.shape
    group = n_row
    order = n * n_row * n_col
    rows = coupling.shape[0] * n
    width = coupling.shape[2]
    axes = ("row", "col")
    flat = [(r, c) for r in range(n_row) for c in range(n_col)]

    def send(value, to):
        pairs = [(r * n_col + c, to(r, c)) for r, c in flat]
        return lax.ppermute(value, axes, [p for p in pairs if p[1] is not None])

    def swap(value):
        return send(value, lambda r, c: r * n_col + (c ^ 1))

    def chip(r, c, s_row, s_z):
        return (r ^ s_row) * n_col + (c ^ (2 * s_z))

    def spread(s):
        def to(r, c):
            along_z = (c % 2 == 0) != (s == group - 1)
            return chip(r, c, 0, s) if along_z else chip(r, c, s, 0)

        return to

    steps = range(1, group)
    tile, parts = 256, 3
    total_pieces = group * parts
    block_shape = shape(rows // parts, 2 * n)
    most = max(len(pieces_of(p, group, n, rows // parts)) for p in range(parts))
    semaphores = lambda count: [pltpu.SemaphoreType.DMA((count, most))]
    work = rows * 2 * n * 256
    a = coupling.reshape(rows, width)
    energy = energies.reshape(1, n)

    other = swap(block.T)
    own, *held = call(
        functools.partial(begin_kernel, k, n, group, parts),
        (shape(k, n), block_shape),
        2,
        scratch=semaphores(1) + [pltpu.SemaphoreType.DMA],
        name="begin",
        far=2,
        flops=work // 4,
    )(a, block.T)
    first = call(functools.partial(order_kernel, k, n), shape(k, 2 * n), 2, name="order")(own, other)

    def products(held, pair, name):
        extra = pair.shape[1] > 2 * n
        sizes = (k, n, group, tile, parts)
        load = len(held) < total_pieces

        def matrix_call(kernel, need, upto, out_shapes, args, scratch, label, flops):
            given = [i for i in need if i < len(held)]
            new = range(len(held), max(upto, len(held)))
            outs = call(
                functools.partial(kernel, *sizes, given, new),
                tuple(out_shapes) + (block_shape,) * len(new),
                (len(new) > 0) + len(given) + len(args),
                scratch=list(scratch) + (semaphores(len(new)) if new else []),
                limit=8 << 20,
                name=name + label,
                far=int(len(new) > 0),
                flops=flops,
            )(*([a] if new else []), *[held[i] for i in given], *args)
            held.extend(outs[len(out_shapes) :])
            return outs[: len(out_shapes)]

        mine = [send(pair, spread(s)) for s in steps]
        (u0,) = matrix_call(
            early_kernel,
            range(parts),
            parts + 2,
            [shape(k, rows)],
            [pair],
            [pltpu.VMEM((2 * k, 2 * n), BF16)],
            "_early",
            2 * work,
        )
        u0, same, *mine = lax.optimization_barrier((u0, pair, *mine))
        theirs = [swap(y) for y in mine]
        (v0,) = matrix_call(
            own_kernel,
            range(parts, parts + group - 1),
            parts + group,
            [shape(k, (group - 1) * 2 * n)],
            [same],
            [pltpu.VMEM((2 * k, n), BF16)],
            "_own",
            work,
        )
        out, keep, mine_u, xr, xg = matrix_call(
            main_kernel,
            range(parts, total_pieces),
            total_pieces,
            [
                shape(group - 1, k, 2 * n),
                shape(group - 1, k, 2 * n),
                shape(k, n),
                jax.ShapeDtypeStruct((2 * k, rows), BF16),
                jax.ShapeDtypeStruct((2 * k, (group - 1) * 2 * n), BF16),
            ],
            [pair, u0, v0, *mine, *theirs],
            [pltpu.VMEM((k, rows), F32), pltpu.VMEM((k, (group - 1) * 2 * n), F32)],
            "",
            8 * work,
        )
        got = swap(out)
        near = call(
            functools.partial(near_kernel, k, n, tile),
            shape(k, 2 * n),
            2,
            limit=8 << 20,
            name=name + "_near",
            flops=work,
        )(held[0], xr)
        got, near = lax.optimization_barrier((got, near))
        sums = call(
            functools.partial(combine_kernel, k, n, group, extra),
            (shape(k, pair.shape[1]),) * (group - 1) + ((shape(k, 8 * k),) if extra else ()),
            2 + (2 * group - 1 if extra else 0),
            name=name + "_combine",
        )(keep, got, *((pair, *mine, *theirs) if extra else ()))
        arrived = [send(sums[s - 1], spread(s)) for s in steps]
        total = call(
            functools.partial(late_kernel, *sizes, extra),
            shape(k, pair.shape[1]),
            parts - 1 + group - 1 + 6 + extra,
            scratch=[pltpu.VMEM((k, 2 * n), F32), pltpu.VMEM((k, n), F32)],
            limit=8 << 20,
            name=name + "_late",
            flops=3 * work,
        )(*held[1 : parts + group - 1], xr, xg, near, mine_u, pair, energy, *sums[group - 1 :])
        for v in arrived:
            total = total + v
        return total, swap(total), held

    mine, got, held = products(held, first, "first")
    pair = call(functools.partial(pair_kernel, k, n), shape(k, 2 * n + 8 * k), 3, name="pair")(first, mine, got)
    mine, got, held = products(held, pair, "second")
    q, prod, moments, proj0, fact0 = call(
        functools.partial(second_kernel, k, n, order),
        (shape(k, 2 * n), shape(k, 2 * n), shape(3 * k, 3 * k), shape(k, k), shape(k, k)),
        4,
        name="middle",
    )(first, pair, mine, got)
    moments = sum([send(moments, lambda r, c, s=s: chip(r, c, s, 0)) for s in steps], moments)
    sums = [moments] + [send(moments, lambda r, c, s=s: chip(r, c, 0, s)) for s in steps]
    basis, proj, fact = call(
        functools.partial(last_kernel, k, n, order),
        (shape(k, n), shape(2, k, k), shape(2, k, k)),
        5 + group,
        name="last",
    )(first, q, prod, proj0, fact0, *sums)
    return basis.T, proj, fact


def solution(mesh):
    n_row, n_col = mesh.shape["row"], mesh.shape["col"]

    def body(coupling, energies, block):
        n, k = block.shape
        paired = n_col == 2 * n_row and n_row & (n_row - 1) == 0 and n_row > 1
        divides = coupling.shape[0] * n % 768 == 0
        whole = divides and n % 64 == 0 and n >= 256 and 8 * k == 128 and coupling.shape[2] == coupling.shape[0] * n * 2
        small = coupling.size * 4 <= 44 << 20
        if paired and whole and small:
            return on_device(n_row, n_col, coupling, energies, block)
        return generic(coupling, energies, block)

    placed = (P(None, "col", "row"), P(("row", "col")), P(("row", "col"), None))
    return jax.shard_map(
        body,
        mesh=mesh,
        in_specs=placed,
        out_specs=(P(("row", "col"), None), P(), P()),
        check_vma=False,
    )
```

```python
import functools

import jax
import jax.numpy as jnp
from jax import lax
from jax.experimental import pallas as pl
from jax.experimental.pallas import tpu as pltpu
from jax.sharding import PartitionSpec as P

ITERS = 2
F32 = jnp.float32
BF16 = jnp.bfloat16

precise = lax.Precision.HIGHEST

NN = (((1,), (0,)), ((), ()))
NT = (((1,), (1,)), ((), ()))
TN = (((0,), (0,)), ((), ()))

VMEM_SPEC = pl.BlockSpec(memory_space=pltpu.VMEM)


def generic(coupling, energies, block):
    order = block.shape[0] * lax.axis_size("row") * lax.axis_size("col")
    segment = block.shape[0]
    width = block.shape[1]
    column = lax.axis_index("col")
    current, energy_rows = (
        lax.all_gather(block, "col", axis=0, tiled=True),
        lax.all_gather(energies, "col", axis=0, tiled=True),
    )
    prior = jnp.zeros_like(current)
    projection_list = []
    factor_list = []
    for section in range(ITERS):
        own_rows = lax.dynamic_slice_in_dim(current, column * segment, segment, 0)
        spread = lax.all_gather(own_rows, "row", axis=0, tiled=True)
        spread = spread.reshape(coupling.shape[0], segment, width)
        direct = lax.psum_scatter(
            jnp.einsum("aig,gk->aik", coupling, current, precision=precise),
            "row",
            scatter_dimension=0,
            tiled=True,
        ).reshape(segment, width)
        partial_value = jnp.einsum("aig,aik->gk", coupling, spread, precision=precise)
        transposed = lax.psum(partial_value, "col")
        direct_rows = lax.all_gather(direct, "col", axis=0, tiled=True)
        product = energy_rows[:, None] * current + direct_rows + transposed
        stacked = jnp.concatenate([current, prior, product], axis=1)
        moments = lax.psum(jnp.einsum("nk,nl->kl", stacked, stacked, precision=precise), "row") / order
        projection = moments[:width, 2 * width :]
        cross = moments[width : 2 * width, 2 * width :]
        weights = jnp.concatenate([-projection, -cross, jnp.eye(width, dtype=F32)], axis=0)
        gram_matrix = jnp.dot(weights.T, jnp.dot(moments, weights, precision=precise), precision=precise)
        factor = jnp.linalg.cholesky(gram_matrix)
        residual = (
            product
            - jnp.dot(current, projection, precision=precise)
            - jnp.dot(prior, cross, precision=precise)
        )
        prior = current
        current = jax.scipy.linalg.solve_triangular(factor, residual.T, lower=True).T
        projection_list.append(projection)
        factor_list.append(factor)
    basis = lax.dynamic_slice_in_dim(current, column * segment, segment, 0)
    return (basis, jnp.stack(projection_list), jnp.stack(factor_list))


def place():
    column = lax.axis_index("col")
    return lax.rem(column, 2), lax.div(column, 2), lax.axis_index("row")


def split(value):
    high = value.astype(BF16)
    return high, (value - high.astype(F32)).astype(BF16)


def dot(left, right, dims):
    return lax.dot_general(left, right, dims, preferred_element_type=F32)


def dot32(left, right, dims):
    return lax.dot_general(left, right, dims, preferred_element_type=F32, precision=precise)


def own_half(value, even, n):
    return jnp.where(even, value[:, :n], value[:, n : 2 * n])


def in_half(value, even):
    zero = jnp.zeros_like(value)
    return jnp.concatenate([jnp.where(even, value, zero), jnp.where(even, zero, value)], axis=1)


def pieces_of(part, group, n, rows):
    found, at, end = [], part * rows, (part + 1) * rows
    while at < end:
        s, off = divmod(at, n)
        count = min(n - off, end - at)
        found.append((s, off, at - part * rows, count))
        at += count
    return found


def order_of(group, parts):
    near = [(0, p) for p in range(parts)]
    lead = [(s, 0) for s in range(1, group)]
    return near + lead + [(s, p) for s in range(1, group) for p in range(1, parts)]


class Loader:
    def __init__(self, source, arrived, n, group, parts, where, held):
        _, z, r = place()

        def copies(i):
            s, part = where[i]
            cols = pl.ds(pl.multiple_of(lax.bitwise_xor(z, s) * (2 * n), 128), 2 * n)
            return [
                pltpu.make_async_copy(
                    source.at[pl.ds(pl.multiple_of(lax.bitwise_xor(r, peer) * n + off, 8), count), cols],
                    held[i].at[pl.ds(at, count), :],
                    arrived.at[i, j],
                )
                for j, (peer, off, at, count) in enumerate(pieces_of(part, group, n, group * n // parts))
            ]

        self.copies = copies
        for i in range(len(held)):
            for copy in copies(i):
                copy.start()

    def wait(self, i):
        for copy in self.copies(i):
            copy.wait()


class Pieces:
    def __init__(self, n, group, parts, given, new, scratch, refs):
        order = order_of(group, parts)
        refs = list(refs)
        source = refs.pop(0) if len(new) else None
        held = {order[i]: refs.pop(0) for i in given}
        self.waits = {}
        if len(new):
            arrived = refs.pop()
            at = len(refs) - scratch - len(new)
            fresh, refs = refs[at : at + len(new)], refs[:at] + refs[at + len(new) :]
            where = [order[i] for i in new]
            self.loader = Loader(source, arrived, n, group, parts, where, fresh)
            self.waits = {key: i for i, key in enumerate(where)}
            held.update(zip(where, fresh))
        self.held, self.refs = held, refs

    def get(self, s, p):
        if (s, p) in self.waits:
            self.loader.wait(self.waits.pop((s, p)))
        return self.held[s, p]

    def finish(self):
        for key in list(self.waits):
            self.get(*key)


def rows_at(start, tile):
    return slice(start, start + tile) if isinstance(start, int) else pl.ds(pl.multiple_of(start, tile), tile)


def tiles_of(piece, tile, first, last, step, loop=False):
    def body(t, carry):
        high, low = split(piece[rows_at(t * tile, tile), :])
        step(t, high, low)
        return carry

    if loop:
        lax.fori_loop(first, last, body, 0)
    else:
        for t in range(first, last):
            body(t, 0)


def across(xg, cols, k, high, low):
    one = dot(xg[:, cols], high, NT)
    two = dot(xg[:k, cols], low, NT)
    return one[:k] + one[k:] + two


def along(xr, at, k, high, low):
    one = dot(xr[:, at], high, NN)
    two = dot(xr[:k, at], low, NN)
    return one[:k] + one[k:] + two


def begin_kernel(k, n, group, parts, source, block_ref, own_ref, *refs):
    *held, arrived, ready = refs
    copy = pltpu.make_async_copy(block_ref, own_ref, ready)
    copy.start()
    loader = Loader(source, arrived, n, group, parts, order_of(group, parts), held)
    copy.wait()
    for i in range(len(held)):
        loader.wait(i)


def order_kernel(k, n, own_ref, other_ref, *outs):
    even = place()[0] == 0
    own, other = own_ref[...], other_ref[...]
    for out in outs:
        out[...] = jnp.concatenate([jnp.where(even, own, other), jnp.where(even, other, own)], axis=1)


def put(slab, at, k, value):
    high, low = split(value)
    slab[:k, at : at + value.shape[1]] = high
    slab[k:, at : at + value.shape[1]] = low


def turned(s, group, even):
    return jnp.logical_not(even) if s == group - 1 else even


def early_kernel(k, n, group, tile, parts, given, new, *refs):
    pieces = Pieces(n, group, parts, given, new, 1, refs)
    xg = pieces.refs.pop(-1)
    pair_ref, u_ref = pieces.refs
    put(xg, 0, k, pair_ref[:, : 2 * n])
    for p in range(parts):
        piece = pieces.get(0, p)
        rows = piece.shape[0]

        def step(t, high, low):
            u_ref[:, rows_at(p * rows + t * tile, tile)] = across(xg, slice(None), k, high, low)

        tiles_of(piece, tile, 0, rows // tile, step, len(new) > 0)
    pieces.finish()


def own_kernel(k, n, group, tile, parts, given, new, *refs):
    pieces = Pieces(n, group, parts, given, new, 1, refs)
    xr = pieces.refs.pop(-1)
    pair_ref, v_ref = pieces.refs
    even = place()[0] == 0
    put(xr, 0, k, own_half(pair_ref, even, n))
    v_ref[...] = jnp.zeros_like(v_ref)
    for s in range(1, group):
        cols = slice((s - 1) * 2 * n, s * 2 * n)

        def step(t, high, low):
            v_ref[:, cols] += along(xr, rows_at(t * tile, tile), k, high, low)

        tiles_of(pieces.get(s, 0), tile, 0, n // tile, step, len(new) > 0)
    pieces.finish()


def main_kernel(k, n, group, tile, parts, given, new, *refs):
    pieces = Pieces(n, group, parts, given, new, 2, refs)
    u_acc, v_acc = pieces.refs[-2:]
    refs = pieces.refs[:-2]
    pair_ref, u0_ref, v0_ref, mine, theirs = refs[0], refs[1], refs[2], refs[3 : group + 2], refs[group + 2 : 2 * group + 1]
    send_ref, keep_ref, own_ref, xr, xg = refs[2 * group + 1 :]
    even = place()[0] == 0

    segments = [own_half(pair_ref, even, n)]
    for s in range(1, group):
        y, w = mine[s - 1][:, : 2 * n], theirs[s - 1][:, : 2 * n]
        to_z = turned(s, group, even)
        put(xg, (s - 1) * 2 * n, k, jnp.where(to_z, y, w))
        segments.append(own_half(jnp.where(to_z, w, y), even, n))
    for a in range(0, group, 2):
        put(xr, a * n, k, jnp.concatenate(segments[a : a + 2], axis=1))
    u_acc[...] = u0_ref[...]
    v_acc[...] = v0_ref[...]

    for s, p in order_of(group, parts)[parts:]:
        piece = pieces.get(s, p)
        rows = piece.shape[0]
        cols = slice((s - 1) * 2 * n, s * 2 * n)

        def step(t, high, low):
            at = rows_at(p * rows + t * tile, tile)
            v_acc[:, cols] += along(xr, at, k, high, low)
            u_acc[:, at] += across(xg, cols, k, high, low)

        tiles_of(piece, tile, n // tile if p == 0 else 0, rows // tile, step, len(new) > 0)

    own_ref[...] = u_acc[:, :n]
    for s in range(1, group):
        to_z = turned(s, group, even)
        by_z = v_acc[:, 2 * n * (s - 1) : 2 * n * s]
        by_row = in_half(u_acc[:, n * s : n * (s + 1)], even)
        keep_ref[s - 1] = jnp.where(to_z, by_z, by_row)
        send_ref[s - 1] = jnp.where(to_z, by_row, by_z)


def near_kernel(k, n, tile, piece, xr, v_ref):
    v_ref[...] = jnp.zeros_like(v_ref)

    def step(t, high, low):
        v_ref[...] += along(xr, rows_at(t * tile, tile), k, high, low)

    tiles_of(piece, tile, 0, piece.shape[0] // tile, step)


def late_kernel(k, n, group, tile, parts, extra, *refs):
    near, lead, refs = refs[: parts - 1], refs[parts - 1 : parts + group - 2], refs[parts + group - 2 :]
    xr, xg, v_ref, own_ref, pair_ref, energy_ref, *refs = refs
    more, refs = (refs[0], refs[1:]) if extra else (None, refs)
    out_ref, v_acc, u_acc = refs
    even = place()[0] == 0
    v_acc[...] = v_ref[...]
    u_acc[...] = own_ref[...]
    rows = near[0].shape[0]
    down = [(p, t) for p in range(1, parts) for t in range(rows // tile)]
    over = [(s, t) for s in range(1, group) for t in range(n // tile)]
    for i in range(max(len(down), len(over))):
        if i < len(down):
            p, t = down[i]
            high, low = split(near[p - 1][t * tile : (t + 1) * tile, :])
            v_acc[...] += along(xr, rows_at(p * rows + t * tile, tile), k, high, low)
        if i < len(over):
            s, t = over[i]
            high, low = split(lead[s - 1][t * tile : (t + 1) * tile, :])
            cols = slice((s - 1) * 2 * n, s * 2 * n)
            u_acc[:, t * tile : (t + 1) * tile] += across(xg, cols, k, high, low)
    own = energy_ref[...] * own_half(pair_ref, even, n) + u_acc[...]
    out_ref[:, : 2 * n] = v_acc[...] + in_half(own, even)
    if extra:
        part = more[...]
        out_ref[:, 2 * n :] = jnp.where(even, part, jnp.zeros_like(part))


def combine_kernel(k, n, group, extra, keep_ref, got_ref, *refs):
    even = place()[0] == 0
    if extra:
        pair_ref, mine, theirs, outs = refs[0], refs[1:group], refs[group : 2 * group - 1], refs[2 * group - 1 :]
        part = pair_ref[:, 2 * n :]
        for s in range(1, group):
            to_z = turned(s, group, even)
            part = part + jnp.where(to_z, theirs[s - 1][:, 2 * n :], mine[s - 1][:, 2 * n :])
        outs[group - 1][...] = part
    else:
        outs = refs
    for s in range(1, group):
        outs[s - 1][:, : 2 * n] = keep_ref[s - 1] + got_ref[s - 1]
        if extra:
            outs[s - 1][:, 2 * n :] = jnp.where(turned(s, group, even), part, jnp.zeros_like(part))


def pair_kernel(k, n, first_ref, mine_ref, got_ref, *outs):
    value = mine_ref[...] + got_ref[...]
    s = jnp.concatenate([first_ref[...], value], axis=0)
    moments = dot32(s, s, NT)
    for out in outs:
        out[:, : 2 * n] = value
        out[:, 2 * n :] = jnp.zeros((k, 8 * k), F32)
        out[:, 2 * n : 2 * n + 2 * k] = moments[:k]
        out[:, 2 * n + 2 * k : 2 * n + 4 * k] = moments[k:]


def factor_of(gram):
    k = gram.shape[0]
    rows = lax.broadcasted_iota(jnp.int32, (k, 2 * k), 0)
    cols = lax.broadcasted_iota(jnp.int32, (k, 2 * k), 1)
    row = lax.broadcasted_iota(jnp.int32, (k, 1), 0)
    both = jnp.concatenate([gram, eye(k)], axis=1)
    for j in range(k - 1):
        lead = both[j : j + 1, :]
        lead = lead * (1.0 / both[j : j + 1, j : j + 1])
        both = both - jnp.where(row > j, both[:, j : j + 1], 0.0) * lead
    pivots = jnp.sum(jnp.where(rows == cols, both, 0.0), axis=1, keepdims=True)
    both = both * (1.0 / jnp.sqrt(pivots))
    upper = jnp.where(rows <= cols, both, 0.0)[:, :k]
    return dot32(upper, eye(k), TN), both[:, k:]


def gram_of(moments, coefficients):
    k = moments.shape[0]
    w = coefficients.shape[1]
    parts = jnp.concatenate([-coefficients, eye(w)], axis=0)
    return dot32(parts, dot32(moments, parts, NN), TN)


def eye(k):
    return jnp.where(
        lax.broadcasted_iota(jnp.int32, (k, k), 0) == lax.broadcasted_iota(jnp.int32, (k, k), 1), 1.0, 0.0
    ).astype(F32)


def second_kernel(k, n, order, first_ref, pair_ref, mine_ref, got_ref, q_ref, prod_ref, proj_ref, fact_ref, *outs):
    packed = mine_ref[:, 2 * n :] + got_ref[:, 2 * n :]
    moments = jnp.concatenate([packed[:, : 2 * k], packed[:, 2 * k : 4 * k]], axis=0) * (1.0 / order)
    projection = moments[:k, k:]
    lower, inverse = factor_of(gram_of(moments, projection))
    proj_ref[...] = projection
    fact_ref[...] = lower
    x, y = first_ref[...], pair_ref[:, : 2 * n]
    w = mine_ref[:, : 2 * n] + got_ref[:, : 2 * n]
    rest = jnp.concatenate([y, w], axis=1) - dot32(projection, jnp.concatenate([x, y], axis=1), TN)
    both = dot32(inverse, rest, NN)
    q, prod = both[:, : 2 * n], both[:, 2 * n :]
    q_ref[...] = q
    prod_ref[...] = prod
    s = jnp.concatenate([q, x, prod], axis=0)
    total = dot32(s, s, NT)
    for out in outs:
        out[...] = total


def sum_kernel(*refs):
    count = (len(refs) + 1) // 2
    total = refs[0][...]
    for m in refs[1:count]:
        total = total + m[...]
    for out in refs[count:]:
        out[...] = total


def last_kernel(k, n, order, first_ref, q_ref, prod_ref, proj0_ref, fact0_ref, *refs):
    *sums, basis_ref, proj_ref, fact_ref = refs
    total = sums[0][...]
    for m in sums[1:]:
        total = total + m[...]
    moments = total * (1.0 / order)
    coefficients = moments[: 2 * k, 2 * k :]
    lower, inverse = factor_of(gram_of(moments, coefficients))
    proj_ref[0] = proj0_ref[...]
    proj_ref[1] = coefficients[:k]
    fact_ref[0] = fact0_ref[...]
    fact_ref[1] = lower
    even = place()[0] == 0
    before = jnp.concatenate([own_half(q_ref, even, n), own_half(first_ref, even, n)], axis=0)
    rest = own_half(prod_ref, even, n) - dot32(coefficients, before, TN)
    basis_ref[...] = dot32(inverse, rest, NN)


def call(kernel, out_shape, n_in, scratch=(), limit=1 << 20, name=None, far=0, flops=0):
    many = isinstance(out_shape, (tuple, list))
    run = pl.pallas_call(
        kernel,
        out_shape=out_shape,
        in_specs=[pl.BlockSpec(memory_space=pl.ANY) if i < far else VMEM_SPEC for i in range(n_in)],
        out_specs=tuple([VMEM_SPEC] * len(out_shape)) if many else VMEM_SPEC,
        scratch_shapes=list(scratch),
        compiler_params=pltpu.CompilerParams(vmem_limit_bytes=limit),
        cost_estimate=pl.CostEstimate(flops=flops, transcendentals=0, bytes_accessed=flops // 128) if flops else None,
        name=name,
    )
    return lambda *args: run(
        *[pltpu.with_memory_space_constraint(v, pltpu.HBM if i < far else pltpu.VMEM) for i, v in enumerate(args)]
    )


def shape(*dims):
    return jax.ShapeDtypeStruct(dims, F32)


def on_device(n_row, n_col, coupling, energies, block):
    n, k = block.shape
    group = n_row
    order = n * n_row * n_col
    rows = coupling.shape[0] * n
    width = coupling.shape[2]
    axes = ("row", "col")
    flat = [(r, c) for r in range(n_row) for c in range(n_col)]

    def send(value, to):
        pairs = [(r * n_col + c, to(r, c)) for r, c in flat]
        return lax.ppermute(value, axes, [p for p in pairs if p[1] is not None])

    def swap(value):
        return send(value, lambda r, c: r * n_col + (c ^ 1))

    def chip(r, c, s_row, s_z):
        return (r ^ s_row) * n_col + (c ^ (2 * s_z))

    def spread(s):
        def to(r, c):
            along_z = (c % 2 == 0) != (s == group - 1)
            return chip(r, c, 0, s) if along_z else chip(r, c, s, 0)

        return to

    steps = range(1, group)
    tile, parts = 256, 3
    total_pieces = group * parts
    block_shape = shape(rows // parts, 2 * n)
    most = max(len(pieces_of(p, group, n, rows // parts)) for p in range(parts))
    semaphores = lambda count: [pltpu.SemaphoreType.DMA((count, most))]
    work = rows * 2 * n * 256
    a = coupling.reshape(rows, width)
    energy = energies.reshape(1, n)

    other = swap(block.T)
    own, *held = call(
        functools.partial(begin_kernel, k, n, group, parts),
        (shape(k, n), block_shape),
        2,
        scratch=semaphores(1) + [pltpu.SemaphoreType.DMA],
        name="begin",
        far=2,
        flops=work // 4,
    )(a, block.T)
    firsts = call(functools.partial(order_kernel, k, n), (shape(k, 2 * n),) * (group - 1), 2, name="order")(own, other)
    first = firsts[0]

    def products(held, copies, name):
        pair = copies[0]
        extra = pair.shape[1] > 2 * n
        sizes = (k, n, group, tile, parts)
        load = len(held) < total_pieces

        def matrix_call(kernel, need, upto, out_shapes, args, scratch, label, flops):
            given = [i for i in need if i < len(held)]
            new = range(len(held), max(upto, len(held)))
            outs = call(
                functools.partial(kernel, *sizes, given, new),
                tuple(out_shapes) + (block_shape,) * len(new),
                (len(new) > 0) + len(given) + len(args),
                scratch=list(scratch) + (semaphores(len(new)) if new else []),
                limit=8 << 20,
                name=name + label,
                far=int(len(new) > 0),
                flops=flops,
            )(*([a] if new else []), *[held[i] for i in given], *args)
            held.extend(outs[len(out_shapes) :])
            return outs[: len(out_shapes)]

        mine = [send(copies[s - 1], spread(s)) for s in steps]
        (u0,) = matrix_call(
            early_kernel,
            range(parts),
            parts + 2,
            [shape(k, rows)],
            [pair],
            [pltpu.VMEM((2 * k, 2 * n), BF16)],
            "_early",
            2 * work,
        )
        u0, same, *mine = lax.optimization_barrier((u0, pair, *mine))
        theirs = [swap(y) for y in mine]
        (v0,) = matrix_call(
            own_kernel,
            range(parts, parts + group - 1),
            parts + group,
            [shape(k, (group - 1) * 2 * n)],
            [same],
            [pltpu.VMEM((2 * k, n), BF16)],
            "_own",
            work,
        )
        out, keep, mine_u, xr, xg = matrix_call(
            main_kernel,
            range(parts, total_pieces),
            total_pieces,
            [
                shape(group - 1, k, 2 * n),
                shape(group - 1, k, 2 * n),
                shape(k, n),
                jax.ShapeDtypeStruct((2 * k, rows), BF16),
                jax.ShapeDtypeStruct((2 * k, (group - 1) * 2 * n), BF16),
            ],
            [pair, u0, v0, *mine, *theirs],
            [pltpu.VMEM((k, rows), F32), pltpu.VMEM((k, (group - 1) * 2 * n), F32)],
            "",
            8 * work,
        )
        got = swap(out)
        near = call(
            functools.partial(near_kernel, k, n, tile),
            shape(k, 2 * n),
            2,
            limit=8 << 20,
            name=name + "_near",
            flops=work,
        )(held[0], xr)
        got, near = lax.optimization_barrier((got, near))
        sums = call(
            functools.partial(combine_kernel, k, n, group, extra),
            (shape(k, pair.shape[1]),) * (group - 1) + ((shape(k, 8 * k),) if extra else ()),
            2 + (2 * group - 1 if extra else 0),
            name=name + "_combine",
        )(keep, got, *((pair, *mine, *theirs) if extra else ()))
        arrived = [send(sums[s - 1], spread(s)) for s in steps]
        total = call(
            functools.partial(late_kernel, *sizes, extra),
            shape(k, pair.shape[1]),
            parts - 1 + group - 1 + 6 + extra,
            scratch=[pltpu.VMEM((k, 2 * n), F32), pltpu.VMEM((k, n), F32)],
            limit=8 << 20,
            name=name + "_late",
            flops=3 * work,
        )(*held[1 : parts + group - 1], xr, xg, near, mine_u, pair, energy, *sums[group - 1 :])
        for v in arrived:
            total = total + v
        return total, swap(total), held

    mine, got, held = products(held, firsts, "first")
    pairs = call(functools.partial(pair_kernel, k, n), (shape(k, 2 * n + 8 * k),) * (group - 1), 3, name="pair")(
        first, mine, got
    )
    pair = pairs[0]
    mine, got, held = products(held, pairs, "second")
    q, prod, proj0, fact0, *moments = call(
        functools.partial(second_kernel, k, n, order),
        (shape(k, 2 * n), shape(k, 2 * n), shape(k, k), shape(k, k)) + (shape(3 * k, 3 * k),) * (group - 1),
        4,
        name="middle",
    )(first, pair, mine, got)
    sums = [moments[0]] + [send(moments[s - 1], lambda r, c, s=s: chip(r, c, s, 0)) for s in steps]
    moments = call(sum_kernel, (shape(3 * k, 3 * k),) * (group - 1), group, name="sum")(*sums)
    sums = [moments[0]] + [send(moments[s - 1], lambda r, c, s=s: chip(r, c, 0, s)) for s in steps]
    basis, proj, fact = call(
        functools.partial(last_kernel, k, n, order),
        (shape(k, n), shape(2, k, k), shape(2, k, k)),
        5 + group,
        name="last",
    )(first, q, prod, proj0, fact0, *sums)
    return basis.T, proj, fact


def solution(mesh):
    n_row, n_col = mesh.shape["row"], mesh.shape["col"]

    def body(coupling, energies, block):
        n, k = block.shape
        paired = n_col == 2 * n_row and n_row & (n_row - 1) == 0 and n_row > 1
        divides = coupling.shape[0] * n % 768 == 0
        whole = divides and n % 64 == 0 and n >= 256 and 8 * k == 128 and coupling.shape[2] == coupling.shape[0] * n * 2
        small = coupling.size * 4 <= 44 << 20
        if paired and whole and small:
            return on_device(n_row, n_col, coupling, energies, block)
        return generic(coupling, energies, block)

    placed = (P(None, "col", "row"), P(("row", "col")), P(("row", "col"), None))
    return jax.shard_map(
        body,
        mesh=mesh,
        in_specs=placed,
        out_specs=(P(("row", "col"), None), P(), P()),
        check_vma=False,
    )
```

```python
import functools

import jax
import jax.numpy as jnp
from jax import lax
from jax.experimental import pallas as pl
from jax.experimental.pallas import tpu as pltpu
from jax.sharding import PartitionSpec as P

ITERS = 2
F32 = jnp.float32
BF16 = jnp.bfloat16

precise = lax.Precision.HIGHEST

NN = (((1,), (0,)), ((), ()))
NT = (((1,), (1,)), ((), ()))
TN = (((0,), (0,)), ((), ()))

VMEM_SPEC = pl.BlockSpec(memory_space=pltpu.VMEM)


def generic(coupling, energies, block):
    order = block.shape[0] * lax.axis_size("row") * lax.axis_size("col")
    segment = block.shape[0]
    width = block.shape[1]
    column = lax.axis_index("col")
    current, energy_rows = (
        lax.all_gather(block, "col", axis=0, tiled=True),
        lax.all_gather(energies, "col", axis=0, tiled=True),
    )
    prior = jnp.zeros_like(current)
    projection_list = []
    factor_list = []
    for section in range(ITERS):
        own_rows = lax.dynamic_slice_in_dim(current, column * segment, segment, 0)
        spread = lax.all_gather(own_rows, "row", axis=0, tiled=True)
        spread = spread.reshape(coupling.shape[0], segment, width)
        direct = lax.psum_scatter(
            jnp.einsum("aig,gk->aik", coupling, current, precision=precise),
            "row",
            scatter_dimension=0,
            tiled=True,
        ).reshape(segment, width)
        partial_value = jnp.einsum("aig,aik->gk", coupling, spread, precision=precise)
        transposed = lax.psum(partial_value, "col")
        direct_rows = lax.all_gather(direct, "col", axis=0, tiled=True)
        product = energy_rows[:, None] * current + direct_rows + transposed
        stacked = jnp.concatenate([current, prior, product], axis=1)
        moments = lax.psum(jnp.einsum("nk,nl->kl", stacked, stacked, precision=precise), "row") / order
        projection = moments[:width, 2 * width :]
        cross = moments[width : 2 * width, 2 * width :]
        weights = jnp.concatenate([-projection, -cross, jnp.eye(width, dtype=F32)], axis=0)
        gram_matrix = jnp.dot(weights.T, jnp.dot(moments, weights, precision=precise), precision=precise)
        factor = jnp.linalg.cholesky(gram_matrix)
        residual = (
            product
            - jnp.dot(current, projection, precision=precise)
            - jnp.dot(prior, cross, precision=precise)
        )
        prior = current
        current = jax.scipy.linalg.solve_triangular(factor, residual.T, lower=True).T
        projection_list.append(projection)
        factor_list.append(factor)
    basis = lax.dynamic_slice_in_dim(current, column * segment, segment, 0)
    return (basis, jnp.stack(projection_list), jnp.stack(factor_list))


def place():
    column = lax.axis_index("col")
    return lax.rem(column, 2), lax.div(column, 2), lax.axis_index("row")


def split(value):
    high = value.astype(BF16)
    return high, (value - high.astype(F32)).astype(BF16)


def dot(left, right, dims):
    return lax.dot_general(left, right, dims, preferred_element_type=F32)


def dot32(left, right, dims):
    return lax.dot_general(left, right, dims, preferred_element_type=F32, precision=precise)


def own_half(value, even, n):
    return jnp.where(even, value[:, :n], value[:, n : 2 * n])


def in_half(value, even):
    zero = jnp.zeros_like(value)
    return jnp.concatenate([jnp.where(even, value, zero), jnp.where(even, zero, value)], axis=1)


def pieces_of(part, group, n, rows):
    found, at, end = [], part * rows, (part + 1) * rows
    while at < end:
        s, off = divmod(at, n)
        count = min(n - off, end - at)
        found.append((s, off, at - part * rows, count))
        at += count
    return found


def order_of(group, parts):
    near = [(0, p) for p in range(parts)]
    lead = [(s, 0) for s in range(1, group)]
    return near + lead + [(s, p) for s in range(1, group) for p in range(1, parts)]


class Loader:
    def __init__(self, source, arrived, n, group, parts, where, held):
        _, z, r = place()

        def copies(i):
            s, part = where[i]
            cols = pl.ds(pl.multiple_of(lax.bitwise_xor(z, s) * (2 * n), 128), 2 * n)
            return [
                pltpu.make_async_copy(
                    source.at[pl.ds(pl.multiple_of(lax.bitwise_xor(r, peer) * n + off, 8), count), cols],
                    held[i].at[pl.ds(at, count), :],
                    arrived.at[i, j],
                )
                for j, (peer, off, at, count) in enumerate(pieces_of(part, group, n, group * n // parts))
            ]

        self.copies = copies
        for i in range(len(held)):
            for copy in copies(i):
                copy.start()

    def wait(self, i):
        for copy in self.copies(i):
            copy.wait()


class Pieces:
    def __init__(self, n, group, parts, given, new, scratch, refs):
        order = order_of(group, parts)
        refs = list(refs)
        source = refs.pop(0) if len(new) else None
        held = {order[i]: refs.pop(0) for i in given}
        self.waits = {}
        if len(new):
            arrived = refs.pop()
            at = len(refs) - scratch - len(new)
            fresh, refs = refs[at : at + len(new)], refs[:at] + refs[at + len(new) :]
            where = [order[i] for i in new]
            self.loader = Loader(source, arrived, n, group, parts, where, fresh)
            self.waits = {key: i for i, key in enumerate(where)}
            held.update(zip(where, fresh))
        self.held, self.refs = held, refs

    def get(self, s, p):
        if (s, p) in self.waits:
            self.loader.wait(self.waits.pop((s, p)))
        return self.held[s, p]

    def finish(self):
        for key in list(self.waits):
            self.get(*key)


def rows_at(start, tile):
    return slice(start, start + tile) if isinstance(start, int) else pl.ds(pl.multiple_of(start, tile), tile)


def tiles_of(piece, tile, first, last, step, loop=False):
    def body(t, carry):
        high, low = split(piece[rows_at(t * tile, tile), :])
        step(t, high, low)
        return carry

    if loop:
        lax.fori_loop(first, last, body, 0)
    else:
        for t in range(first, last):
            body(t, 0)


def across(xg, cols, k, high, low):
    one = dot(xg[:, cols], high, NT)
    two = dot(xg[:k, cols], low, NT)
    return one[:k] + one[k:] + two


def along(xr, at, k, high, low):
    one = dot(xr[:, at], high, NN)
    two = dot(xr[:k, at], low, NN)
    return one[:k] + one[k:] + two


def begin_kernel(k, n, group, parts, source, block_ref, own_ref, *refs):
    *held, arrived, ready = refs
    copy = pltpu.make_async_copy(block_ref, own_ref, ready)
    copy.start()
    loader = Loader(source, arrived, n, group, parts, order_of(group, parts), held)
    copy.wait()
    for i in range(len(held)):
        loader.wait(i)


def order_kernel(k, n, own_ref, other_ref, *outs):
    even = place()[0] == 0
    own, other = own_ref[...], other_ref[...]
    for out in outs:
        out[...] = jnp.concatenate([jnp.where(even, own, other), jnp.where(even, other, own)], axis=1)


def put(slab, at, k, value):
    high, low = split(value)
    slab[:k, at : at + value.shape[1]] = high
    slab[k:, at : at + value.shape[1]] = low


def turned(s, group, even):
    return jnp.logical_not(even) if s >= group // 2 else even


def early_kernel(k, n, group, tile, parts, given, new, *refs):
    pieces = Pieces(n, group, parts, given, new, 1, refs)
    xg = pieces.refs.pop(-1)
    pair_ref, u_ref = pieces.refs
    put(xg, 0, k, pair_ref[:, : 2 * n])
    for p in range(parts):
        piece = pieces.get(0, p)
        rows = piece.shape[0]

        def step(t, high, low):
            u_ref[:, rows_at(p * rows + t * tile, tile)] = across(xg, slice(None), k, high, low)

        tiles_of(piece, tile, 0, rows // tile, step, len(new) > 0)
    pieces.finish()


def own_kernel(k, n, group, tile, parts, given, new, *refs):
    pieces = Pieces(n, group, parts, given, new, 1, refs)
    xr = pieces.refs.pop(-1)
    pair_ref, v_ref = pieces.refs
    even = place()[0] == 0
    put(xr, 0, k, own_half(pair_ref, even, n))
    v_ref[...] = jnp.zeros_like(v_ref)
    for s in range(1, group):
        cols = slice((s - 1) * 2 * n, s * 2 * n)

        def step(t, high, low):
            v_ref[:, cols] += along(xr, rows_at(t * tile, tile), k, high, low)

        tiles_of(pieces.get(s, 0), tile, 0, n // tile, step, len(new) > 0)
    pieces.finish()


def main_kernel(k, n, group, tile, parts, given, new, *refs):
    pieces = Pieces(n, group, parts, given, new, 2, refs)
    u_acc, v_acc = pieces.refs[-2:]
    refs = pieces.refs[:-2]
    pair_ref, u0_ref, v0_ref, mine, theirs = refs[0], refs[1], refs[2], refs[3 : group + 2], refs[group + 2 : 2 * group + 1]
    send_ref, keep_ref, own_ref, xr, xg = refs[2 * group + 1 :]
    even = place()[0] == 0

    segments = [own_half(pair_ref, even, n)]
    for s in range(1, group):
        y, w = mine[s - 1][:, : 2 * n], theirs[s - 1][:, : 2 * n]
        to_z = turned(s, group, even)
        put(xg, (s - 1) * 2 * n, k, jnp.where(to_z, y, w))
        segments.append(own_half(jnp.where(to_z, w, y), even, n))
    for a in range(0, group, 2):
        put(xr, a * n, k, jnp.concatenate(segments[a : a + 2], axis=1))
    u_acc[...] = u0_ref[...]
    v_acc[...] = v0_ref[...]

    for s, p in order_of(group, parts)[parts:]:
        piece = pieces.get(s, p)
        rows = piece.shape[0]
        cols = slice((s - 1) * 2 * n, s * 2 * n)

        def step(t, high, low):
            at = rows_at(p * rows + t * tile, tile)
            v_acc[:, cols] += along(xr, at, k, high, low)
            u_acc[:, at] += across(xg, cols, k, high, low)

        tiles_of(piece, tile, n // tile if p == 0 else 0, rows // tile, step, len(new) > 0)

    own_ref[...] = u_acc[:, :n]
    for s in range(1, group):
        to_z = turned(s, group, even)
        by_z = v_acc[:, 2 * n * (s - 1) : 2 * n * s]
        by_row = in_half(u_acc[:, n * s : n * (s + 1)], even)
        keep_ref[s - 1] = jnp.where(to_z, by_z, by_row)
        send_ref[s - 1] = jnp.where(to_z, by_row, by_z)


def near_kernel(k, n, tile, piece, xr, v_ref):
    v_ref[...] = jnp.zeros_like(v_ref)

    def step(t, high, low):
        v_ref[...] += along(xr, rows_at(t * tile, tile), k, high, low)

    tiles_of(piece, tile, 0, piece.shape[0] // tile, step)


def late_kernel(k, n, group, tile, parts, extra, *refs):
    near, lead, refs = refs[: parts - 1], refs[parts - 1 : parts + group - 2], refs[parts + group - 2 :]
    xr, xg, v_ref, own_ref, pair_ref, energy_ref, *refs = refs
    more, refs = (refs[0], refs[1:]) if extra else (None, refs)
    out_ref, v_acc, u_acc = refs
    even = place()[0] == 0
    v_acc[...] = v_ref[...]
    u_acc[...] = own_ref[...]
    rows = near[0].shape[0]
    down = [(p, t) for p in range(1, parts) for t in range(rows // tile)]
    over = [(s, t) for s in range(1, group) for t in range(n // tile)]
    for i in range(max(len(down), len(over))):
        if i < len(down):
            p, t = down[i]
            high, low = split(near[p - 1][t * tile : (t + 1) * tile, :])
            v_acc[...] += along(xr, rows_at(p * rows + t * tile, tile), k, high, low)
        if i < len(over):
            s, t = over[i]
            high, low = split(lead[s - 1][t * tile : (t + 1) * tile, :])
            cols = slice((s - 1) * 2 * n, s * 2 * n)
            u_acc[:, t * tile : (t + 1) * tile] += across(xg, cols, k, high, low)
    own = energy_ref[...] * own_half(pair_ref, even, n) + u_acc[...]
    out_ref[:, : 2 * n] = v_acc[...] + in_half(own, even)
    if extra:
        part = more[...]
        out_ref[:, 2 * n :] = jnp.where(even, part, jnp.zeros_like(part))


def combine_kernel(k, n, group, extra, keep_ref, got_ref, *refs):
    even = place()[0] == 0
    if extra:
        pair_ref, mine, theirs, outs = refs[0], refs[1:group], refs[group : 2 * group - 1], refs[2 * group - 1 :]
        part = pair_ref[:, 2 * n :]
        for s in range(1, group):
            to_z = turned(s, group, even)
            part = part + jnp.where(to_z, theirs[s - 1][:, 2 * n :], mine[s - 1][:, 2 * n :])
        outs[group - 1][...] = part
    else:
        outs = refs
    for s in range(1, group):
        outs[s - 1][:, : 2 * n] = keep_ref[s - 1] + got_ref[s - 1]
        if extra:
            outs[s - 1][:, 2 * n :] = jnp.where(turned(s, group, even), part, jnp.zeros_like(part))


def pair_kernel(k, n, first_ref, mine_ref, got_ref, *outs):
    value = mine_ref[...] + got_ref[...]
    s = jnp.concatenate([first_ref[...], value], axis=0)
    moments = dot32(s, s, NT)
    for out in outs:
        out[:, : 2 * n] = value
        out[:, 2 * n :] = jnp.zeros((k, 8 * k), F32)
        out[:, 2 * n : 2 * n + 2 * k] = moments[:k]
        out[:, 2 * n + 2 * k : 2 * n + 4 * k] = moments[k:]


def factor_of(gram):
    k = gram.shape[0]
    rows = lax.broadcasted_iota(jnp.int32, (k, 2 * k), 0)
    cols = lax.broadcasted_iota(jnp.int32, (k, 2 * k), 1)
    row = lax.broadcasted_iota(jnp.int32, (k, 1), 0)
    both = jnp.concatenate([gram, eye(k)], axis=1)
    for j in range(k - 1):
        lead = both[j : j + 1, :]
        lead = lead * (1.0 / both[j : j + 1, j : j + 1])
        both = both - jnp.where(row > j, both[:, j : j + 1], 0.0) * lead
    pivots = jnp.sum(jnp.where(rows == cols, both, 0.0), axis=1, keepdims=True)
    both = both * (1.0 / jnp.sqrt(pivots))
    upper = jnp.where(rows <= cols, both, 0.0)[:, :k]
    return dot32(upper, eye(k), TN), both[:, k:]


def gram_of(moments, coefficients):
    k = moments.shape[0]
    w = coefficients.shape[1]
    parts = jnp.concatenate([-coefficients, eye(w)], axis=0)
    return dot32(parts, dot32(moments, parts, NN), TN)


def eye(k):
    return jnp.where(
        lax.broadcasted_iota(jnp.int32, (k, k), 0) == lax.broadcasted_iota(jnp.int32, (k, k), 1), 1.0, 0.0
    ).astype(F32)


def second_kernel(k, n, order, first_ref, pair_ref, mine_ref, got_ref, q_ref, prod_ref, proj_ref, fact_ref, *outs):
    packed = mine_ref[:, 2 * n :] + got_ref[:, 2 * n :]
    moments = jnp.concatenate([packed[:, : 2 * k], packed[:, 2 * k : 4 * k]], axis=0) * (1.0 / order)
    projection = moments[:k, k:]
    lower, inverse = factor_of(gram_of(moments, projection))
    proj_ref[...] = projection
    fact_ref[...] = lower
    x, y = first_ref[...], pair_ref[:, : 2 * n]
    w = mine_ref[:, : 2 * n] + got_ref[:, : 2 * n]
    rest = jnp.concatenate([y, w], axis=1) - dot32(projection, jnp.concatenate([x, y], axis=1), TN)
    both = dot32(inverse, rest, NN)
    q, prod = both[:, : 2 * n], both[:, 2 * n :]
    q_ref[...] = q
    prod_ref[...] = prod
    s = jnp.concatenate([q, x, prod], axis=0)
    total = dot32(s, s, NT)
    for out in outs:
        out[...] = total


def sum_kernel(*refs):
    count = (len(refs) + 1) // 2
    total = refs[0][...]
    for m in refs[1:count]:
        total = total + m[...]
    for out in refs[count:]:
        out[...] = total


def last_kernel(k, n, order, first_ref, q_ref, prod_ref, proj0_ref, fact0_ref, *refs):
    *sums, basis_ref, proj_ref, fact_ref = refs
    total = sums[0][...]
    for m in sums[1:]:
        total = total + m[...]
    moments = total * (1.0 / order)
    coefficients = moments[: 2 * k, 2 * k :]
    lower, inverse = factor_of(gram_of(moments, coefficients))
    proj_ref[0] = proj0_ref[...]
    proj_ref[1] = coefficients[:k]
    fact_ref[0] = fact0_ref[...]
    fact_ref[1] = lower
    even = place()[0] == 0
    before = jnp.concatenate([own_half(q_ref, even, n), own_half(first_ref, even, n)], axis=0)
    rest = own_half(prod_ref, even, n) - dot32(coefficients, before, TN)
    basis_ref[...] = dot32(inverse, rest, NN)


def call(kernel, out_shape, n_in, scratch=(), limit=1 << 20, name=None, far=0, flops=0):
    many = isinstance(out_shape, (tuple, list))
    run = pl.pallas_call(
        kernel,
        out_shape=out_shape,
        in_specs=[pl.BlockSpec(memory_space=pl.ANY) if i < far else VMEM_SPEC for i in range(n_in)],
        out_specs=tuple([VMEM_SPEC] * len(out_shape)) if many else VMEM_SPEC,
        scratch_shapes=list(scratch),
        compiler_params=pltpu.CompilerParams(vmem_limit_bytes=limit),
        cost_estimate=pl.CostEstimate(flops=flops, transcendentals=0, bytes_accessed=flops // 128) if flops else None,
        name=name,
    )
    return lambda *args: run(
        *[pltpu.with_memory_space_constraint(v, pltpu.HBM if i < far else pltpu.VMEM) for i, v in enumerate(args)]
    )


def shape(*dims):
    return jax.ShapeDtypeStruct(dims, F32)


def on_device(n_row, n_col, coupling, energies, block):
    n, k = block.shape
    group = n_row
    order = n * n_row * n_col
    rows = coupling.shape[0] * n
    width = coupling.shape[2]
    axes = ("row", "col")
    flat = [(r, c) for r in range(n_row) for c in range(n_col)]

    def send(value, to):
        pairs = [(r * n_col + c, to(r, c)) for r, c in flat]
        return lax.ppermute(value, axes, [p for p in pairs if p[1] is not None])

    def swap(value):
        return send(value, lambda r, c: r * n_col + (c ^ 1))

    def chip(r, c, s_row, s_z):
        return (r ^ s_row) * n_col + (c ^ (2 * s_z))

    def spread(s):
        def to(r, c):
            along_z = (c % 2 == 0) != (s >= group // 2)
            return chip(r, c, 0, s) if along_z else chip(r, c, s, 0)

        return to

    steps = range(1, group)
    tile, parts = 256, 3
    total_pieces = group * parts
    block_shape = shape(rows // parts, 2 * n)
    most = max(len(pieces_of(p, group, n, rows // parts)) for p in range(parts))
    semaphores = lambda count: [pltpu.SemaphoreType.DMA((count, most))]
    work = rows * 2 * n * 256
    a = coupling.reshape(rows, width)
    energy = energies.reshape(1, n)

    other = swap(block.T)
    own, *held = call(
        functools.partial(begin_kernel, k, n, group, parts),
        (shape(k, n), block_shape),
        2,
        scratch=semaphores(1) + [pltpu.SemaphoreType.DMA],
        name="begin",
        far=2,
        flops=work // 4,
    )(a, block.T)
    firsts = call(functools.partial(order_kernel, k, n), (shape(k, 2 * n),) * (group - 1), 2, name="order")(own, other)
    first = firsts[0]

    def products(held, copies, name):
        pair = copies[0]
        extra = pair.shape[1] > 2 * n
        sizes = (k, n, group, tile, parts)
        load = len(held) < total_pieces

        def matrix_call(kernel, need, upto, out_shapes, args, scratch, label, flops):
            given = [i for i in need if i < len(held)]
            new = range(len(held), max(upto, len(held)))
            outs = call(
                functools.partial(kernel, *sizes, given, new),
                tuple(out_shapes) + (block_shape,) * len(new),
                (len(new) > 0) + len(given) + len(args),
                scratch=list(scratch) + (semaphores(len(new)) if new else []),
                limit=8 << 20,
                name=name + label,
                far=int(len(new) > 0),
                flops=flops,
            )(*([a] if new else []), *[held[i] for i in given], *args)
            held.extend(outs[len(out_shapes) :])
            return outs[: len(out_shapes)]

        mine = [send(copies[s - 1], spread(s)) for s in steps]
        (u0,) = matrix_call(
            early_kernel,
            range(parts),
            parts + 2,
            [shape(k, rows)],
            [pair],
            [pltpu.VMEM((2 * k, 2 * n), BF16)],
            "_early",
            2 * work,
        )
        u0, same, *mine = lax.optimization_barrier((u0, pair, *mine))
        theirs = [swap(y) for y in mine]
        (v0,) = matrix_call(
            own_kernel,
            range(parts, parts + group - 1),
            parts + group,
            [shape(k, (group - 1) * 2 * n)],
            [same],
            [pltpu.VMEM((2 * k, n), BF16)],
            "_own",
            work,
        )
        out, keep, mine_u, xr, xg = matrix_call(
            main_kernel,
            range(parts, total_pieces),
            total_pieces,
            [
                shape(group - 1, k, 2 * n),
                shape(group - 1, k, 2 * n),
                shape(k, n),
                jax.ShapeDtypeStruct((2 * k, rows), BF16),
                jax.ShapeDtypeStruct((2 * k, (group - 1) * 2 * n), BF16),
            ],
            [pair, u0, v0, *mine, *theirs],
            [pltpu.VMEM((k, rows), F32), pltpu.VMEM((k, (group - 1) * 2 * n), F32)],
            "",
            8 * work,
        )
        got = swap(out)
        near = call(
            functools.partial(near_kernel, k, n, tile),
            shape(k, 2 * n),
            2,
            limit=8 << 20,
            name=name + "_near",
            flops=work,
        )(held[0], xr)
        got, near = lax.optimization_barrier((got, near))
        sums = call(
            functools.partial(combine_kernel, k, n, group, extra),
            (shape(k, pair.shape[1]),) * (group - 1) + ((shape(k, 8 * k),) if extra else ()),
            2 + (2 * group - 1 if extra else 0),
            name=name + "_combine",
        )(keep, got, *((pair, *mine, *theirs) if extra else ()))
        arrived = [send(sums[s - 1], spread(s)) for s in steps]
        total = call(
            functools.partial(late_kernel, *sizes, extra),
            shape(k, pair.shape[1]),
            parts - 1 + group - 1 + 6 + extra,
            scratch=[pltpu.VMEM((k, 2 * n), F32), pltpu.VMEM((k, n), F32)],
            limit=8 << 20,
            name=name + "_late",
            flops=3 * work,
        )(*held[1 : parts + group - 1], xr, xg, near, mine_u, pair, energy, *sums[group - 1 :])
        for v in arrived:
            total = total + v
        return total, swap(total), held

    mine, got, held = products(held, firsts, "first")
    pairs = call(functools.partial(pair_kernel, k, n), (shape(k, 2 * n + 8 * k),) * (group - 1), 3, name="pair")(
        first, mine, got
    )
    pair = pairs[0]
    mine, got, held = products(held, pairs, "second")
    q, prod, proj0, fact0, *moments = call(
        functools.partial(second_kernel, k, n, order),
        (shape(k, 2 * n), shape(k, 2 * n), shape(k, k), shape(k, k)) + (shape(3 * k, 3 * k),) * (group - 1),
        4,
        name="middle",
    )(first, pair, mine, got)
    sums = [moments[0]] + [send(moments[s - 1], lambda r, c, s=s: chip(r, c, s, 0)) for s in steps]
    moments = call(sum_kernel, (shape(3 * k, 3 * k),) * (group - 1), group, name="sum")(*sums)
    sums = [moments[0]] + [send(moments[s - 1], lambda r, c, s=s: chip(r, c, 0, s)) for s in steps]
    basis, proj, fact = call(
        functools.partial(last_kernel, k, n, order),
        (shape(k, n), shape(2, k, k), shape(2, k, k)),
        5 + group,
        name="last",
    )(first, q, prod, proj0, fact0, *sums)
    return basis.T, proj, fact


def solution(mesh):
    n_row, n_col = mesh.shape["row"], mesh.shape["col"]

    def body(coupling, energies, block):
        n, k = block.shape
        paired = n_col == 2 * n_row and n_row & (n_row - 1) == 0 and n_row > 1
        divides = coupling.shape[0] * n % 768 == 0
        whole = divides and n % 64 == 0 and n >= 256 and 8 * k == 128 and coupling.shape[2] == coupling.shape[0] * n * 2
        small = coupling.size * 4 <= 44 << 20
        if paired and whole and small:
            return on_device(n_row, n_col, coupling, energies, block)
        return generic(coupling, energies, block)

    placed = (P(None, "col", "row"), P(("row", "col")), P(("row", "col"), None))
    return jax.shard_map(
        body,
        mesh=mesh,
        in_specs=placed,
        out_specs=(P(("row", "col"), None), P(), P()),
        check_vma=False,
    )
```

```python
import functools

import jax
import jax.numpy as jnp
from jax import lax
from jax.experimental import pallas as pl
from jax.experimental.pallas import tpu as pltpu
from jax.sharding import PartitionSpec as P

ITERS = 2
F32 = jnp.float32
BF16 = jnp.bfloat16

precise = lax.Precision.HIGHEST

NN = (((1,), (0,)), ((), ()))
NT = (((1,), (1,)), ((), ()))
TN = (((0,), (0,)), ((), ()))

VMEM_SPEC = pl.BlockSpec(memory_space=pltpu.VMEM)


def generic(coupling, energies, block):
    order = block.shape[0] * lax.axis_size("row") * lax.axis_size("col")
    segment = block.shape[0]
    width = block.shape[1]
    column = lax.axis_index("col")
    current, energy_rows = (
        lax.all_gather(block, "col", axis=0, tiled=True),
        lax.all_gather(energies, "col", axis=0, tiled=True),
    )
    prior = jnp.zeros_like(current)
    projection_list = []
    factor_list = []
    for section in range(ITERS):
        own_rows = lax.dynamic_slice_in_dim(current, column * segment, segment, 0)
        spread = lax.all_gather(own_rows, "row", axis=0, tiled=True)
        spread = spread.reshape(coupling.shape[0], segment, width)
        direct = lax.psum_scatter(
            jnp.einsum("aig,gk->aik", coupling, current, precision=precise),
            "row",
            scatter_dimension=0,
            tiled=True,
        ).reshape(segment, width)
        partial_value = jnp.einsum("aig,aik->gk", coupling, spread, precision=precise)
        transposed = lax.psum(partial_value, "col")
        direct_rows = lax.all_gather(direct, "col", axis=0, tiled=True)
        product = energy_rows[:, None] * current + direct_rows + transposed
        stacked = jnp.concatenate([current, prior, product], axis=1)
        moments = lax.psum(jnp.einsum("nk,nl->kl", stacked, stacked, precision=precise), "row") / order
        projection = moments[:width, 2 * width :]
        cross = moments[width : 2 * width, 2 * width :]
        weights = jnp.concatenate([-projection, -cross, jnp.eye(width, dtype=F32)], axis=0)
        gram_matrix = jnp.dot(weights.T, jnp.dot(moments, weights, precision=precise), precision=precise)
        factor = jnp.linalg.cholesky(gram_matrix)
        residual = (
            product
            - jnp.dot(current, projection, precision=precise)
            - jnp.dot(prior, cross, precision=precise)
        )
        prior = current
        current = jax.scipy.linalg.solve_triangular(factor, residual.T, lower=True).T
        projection_list.append(projection)
        factor_list.append(factor)
    basis = lax.dynamic_slice_in_dim(current, column * segment, segment, 0)
    return (basis, jnp.stack(projection_list), jnp.stack(factor_list))


def place():
    column = lax.axis_index("col")
    return lax.rem(column, 2), lax.div(column, 2), lax.axis_index("row")


def split(value):
    high = value.astype(BF16)
    return high, (value - high.astype(F32)).astype(BF16)


def dot(left, right, dims):
    return lax.dot_general(left, right, dims, preferred_element_type=F32)


def dot32(left, right, dims):
    return lax.dot_general(left, right, dims, preferred_element_type=F32, precision=precise)


def own_half(value, even, n):
    return jnp.where(even, value[:, :n], value[:, n : 2 * n])


def in_half(value, even):
    zero = jnp.zeros_like(value)
    return jnp.concatenate([jnp.where(even, value, zero), jnp.where(even, zero, value)], axis=1)


def pieces_of(part, group, n, rows):
    found, at, end = [], part * rows, (part + 1) * rows
    while at < end:
        s, off = divmod(at, n)
        count = min(n - off, end - at)
        found.append((s, off, at - part * rows, count))
        at += count
    return found


def order_of(group, parts):
    near = [(0, p) for p in range(parts)]
    lead = [(s, 0) for s in range(1, group)]
    return near + lead + [(s, p) for s in range(1, group) for p in range(1, parts)]


class Loader:
    def __init__(self, source, arrived, n, group, parts, where, held):
        _, z, r = place()

        def copies(i):
            s, part = where[i]
            cols = pl.ds(pl.multiple_of(lax.bitwise_xor(z, s) * (2 * n), 128), 2 * n)
            return [
                pltpu.make_async_copy(
                    source.at[pl.ds(pl.multiple_of(lax.bitwise_xor(r, peer) * n + off, 8), count), cols],
                    held[i].at[pl.ds(at, count), :],
                    arrived.at[i, j],
                )
                for j, (peer, off, at, count) in enumerate(pieces_of(part, group, n, group * n // parts))
            ]

        self.copies = copies
        for i in range(len(held)):
            for copy in copies(i):
                copy.start()

    def wait(self, i):
        for copy in self.copies(i):
            copy.wait()


class Pieces:
    def __init__(self, n, group, parts, given, new, scratch, refs):
        order = order_of(group, parts)
        refs = list(refs)
        source = refs.pop(0) if len(new) else None
        held = {order[i]: refs.pop(0) for i in given}
        self.waits = {}
        if len(new):
            arrived = refs.pop()
            at = len(refs) - scratch - len(new)
            fresh, refs = refs[at : at + len(new)], refs[:at] + refs[at + len(new) :]
            where = [order[i] for i in new]
            self.loader = Loader(source, arrived, n, group, parts, where, fresh)
            self.waits = {key: i for i, key in enumerate(where)}
            held.update(zip(where, fresh))
        self.held, self.refs = held, refs

    def get(self, s, p):
        if (s, p) in self.waits:
            self.loader.wait(self.waits.pop((s, p)))
        return self.held[s, p]

    def finish(self):
        for key in list(self.waits):
            self.get(*key)


def rows_at(start, tile):
    return slice(start, start + tile) if isinstance(start, int) else pl.ds(pl.multiple_of(start, tile), tile)


def tiles_of(piece, tile, first, last, step, loop=False):
    def body(t, carry):
        high, low = split(piece[rows_at(t * tile, tile), :])
        step(t, high, low)
        return carry

    if loop:
        lax.fori_loop(first, last, body, 0)
    else:
        for t in range(first, last):
            body(t, 0)


def across(xg, cols, k, high, low):
    one = dot(xg[:, cols], high, NT)
    two = dot(xg[:k, cols], low, NT)
    return one[:k] + one[k:] + two


def along(xr, at, k, high, low):
    one = dot(xr[:, at], high, NN)
    two = dot(xr[:k, at], low, NN)
    return one[:k] + one[k:] + two


def begin_kernel(k, n, group, parts, source, block_ref, own_ref, *refs):
    *held, arrived, ready = refs
    copy = pltpu.make_async_copy(block_ref, own_ref, ready)
    copy.start()
    loader = Loader(source, arrived, n, group, parts, order_of(group, parts), held)
    copy.wait()
    for i in range(len(held)):
        loader.wait(i)


def order_kernel(k, n, own_ref, other_ref, *outs):
    even = place()[0] == 0
    own, other = own_ref[...], other_ref[...]
    for out in outs:
        out[...] = jnp.concatenate([jnp.where(even, own, other), jnp.where(even, other, own)], axis=1)


def put(slab, at, k, value):
    high, low = split(value)
    slab[:k, at : at + value.shape[1]] = high
    slab[k:, at : at + value.shape[1]] = low


def turned(s, group, even):
    return jnp.logical_not(even) if s >= group // 2 else even


def early_kernel(k, n, group, tile, parts, given, new, *refs):
    pieces = Pieces(n, group, parts, given, new, 1, refs)
    xg = pieces.refs.pop(-1)
    pair_ref, u_ref = pieces.refs
    put(xg, 0, k, pair_ref[:, : 2 * n])
    for p in range(parts):
        piece = pieces.get(0, p)
        rows = piece.shape[0]

        def step(t, high, low):
            u_ref[:, rows_at(p * rows + t * tile, tile)] = across(xg, slice(None), k, high, low)

        tiles_of(piece, tile, 0, rows // tile, step, len(new) > 0)
    pieces.finish()


def own_kernel(k, n, group, tile, parts, given, new, *refs):
    pieces = Pieces(n, group, parts, given, new, 1, refs)
    xr = pieces.refs.pop(-1)
    pair_ref, v_ref = pieces.refs
    even = place()[0] == 0
    put(xr, 0, k, own_half(pair_ref, even, n))
    v_ref[...] = jnp.zeros_like(v_ref)
    for s in range(1, group):
        cols = slice((s - 1) * 2 * n, s * 2 * n)

        def step(t, high, low):
            v_ref[:, cols] += along(xr, rows_at(t * tile, tile), k, high, low)

        tiles_of(pieces.get(s, 0), tile, 0, n // tile, step, len(new) > 0)
    pieces.finish()


def main_kernel(k, n, group, tile, parts, given, new, *refs):
    pieces = Pieces(n, group, parts, given, new, 2, refs)
    u_acc, v_acc = pieces.refs[-2:]
    refs = pieces.refs[:-2]
    pair_ref, u0_ref, v0_ref, mine, theirs = refs[0], refs[1], refs[2], refs[3 : group + 2], refs[group + 2 : 2 * group + 1]
    send_ref, keep_ref, own_ref, xr, xg = refs[2 * group + 1 :]
    even = place()[0] == 0

    segments = [own_half(pair_ref, even, n)]
    for s in range(1, group):
        y, w = mine[s - 1][:, : 2 * n], theirs[s - 1][:, : 2 * n]
        to_z = turned(s, group, even)
        put(xg, (s - 1) * 2 * n, k, jnp.where(to_z, y, w))
        segments.append(own_half(jnp.where(to_z, w, y), even, n))
    for a in range(0, group, 2):
        put(xr, a * n, k, jnp.concatenate(segments[a : a + 2], axis=1))
    u_acc[...] = u0_ref[...]
    v_acc[...] = v0_ref[...]

    for s, p in order_of(group, parts)[parts:]:
        piece = pieces.get(s, p)
        rows = piece.shape[0]
        cols = slice((s - 1) * 2 * n, s * 2 * n)

        def step(t, high, low):
            at = rows_at(p * rows + t * tile, tile)
            v_acc[:, cols] += along(xr, at, k, high, low)
            u_acc[:, at] += across(xg, cols, k, high, low)

        tiles_of(piece, tile, n // tile if p == 0 else 0, rows // tile, step, len(new) > 0)

    own_ref[...] = u_acc[:, :n]
    for s in range(1, group):
        to_z = turned(s, group, even)
        by_z = v_acc[:, 2 * n * (s - 1) : 2 * n * s]
        by_row = in_half(u_acc[:, n * s : n * (s + 1)], even)
        keep_ref[s - 1] = jnp.where(to_z, by_z, by_row)
        send_ref[s - 1] = jnp.where(to_z, by_row, by_z)


def near_kernel(k, n, tile, piece, xr, v_ref):
    v_ref[...] = jnp.zeros_like(v_ref)

    def step(t, high, low):
        v_ref[...] += along(xr, rows_at(t * tile, tile), k, high, low)

    tiles_of(piece, tile, 0, piece.shape[0] // tile, step)


def late_kernel(k, n, group, tile, parts, extra, *refs):
    near, lead, refs = refs[: parts - 1], refs[parts - 1 : parts + group - 2], refs[parts + group - 2 :]
    xr, xg, v_ref, own_ref, pair_ref, energy_ref, *refs = refs
    more, refs = (refs[0], refs[1:]) if extra else (None, refs)
    out_ref, v_acc, u_acc = refs
    even = place()[0] == 0
    v_acc[...] = v_ref[...]
    u_acc[...] = own_ref[...]
    rows = near[0].shape[0]
    down = [(p, t) for p in range(1, parts) for t in range(rows // tile)]
    over = [(s, t) for s in range(1, group) for t in range(n // tile)]
    for i in range(max(len(down), len(over))):
        if i < len(down):
            p, t = down[i]
            high, low = split(near[p - 1][t * tile : (t + 1) * tile, :])
            v_acc[...] += along(xr, rows_at(p * rows + t * tile, tile), k, high, low)
        if i < len(over):
            s, t = over[i]
            high, low = split(lead[s - 1][t * tile : (t + 1) * tile, :])
            cols = slice((s - 1) * 2 * n, s * 2 * n)
            u_acc[:, t * tile : (t + 1) * tile] += across(xg, cols, k, high, low)
    own = energy_ref[...] * own_half(pair_ref, even, n) + u_acc[...]
    out_ref[:, : 2 * n] = v_acc[...] + in_half(own, even)
    if extra:
        part = more[...]
        out_ref[:, 2 * n :] = jnp.where(even, part, jnp.zeros_like(part))


def combine_kernel(k, n, group, extra, keep_ref, got_ref, *refs):
    even = place()[0] == 0
    if extra:
        pair_ref, mine, theirs, outs = refs[0], refs[1:group], refs[group : 2 * group - 1], refs[2 * group - 1 :]
        part = pair_ref[:, 2 * n :]
        for s in range(1, group):
            to_z = turned(s, group, even)
            part = part + jnp.where(to_z, theirs[s - 1][:, 2 * n :], mine[s - 1][:, 2 * n :])
        outs[group - 1][...] = part
    else:
        outs = refs
    for s in range(1, group):
        outs[s - 1][:, : 2 * n] = keep_ref[s - 1] + got_ref[s - 1]
        if extra:
            outs[s - 1][:, 2 * n :] = jnp.where(turned(s, group, even), part, jnp.zeros_like(part))


def pair_kernel(k, n, first_ref, mine_ref, got_ref, *outs):
    value = mine_ref[...] + got_ref[...]
    s = jnp.concatenate([first_ref[...], value], axis=0)
    moments = dot32(s, s, NT)
    for out in outs:
        out[:, : 2 * n] = value
        out[:, 2 * n :] = jnp.zeros((k, 8 * k), F32)
        out[:, 2 * n : 2 * n + 2 * k] = moments[:k]
        out[:, 2 * n + 2 * k : 2 * n + 4 * k] = moments[k:]


def factor_of(gram):
    k = gram.shape[0]
    rows = lax.broadcasted_iota(jnp.int32, (k, 2 * k), 0)
    cols = lax.broadcasted_iota(jnp.int32, (k, 2 * k), 1)
    row = lax.broadcasted_iota(jnp.int32, (k, 1), 0)
    both = jnp.concatenate([gram, eye(k)], axis=1)
    for j in range(k - 1):
        lead = both[j : j + 1, :]
        lead = lead * (1.0 / both[j : j + 1, j : j + 1])
        both = both - jnp.where(row > j, both[:, j : j + 1], 0.0) * lead
    pivots = jnp.sum(jnp.where(rows == cols, both, 0.0), axis=1, keepdims=True)
    both = both * (1.0 / jnp.sqrt(pivots))
    upper = jnp.where(rows <= cols, both, 0.0)[:, :k]
    return dot32(upper, eye(k), TN), both[:, k:]


def gram_of(moments, coefficients):
    k = moments.shape[0]
    w = coefficients.shape[1]
    parts = jnp.concatenate([-coefficients, eye(w)], axis=0)
    return dot32(parts, dot32(moments, parts, NN), TN)


def eye(k):
    return jnp.where(
        lax.broadcasted_iota(jnp.int32, (k, k), 0) == lax.broadcasted_iota(jnp.int32, (k, k), 1), 1.0, 0.0
    ).astype(F32)


def second_kernel(k, n, order, first_ref, pair_ref, mine_ref, got_ref, q_ref, prod_ref, proj_ref, fact_ref, *outs):
    packed = mine_ref[:, 2 * n :] + got_ref[:, 2 * n :]
    moments = jnp.concatenate([packed[:, : 2 * k], packed[:, 2 * k : 4 * k]], axis=0) * (1.0 / order)
    projection = moments[:k, k:]
    lower, inverse = factor_of(gram_of(moments, projection))
    proj_ref[...] = projection
    fact_ref[...] = lower
    x, y = first_ref[...], pair_ref[:, : 2 * n]
    w = mine_ref[:, : 2 * n] + got_ref[:, : 2 * n]
    rest = jnp.concatenate([y, w], axis=1) - dot32(projection, jnp.concatenate([x, y], axis=1), TN)
    both = dot32(inverse, rest, NN)
    q, prod = both[:, : 2 * n], both[:, 2 * n :]
    q_ref[...] = q
    prod_ref[...] = prod
    s = jnp.concatenate([q, x, prod], axis=0)
    total = dot32(s, s, NT)
    for out in outs:
        out[...] = total


def sum_kernel(*refs):
    count = (len(refs) + 1) // 2
    total = refs[0][...]
    for m in refs[1:count]:
        total = total + m[...]
    for out in refs[count:]:
        out[...] = total


def last_kernel(k, n, order, first_ref, q_ref, prod_ref, proj0_ref, fact0_ref, *refs):
    *sums, basis_ref, proj_ref, fact_ref = refs
    total = sums[0][...]
    for m in sums[1:]:
        total = total + m[...]
    moments = total * (1.0 / order)
    coefficients = moments[: 2 * k, 2 * k :]
    lower, inverse = factor_of(gram_of(moments, coefficients))
    proj_ref[0] = proj0_ref[...]
    proj_ref[1] = coefficients[:k]
    fact_ref[0] = fact0_ref[...]
    fact_ref[1] = lower
    even = place()[0] == 0
    before = jnp.concatenate([own_half(q_ref, even, n), own_half(first_ref, even, n)], axis=0)
    rest = own_half(prod_ref, even, n) - dot32(coefficients, before, TN)
    basis_ref[...] = dot32(inverse, rest, NN)


def call(kernel, out_shape, n_in, scratch=(), limit=1 << 20, name=None, far=0, flops=0):
    many = isinstance(out_shape, (tuple, list))
    run = pl.pallas_call(
        kernel,
        out_shape=out_shape,
        in_specs=[pl.BlockSpec(memory_space=pl.ANY) if i < far else VMEM_SPEC for i in range(n_in)],
        out_specs=tuple([VMEM_SPEC] * len(out_shape)) if many else VMEM_SPEC,
        scratch_shapes=list(scratch),
        compiler_params=pltpu.CompilerParams(vmem_limit_bytes=limit),
        cost_estimate=pl.CostEstimate(flops=flops, transcendentals=0, bytes_accessed=flops // 128) if flops else None,
        name=name,
    )
    return lambda *args: run(
        *[pltpu.with_memory_space_constraint(v, pltpu.HBM if i < far else pltpu.VMEM) for i, v in enumerate(args)]
    )


def shape(*dims):
    return jax.ShapeDtypeStruct(dims, F32)


def on_device(n_row, n_col, coupling, energies, block):
    n, k = block.shape
    group = n_row
    order = n * n_row * n_col
    rows = coupling.shape[0] * n
    width = coupling.shape[2]
    axes = ("row", "col")
    flat = [(r, c) for r in range(n_row) for c in range(n_col)]

    def send(value, to):
        pairs = [(r * n_col + c, to(r, c)) for r, c in flat]
        return lax.ppermute(value, axes, [p for p in pairs if p[1] is not None])

    def swap(value):
        return send(value, lambda r, c: r * n_col + (c ^ 1))

    def chip(r, c, s_row, s_z):
        return (r ^ s_row) * n_col + (c ^ (2 * s_z))

    def spread(s):
        def to(r, c):
            along_z = (c % 2 == 0) != (s >= group // 2)
            return chip(r, c, 0, s) if along_z else chip(r, c, s, 0)

        return to

    steps = range(1, group)
    tile, parts = 256, 3
    total_pieces = group * parts
    block_shape = shape(rows // parts, 2 * n)
    most = max(len(pieces_of(p, group, n, rows // parts)) for p in range(parts))
    semaphores = lambda count: [pltpu.SemaphoreType.DMA((count, most))]
    work = rows * 2 * n * 256
    a = coupling.reshape(rows, width)
    energy = energies.reshape(1, n)

    other = swap(block.T)
    own, *held = call(
        functools.partial(begin_kernel, k, n, group, parts),
        (shape(k, n), block_shape),
        2,
        scratch=semaphores(1) + [pltpu.SemaphoreType.DMA],
        name="begin",
        far=2,
        flops=work // 4,
    )(a, block.T)
    firsts = call(functools.partial(order_kernel, k, n), (shape(k, 2 * n),) * (group - 1), 2, name="order")(own, other)
    first = firsts[0]

    def products(held, copies, name):
        pair = copies[0]
        extra = pair.shape[1] > 2 * n
        sizes = (k, n, group, tile, parts)
        load = len(held) < total_pieces

        def matrix_call(kernel, need, upto, out_shapes, args, scratch, label, flops):
            given = [i for i in need if i < len(held)]
            new = range(len(held), max(upto, len(held)))
            outs = call(
                functools.partial(kernel, *sizes, given, new),
                tuple(out_shapes) + (block_shape,) * len(new),
                (len(new) > 0) + len(given) + len(args),
                scratch=list(scratch) + (semaphores(len(new)) if new else []),
                limit=8 << 20,
                name=name + label,
                far=int(len(new) > 0),
                flops=flops,
            )(*([a] if new else []), *[held[i] for i in given], *args)
            held.extend(outs[len(out_shapes) :])
            return outs[: len(out_shapes)]

        mine = [send(copies[s - 1], spread(s)) for s in steps]
        (u0,) = matrix_call(
            early_kernel,
            range(parts),
            parts + 3,
            [shape(k, rows)],
            [pair],
            [pltpu.VMEM((2 * k, 2 * n), BF16)],
            "_early",
            2 * work,
        )
        u0, same, *mine = lax.optimization_barrier((u0, pair, *mine))
        theirs = [swap(y) for y in mine]
        (v0,) = matrix_call(
            own_kernel,
            range(parts, parts + group - 1),
            parts + group,
            [shape(k, (group - 1) * 2 * n)],
            [same],
            [pltpu.VMEM((2 * k, n), BF16)],
            "_own",
            work,
        )
        out, keep, mine_u, xr, xg = matrix_call(
            main_kernel,
            range(parts, total_pieces),
            total_pieces,
            [
                shape(group - 1, k, 2 * n),
                shape(group - 1, k, 2 * n),
                shape(k, n),
                jax.ShapeDtypeStruct((2 * k, rows), BF16),
                jax.ShapeDtypeStruct((2 * k, (group - 1) * 2 * n), BF16),
            ],
            [pair, u0, v0, *mine, *theirs],
            [pltpu.VMEM((k, rows), F32), pltpu.VMEM((k, (group - 1) * 2 * n), F32)],
            "",
            8 * work,
        )
        got = swap(out)
        near = call(
            functools.partial(near_kernel, k, n, tile),
            shape(k, 2 * n),
            2,
            limit=8 << 20,
            name=name + "_near",
            flops=work,
        )(held[0], xr)
        got, near = lax.optimization_barrier((got, near))
        sums = call(
            functools.partial(combine_kernel, k, n, group, extra),
            (shape(k, pair.shape[1]),) * (group - 1) + ((shape(k, 8 * k),) if extra else ()),
            2 + (2 * group - 1 if extra else 0),
            name=name + "_combine",
        )(keep, got, *((pair, *mine, *theirs) if extra else ()))
        arrived = [send(sums[s - 1], spread(s)) for s in steps]
        total = call(
            functools.partial(late_kernel, *sizes, extra),
            shape(k, pair.shape[1]),
            parts - 1 + group - 1 + 6 + extra,
            scratch=[pltpu.VMEM((k, 2 * n), F32), pltpu.VMEM((k, n), F32)],
            limit=8 << 20,
            name=name + "_late",
            flops=3 * work,
        )(*held[1 : parts + group - 1], xr, xg, near, mine_u, pair, energy, *sums[group - 1 :])
        for v in arrived:
            total = total + v
        return total, swap(total), held

    mine, got, held = products(held, firsts, "first")
    pairs = call(functools.partial(pair_kernel, k, n), (shape(k, 2 * n + 8 * k),) * (group - 1), 3, name="pair")(
        first, mine, got
    )
    pair = pairs[0]
    mine, got, held = products(held, pairs, "second")
    q, prod, proj0, fact0, *moments = call(
        functools.partial(second_kernel, k, n, order),
        (shape(k, 2 * n), shape(k, 2 * n), shape(k, k), shape(k, k)) + (shape(3 * k, 3 * k),) * (group - 1),
        4,
        name="middle",
    )(first, pair, mine, got)
    sums = [moments[0]] + [send(moments[s - 1], lambda r, c, s=s: chip(r, c, s, 0)) for s in steps]
    moments = call(sum_kernel, (shape(3 * k, 3 * k),) * (group - 1), group, name="sum")(*sums)
    sums = [moments[0]] + [send(moments[s - 1], lambda r, c, s=s: chip(r, c, 0, s)) for s in steps]
    basis, proj, fact = call(
        functools.partial(last_kernel, k, n, order),
        (shape(k, n), shape(2, k, k), shape(2, k, k)),
        5 + group,
        name="last",
    )(first, q, prod, proj0, fact0, *sums)
    return basis.T, proj, fact


def solution(mesh):
    n_row, n_col = mesh.shape["row"], mesh.shape["col"]

    def body(coupling, energies, block):
        n, k = block.shape
        paired = n_col == 2 * n_row and n_row & (n_row - 1) == 0 and n_row > 1
        divides = coupling.shape[0] * n % 768 == 0
        whole = divides and n % 64 == 0 and n >= 256 and 8 * k == 128 and coupling.shape[2] == coupling.shape[0] * n * 2
        small = coupling.size * 4 <= 44 << 20
        if paired and whole and small:
            return on_device(n_row, n_col, coupling, energies, block)
        return generic(coupling, energies, block)

    placed = (P(None, "col", "row"), P(("row", "col")), P(("row", "col"), None))
    return jax.shard_map(
        body,
        mesh=mesh,
        in_specs=placed,
        out_specs=(P(("row", "col"), None), P(), P()),
        check_vma=False,
    )
```
